32 devices in a mesh: dp: 2 (over core), row: 4 (over y, x), col: 4 (over z).
Axes of the slice: x: 2, y: 2, z: 4, core: 2. Of those that a mesh axis runs over, the one named last changes fastest.
Arguments:
- inputs: bfloat16 [32768, 768], P(('dp', 'row', 'col')), may hold values from -6 to 6
- segment_ids: int32 [32768], P(('dp', 'row', 'col')), may hold values from 0 to 3, as said below
- query_weight: bfloat16 [768, 768], P('row', 'col'), may hold values from -0.21875 to 0.21875
- key_weight: bfloat16 [768, 768], P('row', 'col'), may hold values from -0.21875 to 0.21875
- value_weight: bfloat16 [768, 768], P('row', 'col'), may hold values from -0.21875 to 0.21875
- output_weight: bfloat16 [768, 768], P('row', 'col'), may hold values from -1.75 to 1.75
- gate_weight: bfloat16 [768, 2048], P('row', 'col'), may hold values from -0.21875 to 0.21875
- up_weight: bfloat16 [768, 2048], P('row', 'col'), may hold values from -0.21875 to 0.21875
- down_weight: bfloat16 [2048, 768], P('row', 'col'), may hold values from -0.125 to 0.125
- first_gain: bfloat16 [768], P(('row', 'col')), may hold values from 0.099609375 to 1.8984375
- second_gain: bfloat16 [768], P(('row', 'col')), may hold values from 0.099609375 to 1.8984375
- cotangent: bfloat16 [32768, 768], P(('dp', 'row', 'col')), may hold values from -6 to 6
Outputs:
- layer_out: bfloat16 [32768, 768], P(('dp', 'row', 'col'))
- input_grad: bfloat16 [32768, 768], P(('dp', 'row', 'col'))
- query_grad: float32 [768, 768], P('row', 'col')
- key_grad: float32 [768, 768], P('row', 'col')
- value_grad: float32 [768, 768], P('row', 'col')
- output_grad: float32 [768, 768], P('row', 'col')
- gate_grad: float32 [768, 2048], P('row', 'col')
- up_grad: float32 [768, 2048], P('row', 'col')
- down_grad: float32 [2048, 768], P('row', 'col')
- first_gain_grad: float32 [768], P(('row', 'col'))
- second_gain_grad: float32 [768], P(('row', 'col'))
The draws below stay inside these ranges and needn't reach their ends.
Inputs may be any that keep to these rules, and one draw needn't show every extreme that they name: `segment_ids`: within each aligned block of 1024 tokens the ids number that block's sequences 0, 1, ... in order; a block holds 1, 2 or 4 sequences of equal length, and each of the three cases occurs in some block.
All inputs are finite; a program needn't handle non-finite values.
Results may differ from the reference program's by a relative error of at most 0.017.
Values may be sent and summed in bfloat16 or wider, within the bound.
No kernel may reach another device: no remote copies, remote signals or barrier semaphores. Data moves between devices by JAX's collectives and lax.ppermute only.
A program may use at most 192 MiB of HBM per device.

```python
from functools import partial
import jax
import jax.numpy as jnp
from jax import lax

D = 768
FF = 2048
HEAD_DIM = 64
TOK_DEV = 1024
TOKENS = 32768


def draw_segment_ids(key, part):
    blocks = TOKENS // TOK_DEV
    order = jax.random.permutation(jax.random.fold_in(key, 17), blocks)
    groups = (order % 3).astype(jnp.int32)
    lengths = TOK_DEV // jnp.left_shift(jnp.int32(1), groups)
    local = jnp.arange(TOK_DEV, dtype=jnp.int32)
    ids = local[None, :] // lengths[:, None]
    return ids.reshape(TOKENS).astype(jnp.int32)


def with_spikes(result, rng, source, target, shards_of, factor):
    def block_of(axis_at):
        return (jnp.arange(result.shape[axis_at]) // (result.shape[axis_at] // shards_of)).reshape((-1,) + (1,) * (result.ndim - 1 - axis_at))

    first = jax.random.permutation(rng, shards_of)[block_of(target)]
    second = (block_of(target) + shards_of // 2) % shards_of
    return jnp.where((block_of(source) == first) | (block_of(source) == second), factor * result, result)


def shard_levels(stream_key, dims, cuts, smallest, top_value):
    factor_of = 1.0
    for position, shards_of in cuts:
        draws = jax.random.uniform(jax.random.fold_in(jax.random.fold_in(stream_key, 6), position), (shards_of,), jnp.float32, smallest / len(cuts), top_value / len(cuts))
        factor_of = factor_of * jnp.repeat(jnp.exp(draws), dims[position] // shards_of).reshape((-1,) + (1,) * (len(dims) - 1 - position))
    return factor_of


def scatter_about(rng, dims, width, limit, pieces=(), held_as=jnp.bfloat16):
    gain = shard_levels(rng, dims, pieces, -0.22, 0.18) if pieces else 1.0
    drawn = jax.random.normal(rng, dims, jnp.float32) * width * gain
    return jnp.minimum(jnp.maximum(drawn, -limit), limit).astype(held_as)


def heavy_noise(key, extent, spread, bound, shards, heavy, kind=jnp.bfloat16):
    result = spread * jax.random.normal(key, extent, jnp.float32)
    if shards:
        result = result * shard_levels(key, extent, shards, -0.22, 0.18)
    return jnp.clip(with_spikes(result, jax.random.fold_in(key, 3), *heavy), -bound, bound).astype(kind)


def setup_inputs(seed: int = 0) -> dict:
    key_of = jax.random.split(jax.random.key(seed), 13)
    inputs = scatter_about(key_of[0], (TOKENS, D), 1.0, 6.0, ((0, 32),))
    segment_ids = draw_segment_ids(jax.random.fold_in(key_of[12], 71), 0)
    query_weight = scatter_about(key_of[2], (D, D), D ** -0.5, 0.21875, ((0, 4), (1, 4)))
    key_weight = scatter_about(key_of[3], (D, D), D ** -0.5, 0.21875, ((0, 4), (1, 4)))
    value_weight = scatter_about(key_of[4], (D, D), D ** -0.5, 0.21875, ((0, 4), (1, 4)))
    output_weight = scatter_about(key_of[5], (D, D), (D // 64) ** -0.5, 1.75, ((0, 4), (1, 4)))
    gate_weight = scatter_about(key_of[6], (D, FF), D ** -0.5, 0.21875, ((0, 4), (1, 4)))
    up_weight = scatter_about(key_of[7], (D, FF), D ** -0.5, 0.21875, ((0, 4), (1, 4)))
    down_weight = scatter_about(key_of[8], (FF, D), FF ** -0.5, 0.125, ((0, 4), (1, 4)))
    first_gain = jnp.clip(1.0 + 0.18 * jax.random.normal(key_of[9], (D,), jnp.float32), 0.099609375, 1.8984375).astype(jnp.bfloat16)
    second_gain = jnp.clip(1.0 + 0.18 * jax.random.normal(key_of[10], (D,), jnp.float32), 0.099609375, 1.8984375).astype(jnp.bfloat16)
    cotangent = heavy_noise(key_of[11], (TOKENS, D), 1.0, 6.0, ((0, 32),), (0, 1, 32, 2.75))
    return dict(inputs=inputs, segment_ids=segment_ids, query_weight=query_weight, key_weight=key_weight, value_weight=value_weight, output_weight=output_weight, gate_weight=gate_weight, up_weight=up_weight, down_weight=down_weight, first_gain=first_gain, second_gain=second_gain, cotangent=cotangent)


@jax.custom_vjp
def low(v):
    return lax.optimization_barrier(v.astype(jnp.bfloat16)).astype(jnp.float32)

@jax.custom_vjp
def low_back(v):
    return v

def low_keep(v):
    return (low(v), None)

def low_pass(kept, grad):
    return (grad,)

def back_keep(v):
    return (v, None)

def back_low(kept, grad):
    return (low(grad),)
low.defvjp(low_keep, low_pass)
low_back.defvjp(back_keep, back_low)
EPSILON = 1e-06
ROPE_BASE = 10000.0
NEGATIVE = -1e+30
HIGHEST = lax.Precision.HIGHEST

def rms_scale(values):
    return lax.rsqrt(lax.optimization_barrier(jnp.mean(values * values, axis=-1, keepdims=True)) + EPSILON)

def seq_positions(segment):
    token_count = segment.shape[0]
    token_index = jnp.arange(token_count, dtype=jnp.int32)
    same_seq = segment[:, None] == segment[None, :]
    starts = lax.optimization_barrier(jnp.min(jnp.where(same_seq, token_index[None, :], token_count), axis=1))
    return (token_index - starts).astype(jnp.int32)

def rotate(values, cosine, sine):
    half = values.shape[-1] // 2
    front = values[..., :half]
    behind = values[..., half:]
    return jnp.concatenate([front * cosine - behind * sine, behind * cosine + front * sine], axis=-1)

def attend(operands):
    queries, keys, values, segment = operands
    token_count = segment.shape[0]
    token_index = jnp.arange(token_count, dtype=jnp.int32)
    allowed = (segment[:, None] == segment[None, :]) & (token_index[None, :] <= token_index[:, None])
    scores = low_back(jnp.einsum('qhd,khd->hqk', queries, keys, precision=HIGHEST))
    logits = jnp.where(allowed[None], scores * queries.shape[-1] ** (-0.5), NEGATIVE)
    row_top = lax.optimization_barrier(jnp.max(logits, axis=-1, keepdims=True))
    weights = jnp.exp(logits - row_top)
    probs = low(weights / lax.optimization_barrier(jnp.sum(weights, axis=-1, keepdims=True)))
    return jnp.einsum('hqk,khd->qhd', probs, values, precision=HIGHEST)

def project(left, right):
    return jnp.dot(left, right, precision=HIGHEST)

def block_forward(inputs, query_weight, key_weight, value_weight, output_weight, gate_weight, up_weight, down_weight, first_gain, second_gain, cosine, sine, segment):
    token_count, model_width = inputs.shape
    head_count = model_width // HEAD_DIM
    blocks = token_count // TOK_DEV
    query_flat = low_back(project(inputs, query_weight)).reshape(token_count, head_count, HEAD_DIM)
    key_flat = low_back(project(inputs, key_weight)).reshape(token_count, head_count, HEAD_DIM)
    values = low(low_back(project(inputs, value_weight))).reshape(token_count, head_count, HEAD_DIM)
    queries = low(rotate(query_flat, cosine, sine))
    keys = low(rotate(key_flat, cosine, sine))
    shape = (blocks, TOK_DEV, head_count, HEAD_DIM)
    mixed = lax.map(jax.checkpoint(attend), (queries.reshape(shape), keys.reshape(shape), values.reshape(shape), segment.reshape(blocks, TOK_DEV)))
    context = low(low_back(mixed.reshape(token_count, model_width)))
    first_sum = inputs + low_back(project(context, output_weight))
    normed = first_sum * rms_scale(first_sum) * first_gain
    hidden_in = low(normed)
    gate_act = low_back(project(hidden_in, gate_weight))
    up_act = low_back(project(hidden_in, up_weight))
    hidden = low(gate_act * jax.nn.sigmoid(gate_act) * up_act)
    second_sum = normed + low_back(project(hidden, down_weight))
    return second_sum * rms_scale(second_sum) * second_gain

def reference(inputs, segment_ids, query_weight, key_weight, value_weight, output_weight, gate_weight, up_weight, down_weight, first_gain, second_gain, cotangent):
    blocks = segment_ids.shape[0] // TOK_DEV
    positions = lax.map(seq_positions, segment_ids.reshape(blocks, TOK_DEV)).reshape(-1).astype(jnp.float32)
    frequencies = ROPE_BASE ** (-2.0 * jnp.arange(HEAD_DIM // 2, dtype=jnp.float32) / HEAD_DIM)
    phases = positions[:, None] * frequencies[None, :]
    cosine = jnp.cos(phases)[:, None, :]
    sine = jnp.sin(phases)[:, None, :]
    forward = partial(block_forward, cosine=cosine, sine=sine, segment=segment_ids)
    primals = tuple((item.astype(jnp.float32) for item in (inputs, query_weight, key_weight, value_weight, output_weight, gate_weight, up_weight, down_weight, first_gain, second_gain)))
    layer_out, pullback = jax.vjp(forward, *primals)
    grads = pullback(cotangent.astype(jnp.float32))
    return (layer_out.astype(jnp.bfloat16), grads[0].astype(jnp.bfloat16), grads[1], grads[2], grads[3], grads[4], grads[5], grads[6], grads[7], grads[8], grads[9])
```

```python
import jax
import jax.numpy as jnp
from jax import lax
from jax.experimental import pallas as pl
from jax.experimental.pallas import tpu as pltpu
from jax.sharding import PartitionSpec as P

HEAD_DIM = 64
EPSILON = 1e-06
ROPE_BASE = 10000.0
NEGATIVE = -1e30
LOG2E = 1.4426950408889634
QUERY_BLOCK = 256
LANES = 128
BF16 = jnp.bfloat16
F32 = jnp.float32
EVERYWHERE = ("dp", "row", "col")


def dot_nn(left, right):
    return lax.dot_general(left, right, (((1,), (0,)), ((), ())), preferred_element_type=F32)


def dot_nt(left, right):
    return lax.dot_general(left, right, (((1,), (1,)), ((), ())), preferred_element_type=F32)


def bit_count(size):
    return size.bit_length() - 1


def bit_order(grid_rows, grid_cols, core):
    col_bits = [("col", b) for b in range(bit_count(grid_cols))]
    row_bits = [("row", b) for b in range(bit_count(grid_rows))]
    return (col_bits[::-1] + row_bits[::-1]) if core else (col_bits + row_bits)


def step_pairs(grid_rows, grid_cols, step):
    pairs = []
    for core in range(2):
        axis, bit = bit_order(grid_rows, grid_cols, core)[step]
        for row in range(grid_rows):
            for col in range(grid_cols):
                to_row = row ^ (1 << bit) if axis == "row" else row
                to_col = col ^ (1 << bit) if axis == "col" else col
                source = (core * grid_rows + row) * grid_cols + col
                target = (core * grid_rows + to_row) * grid_cols + to_col
                pairs.append((source, target))
    return pairs


def other_core(value):
    return lax.ppermute(value, "dp", [(0, 1), (1, 0)])


def gather_blocks(mine, grid_rows, grid_cols):
    steps = bit_count(grid_rows) + bit_count(grid_cols)
    held = mine[None]
    for step in range(steps):
        came = lax.ppermute(held, EVERYWHERE, step_pairs(grid_rows, grid_cols, step))
        if step < steps - 1:
            held = jnp.concatenate([held, came], axis=0)
    return held, came, other_core(held), other_core(came)


def scatter_blocks(own, other, grid_rows, grid_cols):
    steps = bit_count(grid_rows) + bit_count(grid_cols)
    terms = [own, other_core(other)]
    for step in reversed(range(steps)):
        half = terms[0].shape[0] // 2
        away = sum(term[half:].astype(F32) for term in terms).astype(BF16)
        came = lax.ppermute(away, EVERYWHERE, step_pairs(grid_rows, grid_cols, step))
        terms = [term[:half] for term in terms] + [came]
    mine = sum(term[0].astype(F32) for term in terms).astype(BF16)
    theirs = other_core(mine)
    first = lax.axis_index("dp") == 0
    return jnp.stack([jnp.where(first, mine, theirs), jnp.where(first, theirs, mine)]).astype(F32)


def reversed_bits(value, bits):
    out = 0
    for b in range(bits):
        out = out | (((value >> b) & 1) << (bits - 1 - b))
    return out


def place_of(row, col, place, core, grid_rows, grid_cols):
    far_row = row ^ place[0]
    far_col = col ^ place[1]
    row_bits = bit_count(grid_rows)
    col_bits = bit_count(grid_cols)
    plain = far_col + far_row * grid_cols
    turned = reversed_bits(far_col, col_bits) + reversed_bits(far_row, row_bits) * grid_cols
    return jnp.where(core == 0, plain, turned)


def pack_pair(first, second, odd):
    body_a = jnp.where(odd, first[:, 64:], first[:, :128])
    body_b = jnp.where(odd, second[:, 64:], second[:, :128])
    rest_a = jnp.where(odd, first[:, :64], first[:, 128:])
    rest_b = jnp.where(odd, second[:, :64], second[:, 128:])
    low = jnp.where(odd, rest_b, rest_a)
    high = jnp.where(odd, rest_a, rest_b)
    return jnp.concatenate([body_a, body_b, low, high], axis=1)


def unpack_pair(packed, odd):
    body_a, body_b = packed[:, :128], packed[:, 128:256]
    low, high = packed[:, 256:320], packed[:, 320:384]
    rest_a = jnp.where(odd, high, low)
    rest_b = jnp.where(odd, low, high)
    first = jnp.where(odd, jnp.concatenate([rest_a, body_a], axis=1), jnp.concatenate([body_a, rest_a], axis=1))
    second = jnp.where(odd, jnp.concatenate([rest_b, body_b], axis=1), jnp.concatenate([body_b, rest_b], axis=1))
    return first, second


def halves_of(block, core):
    half = block.shape[0] // 2
    return lax.dynamic_slice_in_dim(block, core * half, half, axis=0)


def pack_attention(query_weight, key_weight, value_weight, core, odd):
    query, key, value = (halves_of(w, core) for w in (query_weight, key_weight, value_weight))
    quarter = value.shape[0] // 2
    return jnp.concatenate(
        [pack_pair(query, key, odd), pack_pair(value[:quarter], value[quarter:], odd)], axis=0
    )


def pack_feed(gate, up, down_turned, output, gain_one, gain_two, core, odd):
    gate, up, down_turned, output = (halves_of(w, core) for w in (gate, up, down_turned, output))
    quarter = output.shape[0] // 2
    packed = pack_pair(output[:quarter], output[quarter:], odd)
    gains = jnp.stack([gain_one, gain_two])
    gains = jnp.pad(gains, ((0, quarter - 2), (0, LANES - gains.shape[1])))
    return jnp.concatenate([gate, up, down_turned, jnp.concatenate([packed, gains], axis=1)], axis=0)


def place_scalars():
    return jnp.stack([lax.axis_index("row"), lax.axis_index("col"), lax.axis_index("dp")]).astype(jnp.int32)


def split_rows(top):
    return lax.broadcasted_iota(jnp.int32, top, 1) < 64


def fill_columns(target, rows, low_even, body_even, low_odd, body_odd, pair, swapped):
    base = 384 * pair
    target[rows, base : base + 128] = body_even
    target[rows, base + 256 : base + 384] = body_odd
    first = split_rows(low_even.shape)
    if swapped:
        mixed = jnp.where(first, low_odd, low_even)
        target[rows, base + 128 : base + 256] = pltpu.roll(mixed.astype(F32), 64, 1).astype(BF16)
    else:
        target[rows, base + 128 : base + 256] = jnp.where(first, low_even, low_odd)


def load_stacks(refs, held, sems):
    count = refs[0].shape[0]
    copies = []
    for k, ref in enumerate(refs):
        copies.append(pltpu.make_async_copy(ref, held.at[k // 2, pl.ds((k % 2) * count, count)], sems.at[k]))
    for copy in copies:
        copy.start()
    for copy in copies:
        copy.wait()


def assemble_attention_body(grid, place, m0, m1, o0, o1, w_query, w_key, w_value, held, sems):
    grid_rows, grid_cols = grid
    load_stacks((m0, m1, o0, o1), held, sems)
    where = (place[0], place[1])
    half = w_query.shape[0] // grid_rows // 2
    quarter = half // 2
    for core in range(2):
        side = core ^ place[2]
        for row in range(grid_rows):
            start = row * 2 * half + core * half
            for pair in range(grid_cols // 2):
                at = [place_of(row, 2 * pair + c, where, core, grid_rows, grid_cols) for c in range(2)]
                even, odd = (held.at[side, p] for p in at)
                top = slice(0, half)
                rows = slice(start, start + half)
                rest_even, rest_odd = even[top, 256:384], odd[top, 256:384]
                fill_columns(w_query, rows, rest_even, even[top, 0:128], rest_odd, odd[top, 0:128], pair, False)
                fill_columns(w_key, rows, rest_even, even[top, 128:256], rest_odd, odd[top, 128:256], pair, True)
                low = slice(half, half + quarter)
                rest_even, rest_odd = even[low, 256:384], odd[low, 256:384]
                rows = slice(start, start + quarter)
                fill_columns(w_value, rows, rest_even, even[low, 0:128], rest_odd, odd[low, 0:128], pair, False)
                rows = slice(start + quarter, start + half)
                fill_columns(w_value, rows, rest_even, even[low, 128:256], rest_odd, odd[low, 128:256], pair, True)


def assemble_attention(stacks, place, grid, width):
    count, height, lanes = stacks[0].shape
    whole = jax.ShapeDtypeStruct((width, width), BF16)
    anywhere = pl.BlockSpec(memory_space=pl.ANY)
    vmem = pl.BlockSpec(memory_space=pltpu.VMEM)
    return pl.pallas_call(
        lambda *refs: assemble_attention_body(grid, *refs),
        in_specs=[pl.BlockSpec(memory_space=pltpu.SMEM)] + [anywhere] * 4,
        out_specs=[vmem] * 3,
        out_shape=[whole] * 3,
        scratch_shapes=[pltpu.VMEM((2, 2 * count, height, lanes), BF16), pltpu.SemaphoreType.DMA((4,))],
        name="assemble_attention",
    )(place, *stacks)


def assemble_feed_body(grid, place, m0, m1, o0, o1, w_gate, w_up, w_down, w_output, gains, held, sems):
    grid_rows, grid_cols = grid
    load_stacks((m0, m1, o0, o1), held, sems)
    where = (place[0], place[1])
    half = w_gate.shape[0] // grid_rows // 2
    span = w_gate.shape[1] // grid_cols
    quarter = half // 2
    share = gains.shape[1] // (grid_rows * grid_cols)
    width = gains.shape[1]
    lane = lax.broadcasted_iota(jnp.int32, (LANES, width), 1)
    spread = (lax.rem(lane, share) == lax.broadcasted_iota(jnp.int32, (LANES, width), 0)).astype(BF16)
    block_of = lax.div(lax.broadcasted_iota(jnp.int32, (16, width), 1), share)
    total = jnp.zeros((16, width), F32)
    for core in range(2):
        side = core ^ place[2]
        for row in range(grid_rows):
            start = row * 2 * half + core * half
            for col in range(grid_cols):
                block = held.at[side, place_of(row, col, where, core, grid_rows, grid_cols)]
                for k, target in enumerate((w_gate, w_up)):
                    target[start : start + half, col * span : (col + 1) * span] = block[k * half : (k + 1) * half, :]
                turned = col * 2 * half + core * half
                w_down[turned : turned + half, row * span : (row + 1) * span] = block[2 * half : 3 * half, :]
            for pair in range(grid_cols // 2):
                at = [place_of(row, 2 * pair + c, where, core, grid_rows, grid_cols) for c in range(2)]
                even, odd = (held.at[side, p] for p in at)
                low = slice(3 * half, 3 * half + quarter)
                rest_even, rest_odd = even[low, 256:384], odd[low, 256:384]
                rows = slice(start, start + quarter)
                fill_columns(w_output, rows, rest_even, even[low, 0:128], rest_odd, odd[low, 0:128], pair, False)
                rows = slice(start + quarter, start + half)
                fill_columns(w_output, rows, rest_even, even[low, 128:256], rest_odd, odd[low, 128:256], pair, True)
                if core == 0:
                    for c, block in enumerate((even, odd)):
                        spreaded = dot_nn(block[3 * half : 3 * half + 16, 384:512], spread)
                        total = total + jnp.where(block_of == row * grid_cols + 2 * pair + c, spreaded, 0.0)
    gains[...] = total[:8]


def assemble_feed(stacks, place, grid, width, hidden):
    count, height, lanes = stacks[0].shape
    anywhere = pl.BlockSpec(memory_space=pl.ANY)
    vmem = pl.BlockSpec(memory_space=pltpu.VMEM)
    return pl.pallas_call(
        lambda *refs: assemble_feed_body(grid, *refs),
        in_specs=[pl.BlockSpec(memory_space=pltpu.SMEM)] + [anywhere] * 4,
        out_specs=[vmem] * 5,
        out_shape=[jax.ShapeDtypeStruct((width, hidden), BF16)] * 3
        + [jax.ShapeDtypeStruct((width, width), BF16), jax.ShapeDtypeStruct((8, width), F32)],
        scratch_shapes=[pltpu.VMEM((2, 2 * count, height, lanes), BF16), pltpu.SemaphoreType.DMA((4,))],
        name="assemble_feed",
    )(place, *stacks)


def swap_halves(values):
    lane = lax.broadcasted_iota(jnp.int32, values.shape, 1)
    back = pltpu.roll(values, 32, 1)
    ahead = pltpu.roll(values, LANES - 32, 1)
    return jnp.where(lax.rem(lane, HEAD_DIM) < HEAD_DIM // 2, ahead, back)


def project_body(x, w_query, w_key, w_value, cosine, sine, query, key, value):
    width = w_query.shape[1]
    step = 256
    for start in range(0, width, step):
        for weight, out in ((w_query, query), (w_key, key)):
            flat = dot_nn(x[...], weight[:, start : start + step])
            for k in range(step // LANES):
                part = flat[:, k * LANES : (k + 1) * LANES]
                turned = part * cosine[...] + swap_halves(part) * sine[...]
                out[:, start + k * LANES : start + (k + 1) * LANES] = turned.astype(BF16)
        value[:, start : start + step] = dot_nn(x[...], w_value[:, start : start + step]).astype(BF16)


def project(x, w_query, w_key, w_value, cosine, sine):
    tokens, width = x.shape
    rows = 256
    tile = pl.BlockSpec((rows, width), lambda i: (i, 0))
    table = pl.BlockSpec((rows, LANES), lambda i: (i, 0))
    whole = pl.BlockSpec((width, width), lambda i: (0, 0))
    return pl.pallas_call(
        project_body,
        grid=(tokens // rows,),
        in_specs=[tile, whole, whole, whole, table, table],
        out_specs=[tile] * 3,
        out_shape=[jax.ShapeDtypeStruct((tokens, width), BF16)] * 3,
        name="project_heads",
    )(x, w_query, w_key, w_value, cosine, sine)


def attention_forward_body(first, q_ref, k_ref, v_ref, context_ref, lse_ref):
    blocks = q_ref.shape[0] // QUERY_BLOCK
    q_turned = (q_ref[...].astype(F32) * HEAD_DIM**-0.5).T.astype(BF16)
    v_turned = v_ref[...].T
    zero = jnp.zeros((HEAD_DIM, QUERY_BLOCK), BF16)
    square = (QUERY_BLOCK, QUERY_BLOCK)
    causal = lax.broadcasted_iota(jnp.int32, square, 0) <= lax.broadcasted_iota(jnp.int32, square, 1)
    lse_ref[...] = jnp.zeros_like(lse_ref)
    for i in range(blocks):
        now = slice(i * QUERY_BLOCK, (i + 1) * QUERY_BLOCK)
        outs = []
        for h in range(2):
            head = slice(h * HEAD_DIM, (h + 1) * HEAD_DIM)
            mine = q_turned[head, now]
            mine = jnp.concatenate([mine, zero] if h == 0 else [zero, mine], axis=0)
            scores = [dot_nn(k_ref[b * QUERY_BLOCK : (b + 1) * QUERY_BLOCK, :], mine) for b in range(i + 1)]
            scores[i] = jnp.where(causal, scores[i], NEGATIVE)
            top = jnp.max(scores[i], axis=0, keepdims=True)
            for b in range(i):
                block_top = jnp.max(scores[b], axis=0, keepdims=True)
                top = jnp.maximum(top, jnp.where(first[i] <= b, block_top, NEGATIVE))
            top = top * LOG2E
            mixed = None
            total = None
            for b in range(i + 1):
                base = top if b == i else top + jnp.where(first[i] <= b, 0.0, -NEGATIVE)
                weights = jnp.exp2(scores[b] * LOG2E - base)
                part_total = jnp.sum(weights, axis=0, keepdims=True)
                part = dot_nn(v_turned[head, b * QUERY_BLOCK : (b + 1) * QUERY_BLOCK], weights.astype(BF16))
                mixed = part if mixed is None else mixed + part
                total = part_total if total is None else total + part_total
            outs.append(mixed * (1.0 / total))
            lse_ref[0, h : h + 1, now] = top + jnp.log2(total)
        context_ref[now, :] = jnp.concatenate(outs, axis=0).T.astype(BF16)


def attention_forward(first, query, key, value):
    tokens, width = query.shape
    pairs = width // LANES
    spec = pl.BlockSpec((tokens, LANES), lambda j, f: (0, j))
    return pl.pallas_call(
        attention_forward_body,
        grid_spec=pltpu.PrefetchScalarGridSpec(
            num_scalar_prefetch=1,
            grid=(pairs,),
            in_specs=[spec] * 3,
            out_specs=[spec, pl.BlockSpec((1, 8, tokens), lambda j, f: (j, 0, 0))],
        ),
        out_shape=[
            jax.ShapeDtypeStruct((tokens, width), BF16),
            jax.ShapeDtypeStruct((pairs, 8, tokens), F32),
        ],
        name="attention_forward",
    )(first, query, key, value)


def attention_backward_body(first, q_ref, k_ref, v_ref, grad_ref, context_ref, lse_ref, cosine, sine, dq_ref, dk_ref, dv_ref, dk_sum, dv_sum):
    blocks = q_ref.shape[0] // QUERY_BLOCK
    scaled = q_ref[...].astype(F32) * HEAD_DIM**-0.5
    q_turned = scaled.T.astype(BF16)
    q_plain = scaled.astype(BF16)
    k_turned = k_ref[...].T
    grad = grad_ref[...]
    grad_turned = grad.T
    inner = (grad.astype(F32) * context_ref[...].astype(F32)).T
    zero = jnp.zeros((HEAD_DIM, QUERY_BLOCK), BF16)
    square = (QUERY_BLOCK, QUERY_BLOCK)
    causal = lax.broadcasted_iota(jnp.int32, square, 0) <= lax.broadcasted_iota(jnp.int32, square, 1)
    low_lanes = lax.broadcasted_iota(jnp.int32, (QUERY_BLOCK, LANES), 1) < HEAD_DIM
    for i in range(blocks):
        now = slice(i * QUERY_BLOCK, (i + 1) * QUERY_BLOCK)
        grads = []
        for h in range(2):
            head = slice(h * HEAD_DIM, (h + 1) * HEAD_DIM)
            own_lanes = low_lanes if h == 0 else jnp.logical_not(low_lanes)
            q_cols, g_cols = (
                jnp.concatenate([part[head, now], zero] if h == 0 else [zero, part[head, now]], axis=0)
                for part in (q_turned, grad_turned)
            )
            q_rows = jnp.where(own_lanes, q_plain[now, :], 0)
            g_rows = jnp.where(own_lanes, grad[now, :], 0)
            delta = jnp.sum(inner[head, now], axis=0, keepdims=True)
            lse = lse_ref[0, h : h + 1, now]
            dq = None
            for b in range(i + 1):
                there = slice(b * QUERY_BLOCK, (b + 1) * QUERY_BLOCK)
                scores = dot_nn(k_ref[there, :], q_cols)
                base = lse if b == i else lse + jnp.where(first[i] <= b, 0.0, -NEGATIVE)
                if b == i:
                    scores = jnp.where(causal, scores, NEGATIVE)
                probs = jnp.exp2(scores * LOG2E - base)
                grad_probs = dot_nn(v_ref[there, :], g_cols)
                grad_scores = (probs * (grad_probs - delta)).astype(BF16)
                dv = dot_nn(probs.astype(BF16), g_rows)
                dk = dot_nn(grad_scores, q_rows)
                if b == i and h == 0:
                    dv_sum[there, :] = dv
                    dk_sum[there, :] = dk
                else:
                    dv_sum[there, :] += dv
                    dk_sum[there, :] += dk
                part = dot_nn(k_turned[head, there], grad_scores)
                dq = part if dq is None else dq + part
            grads.append(dq * HEAD_DIM**-0.5)
        dq = jnp.concatenate(grads, axis=0).T
        dq_ref[now, :] = (dq * cosine[now, :] - swap_halves(dq) * sine[now, :]).astype(BF16)
    dk = dk_sum[...]
    dk_ref[...] = (dk * cosine[...] - swap_halves(dk) * sine[...]).astype(BF16)
    dv_ref[...] = dv_sum[...].astype(BF16)


def attention_backward(first, query, key, value, grad, context, lse, cosine, sine):
    tokens, width = query.shape
    pairs = width // LANES
    spec = pl.BlockSpec((tokens, LANES), lambda j, f: (0, j))
    table = pl.BlockSpec((tokens, LANES), lambda j, f: (0, 0))
    return pl.pallas_call(
        attention_backward_body,
        grid_spec=pltpu.PrefetchScalarGridSpec(
            num_scalar_prefetch=1,
            grid=(pairs,),
            in_specs=[spec] * 5 + [pl.BlockSpec((1, 8, tokens), lambda j, f: (j, 0, 0)), table, table],
            out_specs=[spec] * 3,
            scratch_shapes=[pltpu.VMEM((tokens, LANES), F32)] * 2,
        ),
        out_shape=[jax.ShapeDtypeStruct((tokens, width), BF16)] * 3,
        name="attention_backward",
    )(first, query, key, value, grad, context, lse, cosine, sine)


def middle_body(
    context, x, cotangent, w_output, w_gate, w_up, w_down, gains,
    layer_out, hidden_in_turned, branch_two_turned, context_turned, hidden, grad_gate, grad_up, grad_first, branch_one, grad_context, gain_grads,
    slope, act,
):
    width = x.shape[1]
    span = w_gate.shape[1]
    chunk = 512
    gain_one = gains[0:1, :]
    gain_two = gains[1:2, :]
    context_now = context[...]
    first_sum = x[...].astype(F32) + dot_nn(context_now, w_output[...])
    scale_one = lax.rsqrt(jnp.mean(first_sum * first_sum, axis=1, keepdims=True) + EPSILON)
    normed_one = first_sum * scale_one
    normed = normed_one * gain_one
    hidden_in = normed.astype(BF16)
    second_sum = normed
    for start in range(0, span, chunk):
        cols = slice(start, start + chunk)
        gate_act = dot_nn(hidden_in, w_gate[:, cols])
        up_act = dot_nn(hidden_in, w_up[:, cols])
        sigmoid = jax.nn.sigmoid(gate_act)
        silu = gate_act * sigmoid
        act[:, cols] = silu
        slope[:, cols] = up_act * (sigmoid + silu * (1.0 - sigmoid))
        hidden_now = (silu * up_act).astype(BF16)
        hidden[:, cols] = hidden_now
        second_sum = second_sum + dot_nt(hidden_now, w_down[:, cols])
    scale_two = lax.rsqrt(jnp.mean(second_sum * second_sum, axis=1, keepdims=True) + EPSILON)
    normed_two = second_sum * scale_two
    layer_out[...] = (normed_two * gain_two).astype(BF16)
    grad_out = cotangent[...].astype(F32)
    two_term = jnp.sum(grad_out * normed_two, axis=0, keepdims=True)
    scaled = grad_out * gain_two
    grad_second = scale_two * (scaled - normed_two * jnp.mean(scaled * normed_two, axis=1, keepdims=True))
    branch_two = grad_second.astype(BF16)
    grad_normed = grad_second
    for start in range(0, span, chunk):
        cols = slice(start, start + chunk)
        grad_hidden = dot_nn(branch_two, w_down[:, cols])
        gate_now = (grad_hidden * slope[:, cols]).astype(BF16)
        up_now = (grad_hidden * act[:, cols]).astype(BF16)
        grad_gate[:, cols] = gate_now
        grad_up[:, cols] = up_now
        grad_normed = grad_normed + dot_nt(gate_now, w_gate[:, cols]) + dot_nt(up_now, w_up[:, cols])
    one_term = jnp.sum(grad_normed * normed_one, axis=0, keepdims=True)
    scaled = grad_normed * gain_one
    first_grad = scale_one * (scaled - normed_one * jnp.mean(scaled * normed_one, axis=1, keepdims=True))
    grad_first[...] = first_grad
    one_now = first_grad.astype(BF16)
    branch_one[...] = one_now
    grad_context[...] = dot_nt(one_now, w_output[...]).astype(BF16)
    hidden_in_turned[...] = hidden_in.T
    branch_two_turned[...] = branch_two.T
    context_turned[...] = context_now.T
    terms = jnp.concatenate([one_term, two_term, jnp.zeros((6, width), F32)], axis=0)

    @pl.when(pl.program_id(0) == 0)
    def _():
        gain_grads[...] = terms

    @pl.when(pl.program_id(0) > 0)
    def _():
        gain_grads[...] += terms


def middle(context, x, cotangent, w_output, w_gate, w_up, w_down, gains):
    tokens, width = x.shape
    span = w_gate.shape[1]
    rows = 256
    tile = pl.BlockSpec((rows, width), lambda i: (i, 0))
    wide = pl.BlockSpec((rows, span), lambda i: (i, 0))
    turned = pl.BlockSpec((width, rows), lambda i: (0, i))
    square = pl.BlockSpec((width, width), lambda i: (0, 0), pipeline_mode=pl.Buffered(1))
    whole = pl.BlockSpec((width, span), lambda i: (0, 0), pipeline_mode=pl.Buffered(1))
    eight = pl.BlockSpec((8, width), lambda i: (0, 0))
    flat = jax.ShapeDtypeStruct((tokens, width), BF16)
    flat_turned = jax.ShapeDtypeStruct((width, tokens), BF16)
    broad = jax.ShapeDtypeStruct((tokens, span), BF16)
    return pl.pallas_call(
        middle_body,
        grid=(tokens // rows,),
        in_specs=[tile, tile, tile, square, whole, whole, whole, eight],
        out_specs=[tile, turned, turned, turned, wide, wide, wide, tile, tile, tile, eight],
        out_shape=[
            flat, flat_turned, flat_turned, flat_turned, broad, broad, broad,
            jax.ShapeDtypeStruct((tokens, width), F32), flat, flat, jax.ShapeDtypeStruct((8, width), F32),
        ],
        scratch_shapes=[pltpu.VMEM((rows, span), F32)] * 2,
        name="feed_forward_and_back",
    )(context, x, cotangent, w_output, w_gate, w_up, w_down, gains)


def store_halves(own, other, where, grid, core_here, row, col, rows, lanes, halves):
    grid_rows, grid_cols = grid
    here = core_here == 0
    at_own = place_of(row, col, where, core_here, grid_rows, grid_cols)
    at_other = place_of(row, col, where, 1 - core_here, grid_rows, grid_cols)
    own[at_own, rows, lanes] = jnp.where(here, halves[0], halves[1])
    other[at_other, rows, lanes] = jnp.where(here, halves[1], halves[0])


def rest_tile(first, second, odd):
    low = split_rows(first.shape)
    rolled = pltpu.roll(second, 64, 1)
    return jnp.where(low, rolled, first) if odd else jnp.where(low, first, rolled)


def feed_grads_body(grid, place, hidden_in_turned, branch_two_turned, context_turned, hidden, grad_gate, grad_up, branch_one, gain_grads, own, other):
    grid_rows, grid_cols = grid
    where = (place[0], place[1])
    width = hidden_in_turned.shape[0]
    half = width // grid_rows // 2
    quarter = half // 2
    span = hidden.shape[1]
    col = pl.program_id(0)
    for k, (left, right) in enumerate(
        ((hidden_in_turned, grad_gate), (hidden_in_turned, grad_up), (branch_two_turned, hidden))
    ):
        product = dot_nn(left[...], right[...]).astype(BF16)
        for row in range(grid_rows):
            halves = [product[row * 2 * half + c * half :][:half] for c in range(2)]
            at = (row, col) if k < 2 else (col, row)
            store_halves(own, other, where, grid, place[2], *at, slice(k * half, (k + 1) * half), slice(0, span), halves)

    @pl.when(col == 0)
    def _():
        product = dot_nn(context_turned[...], branch_one[...])
        share = width // (grid_rows * grid_cols)
        lane = lax.broadcasted_iota(jnp.int32, (width, LANES), 0)
        gather = (lax.rem(lane, share) == lax.broadcasted_iota(jnp.int32, (width, LANES), 1)).astype(BF16)
        block_of = lax.div(lax.broadcasted_iota(jnp.int32, (8, width), 1), share)
        sums = gain_grads[...]
        base = 3 * half
        for row in range(grid_rows):
            for c in range(grid_cols):
                tile = 384 * (c // 2)
                odd = c % 2
                bodies, rests = [], []
                for core in range(2):
                    start = row * 2 * half + core * half
                    lanes = slice(tile + 256 * odd, tile + 256 * odd + 128)
                    mid = slice(tile + 128, tile + 256)
                    top, low = slice(start, start + quarter), slice(start + quarter, start + half)
                    bodies.append((product[top, lanes], product[low, lanes]))
                    rests.append(rest_tile(product[top, mid], product[low, mid], odd))
                rows = slice(base, base + quarter)
                for k in range(2):
                    store_halves(own, other, where, grid, place[2], row, c, rows, slice(128 * k, 128 * (k + 1)), [b[k].astype(BF16) for b in bodies])
                store_halves(own, other, where, grid, place[2], row, c, rows, slice(256, 384), [r.astype(BF16) for r in rests])
                picked = jnp.where(block_of == row * grid_cols + c, sums, 0.0).astype(BF16)
                gain = dot_nn(picked, gather)
                gain = jnp.concatenate([gain, jnp.zeros((quarter - 8, LANES), F32)], axis=0).astype(BF16)
                store_halves(own, other, where, grid, place[2], row, c, rows, slice(384, 512), [gain, gain])


def feed_grads(place, grid, hidden_in_turned, branch_two_turned, context_turned, hidden, grad_gate, grad_up, branch_one, gain_grads):
    width, tokens = hidden_in_turned.shape
    grid_rows, grid_cols = grid
    span = hidden.shape[1] // grid_cols
    half = width // grid_rows // 2
    turned = pl.BlockSpec((width, tokens), lambda i, s: (0, 0), pipeline_mode=pl.Buffered(1))
    piece = pl.BlockSpec((tokens, span), lambda i, s: (0, i))
    flat = pl.BlockSpec((tokens, width), lambda i, s: (0, 0), pipeline_mode=pl.Buffered(1))
    eight = pl.BlockSpec((8, width), lambda i, s: (0, 0))
    shape = (grid_rows * grid_cols, 3 * half + half // 2, span)
    out = pl.BlockSpec(shape, lambda i, s: (0, 0, 0), pipeline_mode=pl.Buffered(1))
    return pl.pallas_call(
        lambda *refs: feed_grads_body(grid, *refs),
        grid_spec=pltpu.PrefetchScalarGridSpec(
            num_scalar_prefetch=1,
            grid=(grid_cols,),
            in_specs=[turned] * 3 + [piece] * 3 + [flat, eight],
            out_specs=[out] * 2,
        ),
        out_shape=[jax.ShapeDtypeStruct(shape, BF16)] * 2,
        name="feed_forward_weight_grads",
    )(place, hidden_in_turned, branch_two_turned, context_turned, hidden, grad_gate, grad_up, branch_one, gain_grads)


def attention_grads_body(grid, place, x_turned, grad_query, grad_key, grad_value, own, other):
    grid_rows, grid_cols = grid
    where = (place[0], place[1])
    width = x_turned.shape[0]
    half = width // grid_rows // 2
    quarter = half // 2
    query, key, value = (dot_nn(x_turned[...], g[...]) for g in (grad_query, grad_key, grad_value))
    for row in range(grid_rows):
        for c in range(grid_cols):
            odd = c % 2
            lanes = slice(256 * odd, 256 * odd + 128)
            tile = 384 * (c // 2)
            body = slice(tile + 256 * odd, tile + 256 * odd + 128)
            mid = slice(tile + 128, tile + 256)
            parts = []
            for core in range(2):
                start = row * 2 * half + core * half
                rows = slice(start, start + half)
                top, low = slice(start, start + quarter), slice(start + quarter, start + half)
                pair = (query[rows, body], key[rows, body], rest_tile(query[rows, mid], key[rows, mid], odd))
                last = (value[top, body], value[low, body], rest_tile(value[top, mid], value[low, mid], odd))
                parts.append([p.astype(BF16) for p in pair + last])
            for k in range(3):
                lanes = slice(128 * k, 128 * (k + 1))
                store_halves(own, other, where, grid, place[2], row, c, slice(0, half), lanes, [p[k] for p in parts])
                store_halves(own, other, where, grid, place[2], row, c, slice(half, half + quarter), lanes, [p[3 + k] for p in parts])


def attention_grads(place, grid, x_turned, grad_query, grad_key, grad_value):
    width, tokens = x_turned.shape
    grid_rows, grid_cols = grid
    half = width // grid_rows // 2
    vmem = pl.BlockSpec(memory_space=pltpu.VMEM)
    shape = (grid_rows * grid_cols, half + half // 2, 384)
    return pl.pallas_call(
        lambda *refs: attention_grads_body(grid, *refs),
        in_specs=[pl.BlockSpec(memory_space=pltpu.SMEM)] + [vmem] * 4,
        out_specs=[vmem] * 2,
        out_shape=[jax.ShapeDtypeStruct(shape, BF16)] * 2,
        name="attention_weight_grads",
    )(place, x_turned, grad_query, grad_key, grad_value)


def input_grad_body(grad_first, grad_query, grad_key, grad_value, w_query, w_key, w_value, out):
    total = grad_first[...]
    for grad, weight in ((grad_query, w_query), (grad_key, w_key), (grad_value, w_value)):
        total = total + dot_nt(grad[...], weight[...])
    out[...] = total.astype(BF16)


def input_gradient(grad_first, grad_query, grad_key, grad_value, w_query, w_key, w_value):
    tokens, width = grad_first.shape
    rows = 256
    tile = pl.BlockSpec((rows, width), lambda i: (i, 0))
    whole = pl.BlockSpec((width, width), lambda i: (0, 0), pipeline_mode=pl.Buffered(1))
    return pl.pallas_call(
        input_grad_body,
        grid=(tokens // rows,),
        in_specs=[tile] * 4 + [whole] * 3,
        out_specs=tile,
        out_shape=jax.ShapeDtypeStruct((tokens, width), BF16),
        name="input_gradient",
    )(grad_first, grad_query, grad_key, grad_value, w_query, w_key, w_value)


def gather_plain(block):
    whole = lax.all_gather(block, "col", axis=1, tiled=True)
    return lax.all_gather(whole, "row", axis=0, tiled=True)


def scatter_plain(whole):
    part = lax.psum_scatter(whole.astype(BF16), "row", scatter_dimension=0, tiled=True)
    part = lax.psum_scatter(part, "col", scatter_dimension=1, tiled=True)
    return lax.psum(part, "dp").astype(F32)


def scatter_gain(whole):
    part = lax.psum_scatter(whole.astype(BF16), ("row", "col"), scatter_dimension=0, tiled=True)
    return lax.psum(part, "dp").astype(F32)


def on_device(
    inputs,
    segment_ids,
    query_weight,
    key_weight,
    value_weight,
    output_weight,
    gate_weight,
    up_weight,
    down_weight,
    first_gain,
    second_gain,
    cotangent,
):
    grid = (lax.axis_size("row"), lax.axis_size("col"))
    tokens, width = inputs.shape
    hidden_width = gate_weight.shape[1] * grid[1]
    core = lax.axis_index("dp")
    odd = (lax.axis_index("col") & 1) == 1
    place = place_scalars()
    packs = grid == (4, 4) and query_weight.shape[1] == 192 and gate_weight.shape[1] == 512

    token_index = jnp.arange(tokens, dtype=jnp.int32)
    same = segment_ids[:, None] == segment_ids[None, :]
    starts = jnp.min(jnp.where(same, token_index[None, :], tokens), axis=1)
    positions = (token_index - starts).astype(F32)
    frequencies = ROPE_BASE ** (-2.0 * jnp.arange(HEAD_DIM // 2, dtype=F32) / HEAD_DIM)
    phases = positions[:, None] * frequencies[None, :]
    cosine = jnp.tile(jnp.cos(phases), (1, 4))
    sine = jnp.sin(phases)
    sine = jnp.tile(jnp.concatenate([-sine, sine], axis=1), (1, 2))
    first = starts[::QUERY_BLOCK] // QUERY_BLOCK
    x_turned = inputs.T

    if packs:
        stacks = gather_blocks(pack_attention(query_weight, key_weight, value_weight, core, odd), *grid)
        w_query, w_key, w_value = assemble_attention(stacks, place, grid, width)
        feed = pack_feed(gate_weight, up_weight, down_weight.T, output_weight, first_gain, second_gain, core, odd)
        feed_stacks = gather_blocks(feed, *grid)
        w_gate, w_up, w_down, w_output, gains = assemble_feed(feed_stacks, place, grid, width, hidden_width)
    else:
        w_query, w_key, w_value, w_output = (
            gather_plain(w) for w in (query_weight, key_weight, value_weight, output_weight)
        )
        w_gate, w_up, w_down = gather_plain(gate_weight), gather_plain(up_weight), gather_plain(down_weight).T
        gains = jnp.stack(
            [lax.all_gather(g, ("row", "col"), axis=0, tiled=True).astype(F32) for g in (first_gain, second_gain)]
        )
        gains = jnp.pad(gains, ((0, 6), (0, 0)))

    query, key, value = project(inputs, w_query, w_key, w_value, cosine, sine)
    context, lse = attention_forward(first, query, key, value)
    (
        layer_out, hidden_in_turned, branch_two_turned, context_turned, hidden, grad_gate, grad_up, grad_first, branch_one, grad_context, gain_grads,
    ) = middle(context, inputs, cotangent, w_output, w_gate, w_up, w_down, gains)

    if packs:
        feed_own, feed_other = feed_grads(
            place, grid, hidden_in_turned, branch_two_turned, context_turned, hidden, grad_gate, grad_up, branch_one, gain_grads
        )
        feed_sum = scatter_blocks(feed_own, feed_other, *grid)
    grad_query, grad_key, grad_value = attention_backward(first, query, key, value, grad_context, context, lse, cosine, sine)
    if packs:
        own, other = attention_grads(place, grid, x_turned, grad_query, grad_key, grad_value)
        heads_sum = scatter_blocks(own, other, *grid)
    input_grad = input_gradient(grad_first, grad_query, grad_key, grad_value, w_query, w_key, w_value)

    if packs:
        half = query_weight.shape[0] // 2
        quarter = half // 2
        gate_out, up_out, down_out = (
            jnp.concatenate([feed_sum[c, k * half : (k + 1) * half] for c in range(2)], axis=0) for k in range(3)
        )
        output_parts = [unpack_pair(feed_sum[c, 3 * half :, :384], odd) for c in range(2)]
        output_out = jnp.concatenate([p for pair in output_parts for p in pair], axis=0)
        share = first_gain.shape[0]
        gain_one_out = feed_sum[0, 3 * half, 384 : 384 + share]
        gain_two_out = feed_sum[0, 3 * half + 1, 384 : 384 + share]
        pairs = [unpack_pair(heads_sum[c, :half], odd) for c in range(2)]
        query_out = jnp.concatenate([p[0] for p in pairs], axis=0)
        key_out = jnp.concatenate([p[1] for p in pairs], axis=0)
        values = [unpack_pair(heads_sum[c, half:], odd) for c in range(2)]
        value_out = jnp.concatenate([p for pair in values for p in pair], axis=0)
        down_out = down_out.T
    else:
        query_out, key_out, value_out = (scatter_plain(dot_nn(x_turned, g)) for g in (grad_query, grad_key, grad_value))
        output_out = scatter_plain(dot_nn(context_turned, branch_one))
        gate_out, up_out = (scatter_plain(dot_nn(hidden_in_turned, g)) for g in (grad_gate, grad_up))
        down_out = scatter_plain(dot_nn(branch_two_turned, hidden).T)
        gain_one_out, gain_two_out = scatter_gain(gain_grads[0]), scatter_gain(gain_grads[1])
    return (
        layer_out,
        input_grad,
        query_out,
        key_out,
        value_out,
        output_out,
        gate_out,
        up_out,
        down_out,
        gain_one_out,
        gain_two_out,
    )


def solution(mesh):
    tokens = P(("dp", "row", "col"), None)
    block = P("row", "col")
    gain = P(("row", "col"))
    return jax.shard_map(
        on_device,
        mesh=mesh,
        in_specs=(tokens, P(("dp", "row", "col"))) + (block,) * 7 + (gain, gain, tokens),
        out_specs=(tokens, tokens) + (block,) * 7 + (gain, gain),
        check_vma=False,
    )
```

```python
import jax
import jax.numpy as jnp
from jax import lax
from jax.experimental import pallas as pl
from jax.experimental.pallas import tpu as pltpu
from jax.sharding import PartitionSpec as P

HEAD_DIM = 64
EPSILON = 1e-06
ROPE_BASE = 10000.0
NEGATIVE = -1e30
LOG2E = 1.4426950408889634
QUERY_BLOCK = 256
LANES = 128
BF16 = jnp.bfloat16
F32 = jnp.float32
EVERYWHERE = ("dp", "row", "col")


def costs(microseconds):
    return pl.CostEstimate(flops=int(microseconds * 1e7), bytes_accessed=int(microseconds * 1e4), transcendentals=0)


def dot_nn(left, right):
    return lax.dot_general(left, right, (((1,), (0,)), ((), ())), preferred_element_type=F32)


def dot_nt(left, right):
    return lax.dot_general(left, right, (((1,), (1,)), ((), ())), preferred_element_type=F32)


def bit_count(size):
    return size.bit_length() - 1


def bit_order(grid_rows, grid_cols, core):
    col_bits = [("col", b) for b in range(bit_count(grid_cols))]
    row_bits = [("row", b) for b in range(bit_count(grid_rows))]
    return (col_bits[::-1] + row_bits[::-1]) if core else (col_bits + row_bits)


def step_pairs(grid_rows, grid_cols, step):
    pairs = []
    for core in range(2):
        axis, bit = bit_order(grid_rows, grid_cols, core)[step]
        for row in range(grid_rows):
            for col in range(grid_cols):
                to_row = row ^ (1 << bit) if axis == "row" else row
                to_col = col ^ (1 << bit) if axis == "col" else col
                source = (core * grid_rows + row) * grid_cols + col
                target = (core * grid_rows + to_row) * grid_cols + to_col
                pairs.append((source, target))
    return pairs


def other_core(value):
    return lax.ppermute(value, "dp", [(0, 1), (1, 0)])


def exchange(value, grid, step):
    return lax.ppermute(value, EVERYWHERE, step_pairs(*grid, step))


def tie(*values):
    return lax.optimization_barrier(values)


class Scatter:
    def __init__(self, own, other, grid):
        self.grid = grid
        self.terms = [own]
        self.other = other
        self.step = bit_count(grid[0]) + bit_count(grid[1])

    def swap(self):
        self.terms.append(other_core(self.other))
        return self.terms[-1]

    def go(self, *after):
        self.step -= 1
        half = self.terms[0].shape[0] // 2
        away = sum(term[half:].astype(F32) for term in self.terms).astype(BF16)
        if after:
            away = tie(away, *after)[0]
        came = exchange(away, self.grid, self.step)
        self.terms = [term[:half] for term in self.terms] + [came]
        return came

    def mine(self):
        return sum(term[0].astype(F32) for term in self.terms).astype(BF16)


def reversed_bits(value, bits):
    out = 0
    for b in range(bits):
        out = out | (((value >> b) & 1) << (bits - 1 - b))
    return out


def place_of(row, col, place, core, grid_rows, grid_cols):
    far_row = row ^ place[0]
    far_col = col ^ place[1]
    row_bits = bit_count(grid_rows)
    col_bits = bit_count(grid_cols)
    plain = far_col + far_row * grid_cols
    turned = reversed_bits(far_col, col_bits) + reversed_bits(far_row, row_bits) * grid_cols
    return jnp.where(core == 0, plain, turned)


def unpack_pair(packed, odd):
    firsts = []
    for k in range(2):
        body = packed[:, 128 * k : 128 * (k + 1)]
        rest_low, rest_high = packed[:, 256:320], packed[:, 320:384]
        in_order, turned = (rest_low, rest_high) if k == 0 else (rest_high, rest_low)
        plain = jnp.concatenate([body, in_order], axis=1)
        other = jnp.concatenate([turned, body], axis=1)
        firsts.append(jnp.where(odd, other, plain))
    return firsts


def by_core(place, mine, theirs):
    mine, theirs = mine.astype(F32), theirs.astype(F32)
    first = place[2] == 0
    return jnp.where(first, mine, theirs), jnp.where(first, theirs, mine)


def finish_one_body(place, mine, theirs, down):
    half = down.shape[0] // 2
    for core, part in enumerate(by_core(place, mine[...], theirs[...])):
        down[core * half : (core + 1) * half, :] = part


def finish_two_body(place, mine, theirs, gate, up, output, gains):
    half = gate.shape[0] // 2
    quarter = half // 2
    odd = (place[1] & 1) == 1
    halves = by_core(place, mine[...], theirs[...])
    for core, part in enumerate(halves):
        for k, out in enumerate((gate, up)):
            out[core * half : (core + 1) * half, :] = part[k * half : (k + 1) * half]
        for k, block in enumerate(unpack_pair(part[2 * half :], odd)):
            output[core * half + k * quarter : core * half + (k + 1) * quarter, :] = block
    gains[...] = halves[0][2 * half : 2 * half + 8, 384:512]


def finish_three_body(place, mine, theirs, query, key, value):
    half = query.shape[0] // 2
    quarter = half // 2
    odd = (place[1] & 1) == 1
    for core, part in enumerate(by_core(place, mine[...], theirs[...])):
        rows = slice(core * half, (core + 1) * half)
        query[rows, :], key[rows, :] = unpack_pair(part[:half], odd)
        for k, block in enumerate(unpack_pair(part[half:], odd)):
            value[core * half + k * quarter : core * half + (k + 1) * quarter, :] = block


def finish(body, name, place, mine, theirs, shapes):
    vmem = pl.BlockSpec(memory_space=pltpu.VMEM)
    return pl.pallas_call(
        body,
        in_specs=[pl.BlockSpec(memory_space=pltpu.SMEM)] + [vmem] * 2,
        out_specs=[vmem] * len(shapes),
        out_shape=[jax.ShapeDtypeStruct(shape, F32) for shape in shapes],
        cost_estimate=costs(1),
        name=name,
    )(place, mine, theirs)


def pack_pair(first, second, odd, out, rows):
    rolled = [jnp.concatenate([v[:, 64:], v[:, :64]], axis=1) for v in (first, second)]
    bodies = [jnp.where(odd, r[:, :128], v[:, :128]) for r, v in zip(rolled, (first, second))]
    rests = [jnp.where(odd, v[:, :64], v[:, 128:]) for v in (first, second)]
    low = jnp.where(odd, rests[1], rests[0])
    high = jnp.where(odd, rests[0], rests[1])
    out[rows, 0:128] = bodies[0].astype(BF16)
    out[rows, 128:256] = bodies[1].astype(BF16)
    out[rows, 256:384] = jnp.concatenate([low, high], axis=1).astype(BF16)


def pack_attention_body(place, query, key, value, out):
    half = query.shape[0] // 2
    quarter = half // 2
    odd = (place[1] & 1) == 1
    base = place[2] * half
    query, key = (w[pl.ds(pl.multiple_of(base, half), half), :].astype(F32) for w in (query, key))
    pack_pair(query, key, odd, out, slice(0, half))
    value = value[pl.ds(pl.multiple_of(base, half), half), :].astype(F32)
    pack_pair(value[:quarter], value[quarter:], odd, out, slice(half, half + quarter))


def pack_attention(place, query, key, value):
    half = query.shape[0] // 2
    vmem = pl.BlockSpec(memory_space=pltpu.VMEM)
    return pl.pallas_call(
        pack_attention_body,
        in_specs=[pl.BlockSpec(memory_space=pltpu.SMEM)] + [vmem] * 3,
        out_specs=vmem,
        out_shape=jax.ShapeDtypeStruct((half + half // 2, 384), BF16),
        cost_estimate=costs(2),
        name="pack_attention",
    )(place, query, key, value)


def pack_feed_body(place, gate, up, down, output, gain_one, gain_two, out):
    half = gate.shape[0] // 2
    quarter = half // 2
    odd = (place[1] & 1) == 1
    rows = pl.ds(pl.multiple_of(place[2] * half, half), half)
    out[0:half, :] = gate[rows, :]
    out[half : 2 * half, :] = up[rows, :]
    out[2 * half + quarter : 3 * half + quarter, :] = down[rows, :]
    output = output[rows, :].astype(F32)
    low = slice(2 * half, 2 * half + quarter)
    pack_pair(output[:quarter], output[quarter:], odd, out, low)
    share = gain_one.shape[1]
    gains = jnp.concatenate([gain_one[...].astype(F32), gain_two[...].astype(F32)], axis=0)
    gains = jnp.concatenate([gains, jnp.zeros((2, LANES - share), F32)], axis=1)
    gains = jnp.concatenate([gains, jnp.zeros((quarter - 2, LANES), F32)], axis=0)
    out[low, 384:512] = gains.astype(BF16)


def pack_feed(place, gate, up, down_turned, output, gain_one, gain_two):
    half = gate.shape[0] // 2
    vmem = pl.BlockSpec(memory_space=pltpu.VMEM)
    return pl.pallas_call(
        pack_feed_body,
        in_specs=[pl.BlockSpec(memory_space=pltpu.SMEM)] + [vmem] * 6,
        out_specs=vmem,
        out_shape=jax.ShapeDtypeStruct((3 * half + half // 2, gate.shape[1]), BF16),
        cost_estimate=costs(2),
        name="pack_feed",
    )(place, gate, up, down_turned, output, gain_one[None], gain_two[None])


def place_scalars():
    return jnp.stack([lax.axis_index("row"), lax.axis_index("col"), lax.axis_index("dp")]).astype(jnp.int32)


def split_rows(top):
    return lax.broadcasted_iota(jnp.int32, top, 1) < 64


def fill_columns(target, rows, low_even, body_even, low_odd, body_odd, pair, swapped):
    base = 384 * pair
    target[rows, base : base + 128] = body_even
    target[rows, base + 256 : base + 384] = body_odd
    first = split_rows(low_even.shape)
    if swapped:
        mixed = jnp.where(first, low_odd, low_even)
        target[rows, base + 128 : base + 256] = pltpu.roll(mixed.astype(F32), 64, 1).astype(BF16)
    else:
        target[rows, base + 128 : base + 256] = jnp.where(first, low_even, low_odd)


def piece_places(pieces):
    counts = [p.shape[0] for p in pieces]
    out = []
    for side in range(2):
        at = 0
        for count in counts[side * len(counts) // 2 : (side + 1) * len(counts) // 2]:
            out.append((side, at, count))
            at += count
    return out


def load_stacks(pieces, held, sems):
    copies = []
    for k, (piece, (side, at, count)) in enumerate(zip(pieces, piece_places(pieces))):
        copies.append(pltpu.make_async_copy(piece, held.at[side, pl.ds(at, count)], sems.at[k]))
    for copy in copies:
        copy.start()
    for copy in copies:
        copy.wait()


def assemble_attention(grid, place, held, w_query, w_key, w_value):
    grid_rows, grid_cols = grid
    where = (place[0], place[1])
    half = w_query.shape[0] // grid_rows // 2
    quarter = half // 2
    for core in range(2):
        side = core ^ place[2]
        for row in range(grid_rows):
            start = row * 2 * half + core * half
            for pair in range(grid_cols // 2):
                at = [place_of(row, 2 * pair + c, where, core, grid_rows, grid_cols) for c in range(2)]
                even, odd = (held.at[side, p] for p in at)
                top = slice(0, half)
                rows = slice(start, start + half)
                rest_even, rest_odd = even[top, 256:384], odd[top, 256:384]
                fill_columns(w_query, rows, rest_even, even[top, 0:128], rest_odd, odd[top, 0:128], pair, False)
                fill_columns(w_key, rows, rest_even, even[top, 128:256], rest_odd, odd[top, 128:256], pair, True)
                low = slice(half, half + quarter)
                rest_even, rest_odd = even[low, 256:384], odd[low, 256:384]
                rows = slice(start, start + quarter)
                fill_columns(w_value, rows, rest_even, even[low, 0:128], rest_odd, odd[low, 0:128], pair, False)
                rows = slice(start + quarter, start + half)
                fill_columns(w_value, rows, rest_even, even[low, 128:256], rest_odd, odd[low, 128:256], pair, True)


def assemble_output(grid, place, held, w_output, gains):
    grid_rows, grid_cols = grid
    where = (place[0], place[1])
    half = w_output.shape[0] // grid_rows // 2
    quarter = half // 2
    width = gains.shape[1]
    share = width // (grid_rows * grid_cols)
    lane = lax.broadcasted_iota(jnp.int32, (LANES, width), 1)
    spread = (lax.rem(lane, share) == lax.broadcasted_iota(jnp.int32, (LANES, width), 0)).astype(BF16)
    block_of = lax.div(lax.broadcasted_iota(jnp.int32, (16, width), 1), share)
    total = jnp.zeros((16, width), F32)
    every = slice(0, quarter)
    for core in range(2):
        side = core ^ place[2]
        for row in range(grid_rows):
            start = row * 2 * half + core * half
            for pair in range(grid_cols // 2):
                at = [place_of(row, 2 * pair + c, where, core, grid_rows, grid_cols) for c in range(2)]
                even, odd = (held.at[side, p] for p in at)
                rest_even, rest_odd = even[every, 256:384], odd[every, 256:384]
                rows = slice(start, start + quarter)
                fill_columns(w_output, rows, rest_even, even[every, 0:128], rest_odd, odd[every, 0:128], pair, False)
                rows = slice(start + quarter, start + half)
                fill_columns(w_output, rows, rest_even, even[every, 128:256], rest_odd, odd[every, 128:256], pair, True)
                if core == 0:
                    for c, block in enumerate((even, odd)):
                        spreaded = dot_nn(block[0:16, 384:512], spread)
                        total = total + jnp.where(block_of == row * grid_cols + 2 * pair + c, spreaded, 0.0)
    gains[...] = total[:8]


def block_at(position, place, core, grid):
    grid_rows, grid_cols = grid
    far_row, far_col = position // grid_cols, position % grid_cols
    turned_row, turned_col = reversed_bits(far_row, bit_count(grid_rows)), reversed_bits(far_col, bit_count(grid_cols))
    first = core == 0
    return jnp.where(first, far_row, turned_row) ^ place[0], jnp.where(first, far_col, turned_col) ^ place[1]


def feed_copies(grid, place, pieces, w_gate, w_up, w_down, held, sems):
    grid_rows, grid_cols = grid
    half = w_gate.shape[0] // grid_rows // 2
    quarter = half // 2
    span = w_gate.shape[1] // grid_cols
    groups = ([], [], [])
    for piece, (side, at, count) in zip(pieces, piece_places(pieces)):
        core = side ^ place[2]
        for n in range(count):
            row, col = block_at(at + n, place, core, grid)
            block = piece.at[n]
            rows = pl.ds(pl.multiple_of((2 * row + core) * half, half), half)
            lanes = pl.ds(pl.multiple_of(col * span, span), span)
            turned_rows = pl.ds(pl.multiple_of((2 * col + core) * half, half), half)
            turned_lanes = pl.ds(pl.multiple_of(row * span, span), span)
            parts = (
                (0, 2 * half, quarter, held.at[side, at + n]),
                (1, 0, half, w_gate.at[rows, lanes]),
                (1, half, half, w_up.at[rows, lanes]),
                (2, 2 * half + quarter, half, w_down.at[turned_rows, turned_lanes]),
            )
            for group, start, size, target in parts:
                groups[group].append((block.at[pl.ds(start, size)], target, sems.at[group]))
    return groups


def swap_halves(values):
    lane = lax.broadcasted_iota(jnp.int32, values.shape, 1)
    back = pltpu.roll(values, 32, 1)
    ahead = pltpu.roll(values, LANES - 32, 1)
    return jnp.where(lax.rem(lane, HEAD_DIM) < HEAD_DIM // 2, ahead, back)


def project_tile(x, w_query, w_key, w_value, cosine, sine, query, key, value):
    width = w_query.shape[1]
    step = 256
    for start in range(0, width, step):
        for weight, out in ((w_query, query), (w_key, key)):
            flat = dot_nn(x[...], weight[:, start : start + step])
            for k in range(step // LANES):
                part = flat[:, k * LANES : (k + 1) * LANES]
                turned = part * cosine[...] + swap_halves(part) * sine[...]
                out[:, start + k * LANES : start + (k + 1) * LANES] = turned.astype(BF16)
        value[:, start : start + step] = dot_nn(x[...], w_value[:, start : start + step]).astype(BF16)


def project_blocks_body(grid, count, place, *refs):
    pieces, refs = refs[:count], refs[count:]
    x, cosine, sine, query, key, value, w_query, w_key, w_value, held, sems = refs

    @pl.when(pl.program_id(0) == 0)
    def _():
        load_stacks(pieces, held, sems)
        assemble_attention(grid, place, held, w_query, w_key, w_value)

    project_tile(x, w_query, w_key, w_value, cosine, sine, query, key, value)


def project_blocks(pieces, place, grid, x, cosine, sine):
    tokens, width = x.shape
    _, height, lanes = pieces[0].shape
    rows = 256
    tile = pl.BlockSpec((rows, width), lambda i: (i, 0))
    table = pl.BlockSpec((rows, LANES), lambda i: (i, 0))
    whole = pl.BlockSpec((width, width), lambda i: (0, 0), pipeline_mode=pl.Buffered(1))
    anywhere = pl.BlockSpec(memory_space=pl.ANY)
    return pl.pallas_call(
        lambda *refs: project_blocks_body(grid, len(pieces), *refs),
        grid=(tokens // rows,),
        in_specs=[pl.BlockSpec(memory_space=pltpu.SMEM)] + [anywhere] * len(pieces) + [tile, table, table],
        out_specs=[tile] * 3 + [whole] * 3,
        out_shape=[jax.ShapeDtypeStruct((tokens, width), BF16)] * 3 + [jax.ShapeDtypeStruct((width, width), BF16)] * 3,
        scratch_shapes=[
            pltpu.VMEM((2, grid[0] * grid[1], height, lanes), BF16),
            pltpu.SemaphoreType.DMA((len(pieces),)),
        ],
        cost_estimate=costs(10),
        name="project_heads",
    )(place, *pieces, x, cosine, sine)


def project(x, w_query, w_key, w_value, cosine, sine):
    tokens, width = x.shape
    rows = 256
    tile = pl.BlockSpec((rows, width), lambda i: (i, 0))
    table = pl.BlockSpec((rows, LANES), lambda i: (i, 0))
    whole = pl.BlockSpec((width, width), lambda i: (0, 0))
    return pl.pallas_call(
        project_tile,
        grid=(tokens // rows,),
        in_specs=[tile, whole, whole, whole, table, table],
        out_specs=[tile] * 3,
        out_shape=[jax.ShapeDtypeStruct((tokens, width), BF16)] * 3,
        name="project_heads_plain",
    )(x, w_query, w_key, w_value, cosine, sine)


def attention_forward_body(first, q_ref, k_ref, v_ref, context_ref, lse_ref):
    blocks = q_ref.shape[0] // QUERY_BLOCK
    q_turned = (q_ref[...].astype(F32) * HEAD_DIM**-0.5).T.astype(BF16)
    v_turned = v_ref[...].T
    zero = jnp.zeros((HEAD_DIM, QUERY_BLOCK), BF16)
    square = (QUERY_BLOCK, QUERY_BLOCK)
    causal = lax.broadcasted_iota(jnp.int32, square, 0) <= lax.broadcasted_iota(jnp.int32, square, 1)
    lse_ref[...] = jnp.zeros_like(lse_ref)
    for i in range(blocks):
        now = slice(i * QUERY_BLOCK, (i + 1) * QUERY_BLOCK)
        outs = []
        for h in range(2):
            head = slice(h * HEAD_DIM, (h + 1) * HEAD_DIM)
            mine = q_turned[head, now]
            mine = jnp.concatenate([mine, zero] if h == 0 else [zero, mine], axis=0)
            scores = [dot_nn(k_ref[b * QUERY_BLOCK : (b + 1) * QUERY_BLOCK, :], mine) for b in range(i + 1)]
            scores[i] = jnp.where(causal, scores[i], NEGATIVE)
            top = jnp.max(scores[i], axis=0, keepdims=True)
            for b in range(i):
                block_top = jnp.max(scores[b], axis=0, keepdims=True)
                top = jnp.maximum(top, jnp.where(first[i] <= b, block_top, NEGATIVE))
            top = top * LOG2E
            mixed = None
            total = None
            for b in range(i + 1):
                base = top if b == i else top + jnp.where(first[i] <= b, 0.0, -NEGATIVE)
                weights = jnp.exp2(scores[b] * LOG2E - base)
                part_total = jnp.sum(weights, axis=0, keepdims=True)
                part = dot_nn(v_turned[head, b * QUERY_BLOCK : (b + 1) * QUERY_BLOCK], weights.astype(BF16))
                mixed = part if mixed is None else mixed + part
                total = part_total if total is None else total + part_total
            outs.append(mixed * (1.0 / total))
            lse_ref[0, h : h + 1, now] = top + jnp.log2(total)
        context_ref[now, :] = jnp.concatenate(outs, axis=0).T.astype(BF16)


def attention_forward(first, query, key, value, begin, pairs):
    tokens = query.shape[0]
    spec = pl.BlockSpec((tokens, LANES), lambda j, f: (0, j + begin))
    part = pl.BlockSpec((tokens, LANES), lambda j, f: (0, j))
    return pl.pallas_call(
        attention_forward_body,
        grid_spec=pltpu.PrefetchScalarGridSpec(
            num_scalar_prefetch=1,
            grid=(pairs,),
            in_specs=[spec] * 3,
            out_specs=[part, pl.BlockSpec((1, 8, tokens), lambda j, f: (j, 0, 0))],
        ),
        out_shape=[
            jax.ShapeDtypeStruct((tokens, pairs * LANES), BF16),
            jax.ShapeDtypeStruct((pairs, 8, tokens), F32),
        ],
        cost_estimate=costs(4 * pairs),
        name="attention_forward",
    )(first, query, key, value)


def attention_backward_body(first, q_ref, k_ref, v_ref, grad_ref, context_ref, lse_ref, cosine, sine, dq_ref, dk_ref, dv_ref, dk_sum, dv_sum):
    blocks = q_ref.shape[0] // QUERY_BLOCK
    scaled = q_ref[...].astype(F32) * HEAD_DIM**-0.5
    q_turned = scaled.T.astype(BF16)
    q_plain = scaled.astype(BF16)
    k_turned = k_ref[...].T
    grad = grad_ref[...]
    grad_turned = grad.T
    inner = (grad.astype(F32) * context_ref[...].astype(F32)).T
    zero = jnp.zeros((HEAD_DIM, QUERY_BLOCK), BF16)
    square = (QUERY_BLOCK, QUERY_BLOCK)
    causal = lax.broadcasted_iota(jnp.int32, square, 0) <= lax.broadcasted_iota(jnp.int32, square, 1)
    low_lanes = lax.broadcasted_iota(jnp.int32, (QUERY_BLOCK, LANES), 1) < HEAD_DIM
    for i in range(blocks):
        now = slice(i * QUERY_BLOCK, (i + 1) * QUERY_BLOCK)
        grads = []
        for h in range(2):
            head = slice(h * HEAD_DIM, (h + 1) * HEAD_DIM)
            own_lanes = low_lanes if h == 0 else jnp.logical_not(low_lanes)
            q_cols, g_cols = (
                jnp.concatenate([part[head, now], zero] if h == 0 else [zero, part[head, now]], axis=0)
                for part in (q_turned, grad_turned)
            )
            q_rows = jnp.where(own_lanes, q_plain[now, :], 0)
            g_rows = jnp.where(own_lanes, grad[now, :], 0)
            delta = jnp.sum(inner[head, now], axis=0, keepdims=True)
            lse = lse_ref[0, h : h + 1, now]
            dq = None
            for b in range(i + 1):
                there = slice(b * QUERY_BLOCK, (b + 1) * QUERY_BLOCK)
                scores = dot_nn(k_ref[there, :], q_cols)
                base = lse if b == i else lse + jnp.where(first[i] <= b, 0.0, -NEGATIVE)
                if b == i:
                    scores = jnp.where(causal, scores, NEGATIVE)
                probs = jnp.exp2(scores * LOG2E - base)
                grad_probs = dot_nn(v_ref[there, :], g_cols)
                grad_scores = (probs * (grad_probs - delta)).astype(BF16)
                dv = dot_nn(probs.astype(BF16), g_rows)
                dk = dot_nn(grad_scores, q_rows)
                if b == i and h == 0:
                    dv_sum[there, :] = dv
                    dk_sum[there, :] = dk
                else:
                    dv_sum[there, :] += dv
                    dk_sum[there, :] += dk
                part = dot_nn(k_turned[head, there], grad_scores)
                dq = part if dq is None else dq + part
            grads.append(dq * HEAD_DIM**-0.5)
        dq = jnp.concatenate(grads, axis=0).T
        dq_ref[now, :] = (dq * cosine[now, :] - swap_halves(dq) * sine[now, :]).astype(BF16)
    dk = dk_sum[...]
    dk_ref[...] = (dk * cosine[...] - swap_halves(dk) * sine[...]).astype(BF16)
    dv_ref[...] = dv_sum[...].astype(BF16)


def attention_backward(first, query, key, value, grad, context, lse, cosine, sine, begin, pairs, shift):
    tokens = query.shape[0]
    width = pairs * LANES
    spec = pl.BlockSpec((tokens, LANES), lambda j, f: (0, j + begin))
    part = pl.BlockSpec((tokens, LANES), lambda j, f: (0, j))
    inner = pl.BlockSpec((tokens, LANES), lambda j, f: (0, j + shift))
    table = pl.BlockSpec((tokens, LANES), lambda j, f: (0, 0))
    return pl.pallas_call(
        attention_backward_body,
        grid_spec=pltpu.PrefetchScalarGridSpec(
            num_scalar_prefetch=1,
            grid=(pairs,),
            in_specs=[spec] * 4 + [inner, pl.BlockSpec((1, 8, tokens), lambda j, f: (j + shift, 0, 0)), table, table],
            out_specs=[part] * 3,
            scratch_shapes=[pltpu.VMEM((tokens, LANES), F32)] * 2,
        ),
        out_shape=[jax.ShapeDtypeStruct((tokens, width), BF16)] * 3,
        cost_estimate=costs(6 * pairs),
        name="attention_backward",
    )(first, query, key, value, grad, context, lse, cosine, sine)


def middle_tile(
    contexts, x, cotangent, w_output, w_gate, w_up, w_down, gains, ready,
    layer_out, hidden_in_turned, branch_two_turned, context_turned, hidden, grad_gate, grad_up, grad_first, branch_one, grad_context, gain_grads,
    slope, act,
):
    width = x.shape[1]
    span = w_gate.shape[1]
    chunk = 512
    ready(0)
    gain_one = gains[0:1, :]
    gain_two = gains[1:2, :]
    context_now = jnp.concatenate([part[...] for part in contexts], axis=1)
    first_sum = x[...].astype(F32) + dot_nn(context_now, w_output[...])
    scale_one = lax.rsqrt(jnp.mean(first_sum * first_sum, axis=1, keepdims=True) + EPSILON)
    normed_one = first_sum * scale_one
    normed = normed_one * gain_one
    hidden_in = normed.astype(BF16)
    second_sum = normed
    ready(1)
    for start in range(0, span, chunk):
        cols = slice(start, start + chunk)
        gate_act = dot_nn(hidden_in, w_gate[:, cols])
        up_act = dot_nn(hidden_in, w_up[:, cols])
        sigmoid = jax.nn.sigmoid(gate_act)
        silu = gate_act * sigmoid
        act[:, cols] = silu
        slope[:, cols] = up_act * (sigmoid + silu * (1.0 - sigmoid))
        hidden_now = (silu * up_act).astype(BF16)
        hidden[:, cols] = hidden_now
        if start == 0:
            ready(2)
        second_sum = second_sum + dot_nt(hidden_now, w_down[:, cols])
    scale_two = lax.rsqrt(jnp.mean(second_sum * second_sum, axis=1, keepdims=True) + EPSILON)
    normed_two = second_sum * scale_two
    layer_out[...] = (normed_two * gain_two).astype(BF16)
    grad_out = cotangent[...].astype(F32)
    two_term = jnp.sum(grad_out * normed_two, axis=0, keepdims=True)
    scaled = grad_out * gain_two
    grad_second = scale_two * (scaled - normed_two * jnp.mean(scaled * normed_two, axis=1, keepdims=True))
    branch_two = grad_second.astype(BF16)
    grad_normed = grad_second
    for start in range(0, span, chunk):
        cols = slice(start, start + chunk)
        grad_hidden = dot_nn(branch_two, w_down[:, cols])
        gate_now = (grad_hidden * slope[:, cols]).astype(BF16)
        up_now = (grad_hidden * act[:, cols]).astype(BF16)
        grad_gate[:, cols] = gate_now
        grad_up[:, cols] = up_now
        grad_normed = grad_normed + dot_nt(gate_now, w_gate[:, cols]) + dot_nt(up_now, w_up[:, cols])
    one_term = jnp.sum(grad_normed * normed_one, axis=0, keepdims=True)
    scaled = grad_normed * gain_one
    first_grad = scale_one * (scaled - normed_one * jnp.mean(scaled * normed_one, axis=1, keepdims=True))
    grad_first[...] = first_grad
    one_now = first_grad.astype(BF16)
    branch_one[...] = one_now
    grad_context[...] = dot_nt(one_now, w_output[...]).astype(BF16)
    hidden_in_turned[...] = hidden_in.T
    branch_two_turned[...] = branch_two.T
    context_turned[...] = context_now.T
    terms = jnp.concatenate([one_term, two_term, jnp.zeros((6, width), F32)], axis=0)

    @pl.when(pl.program_id(0) == 0)
    def _():
        gain_grads[...] = terms

    @pl.when(pl.program_id(0) > 0)
    def _():
        gain_grads[...] += terms


def middle_specs(tokens, width, span, rows):
    tile = pl.BlockSpec((rows, width), lambda i: (i, 0))
    wide = pl.BlockSpec((rows, span), lambda i: (i, 0))
    turned = pl.BlockSpec((width, rows), lambda i: (0, i))
    eight = pl.BlockSpec((8, width), lambda i: (0, 0))
    flat = jax.ShapeDtypeStruct((tokens, width), BF16)
    flat_turned = jax.ShapeDtypeStruct((width, tokens), BF16)
    broad = jax.ShapeDtypeStruct((tokens, span), BF16)
    return (
        [tile, turned, turned, turned, wide, wide, wide, tile, tile, tile, eight],
        [
            flat, flat_turned, flat_turned, flat_turned, broad, broad, broad,
            jax.ShapeDtypeStruct((tokens, width), F32), flat, flat, jax.ShapeDtypeStruct((8, width), F32),
        ],
    )


def middle_plain_body(context, x, cotangent, w_output, w_gate, w_up, w_down, gains, *rest):
    middle_tile((context,), x, cotangent, w_output, w_gate, w_up, w_down, gains, lambda k: None, *rest)


def middle_plain(context, x, cotangent, w_output, w_gate, w_up, w_down, gains):
    tokens, width = x.shape
    span = w_gate.shape[1]
    rows = 256
    tile = pl.BlockSpec((rows, width), lambda i: (i, 0))
    square = pl.BlockSpec((width, width), lambda i: (0, 0), pipeline_mode=pl.Buffered(1))
    whole = pl.BlockSpec((width, span), lambda i: (0, 0), pipeline_mode=pl.Buffered(1))
    eight = pl.BlockSpec((8, width), lambda i: (0, 0))
    out_specs, out_shape = middle_specs(tokens, width, span, rows)
    return pl.pallas_call(
        middle_plain_body,
        grid=(tokens // rows,),
        in_specs=[tile, tile, tile, square, whole, whole, whole, eight],
        out_specs=out_specs,
        out_shape=out_shape,
        scratch_shapes=[pltpu.VMEM((rows, span), F32)] * 2,
        name="feed_forward_and_back_plain",
    )(context, x, cotangent, w_output, w_gate, w_up, w_down, gains)


def middle_body(grid, count, place, *refs):
    pieces, refs = refs[:count], refs[count:]
    context, x, cotangent = refs[:3]
    outs = refs[3:14]
    slope, act, w_output, w_gate, w_up, w_down, gains, held, sems = refs[14:]
    here = pl.program_id(0) == 0

    @pl.when(here)
    def _():
        for group in feed_copies(grid, place, pieces, w_gate, w_up, w_down, held, sems):
            for source, target, sem in group:
                pltpu.make_async_copy(source, target, sem).start()

    def ready(k):
        @pl.when(here)
        def _():
            for source, target, sem in feed_copies(grid, place, pieces, w_gate, w_up, w_down, held, sems)[k]:
                pltpu.make_async_copy(source, target, sem).wait()
            if k == 0:
                assemble_output(grid, place, held, w_output, gains)

    middle_tile((context,), x, cotangent, w_output, w_gate, w_up, w_down, gains, ready, *outs, slope, act)


def middle(pieces, place, grid, context, x, cotangent):
    tokens, width = x.shape
    _, height, lanes = pieces[0].shape
    span = lanes * grid[1]
    rows = 256
    tile = pl.BlockSpec((rows, width), lambda i: (i, 0))
    anywhere = pl.BlockSpec(memory_space=pl.ANY)
    out_specs, out_shape = middle_specs(tokens, width, span, rows)
    return pl.pallas_call(
        lambda *refs: middle_body(grid, len(pieces), *refs),
        grid=(tokens // rows,),
        in_specs=[pl.BlockSpec(memory_space=pltpu.SMEM)] + [anywhere] * len(pieces) + [tile] * 3,
        out_specs=out_specs,
        out_shape=out_shape,
        scratch_shapes=[pltpu.VMEM((rows, span), F32)] * 2
        + [pltpu.VMEM((width, width), BF16)]
        + [pltpu.VMEM((width, span), BF16)] * 3
        + [
            pltpu.VMEM((8, width), F32),
            pltpu.VMEM((2, grid[0] * grid[1], height // 7, lanes), BF16),
            pltpu.SemaphoreType.DMA((3,)),
        ],
        cost_estimate=costs(40),
        name="feed_forward_and_back",
    )(place, *pieces, context, x, cotangent)


def store_halves(own, other, where, grid, core_here, row, col, rows, lanes, halves):
    grid_rows, grid_cols = grid
    here = core_here == 0
    at_own = place_of(row, col, where, core_here, grid_rows, grid_cols)
    at_other = place_of(row, col, where, 1 - core_here, grid_rows, grid_cols)
    own[at_own, rows, lanes] = jnp.where(here, halves[0], halves[1])
    other[at_other, rows, lanes] = jnp.where(here, halves[1], halves[0])


def rest_tile(first, second, odd):
    low = split_rows(first.shape)
    rolled = pltpu.roll(second, 64, 1)
    return jnp.where(low, rolled, first) if odd else jnp.where(low, first, rolled)


def part_of(index, place_index, core, count):
    far = index ^ place_index
    return jnp.where(core == 0, far, reversed_bits(far, bit_count(count)))


def feed_grads_body(grid, turned, count, place, left, *refs):
    rights, (own, other) = refs[:count], refs[-2:]
    grid_rows, grid_cols = grid
    half = left.shape[0] // (grid_cols if turned else grid_rows) // 2
    step = pl.program_id(0)
    here = place[2] == 0
    inner = grid_cols if turned else grid_rows
    outer = grid_rows if turned else grid_cols
    for k, right in enumerate(rights):

        @pl.when(step // outer == k)
        def _():
            product = dot_nn(left[...], right[...]).astype(BF16)
            for i in range(inner):
                first, second = (product[(2 * i + c) * half : (2 * i + c + 1) * half] for c in range(2))
                at = place[1] if turned else place[0]
                mine, theirs = part_of(i, at, place[2], inner), part_of(i, at, 1 - place[2], inner)
                first, second = jnp.where(here, first, second), jnp.where(here, second, first)
                if turned:
                    own[0, mine] = first
                    other[0, theirs] = second
                else:
                    own[mine, 0] = first
                    other[theirs, 0] = second


def feed_grads(place, grid, left, rights, turned, height, into):
    width, tokens = left.shape
    grid_rows, grid_cols = grid
    outer = grid_rows if turned else grid_cols
    span = rights[0].shape[1] // outer
    half = width // (grid_cols if turned else grid_rows) // 2
    count = len(rights)

    def out_index(flip):
        def index(i, s):
            core = s[2] ^ flip
            at = part_of(lax.rem(i, outer), s[0] if turned else s[1], core, outer)
            return (at, 0, i // outer, 0) if turned else (0, at, i // outer, 0)

        return index

    block = (1, grid_cols, half, span) if turned else (grid_rows, 1, half, span)
    shape = (grid_rows, grid_cols, height, span)
    anywhere = pl.BlockSpec(memory_space=pl.ANY)
    own, other = pl.pallas_call(
        lambda *refs: feed_grads_body(grid, turned, count, *refs),
        grid_spec=pltpu.PrefetchScalarGridSpec(
            num_scalar_prefetch=1,
            grid=(outer * count,),
            in_specs=[pl.BlockSpec((width, tokens), lambda i, s: (0, 0), pipeline_mode=pl.Buffered(1))]
            + [
                pl.BlockSpec((tokens, span), lambda i, s, k=k: (0, jnp.clip(i - k * outer, 0, outer - 1)))
                for k in range(count)
            ]
            + [anywhere] * len(into),
            out_specs=[pl.BlockSpec(block, out_index(0)), pl.BlockSpec(block, out_index(1))],
        ),
        out_shape=[jax.ShapeDtypeStruct(shape, BF16)] * 2,
        input_output_aliases={2 + count + k: k for k in range(len(into))},
        cost_estimate=costs(7 * count),
        name="feed_forward_weight_grad",
    )(place, left, *rights, *(v.reshape(shape) for v in into))
    flat = (grid_rows * grid_cols, height, span)
    return own.reshape(flat), other.reshape(flat)


def output_grads_body(grid, place, context_turned, branch_one, gain_grads, own, other):
    grid_rows, grid_cols = grid
    where = (place[0], place[1])
    width = context_turned.shape[0]
    half = width // grid_rows // 2
    quarter = half // 2
    product = dot_nn(context_turned[...], branch_one[...])
    share = width // (grid_rows * grid_cols)
    lane = lax.broadcasted_iota(jnp.int32, (width, LANES), 0)
    gather = (lax.rem(lane, share) == lax.broadcasted_iota(jnp.int32, (width, LANES), 1)).astype(BF16)
    block_of = lax.div(lax.broadcasted_iota(jnp.int32, (8, width), 1), share)
    sums = gain_grads[...]
    every = slice(0, quarter)
    for row in range(grid_rows):
        for c in range(grid_cols):
            tile = 384 * (c // 2)
            odd = c % 2
            body = slice(tile + 256 * odd, tile + 256 * odd + 128)
            mid = slice(tile + 128, tile + 256)
            bodies, rests = [], []
            for core in range(2):
                start = row * 2 * half + core * half
                top, low = slice(start, start + quarter), slice(start + quarter, start + half)
                bodies.append((product[top, body], product[low, body]))
                rests.append(rest_tile(product[top, mid], product[low, mid], odd))
            for k in range(2):
                lanes = slice(128 * k, 128 * (k + 1))
                store_halves(own, other, where, grid, place[2], row, c, every, lanes, [b[k].astype(BF16) for b in bodies])
            store_halves(own, other, where, grid, place[2], row, c, every, slice(256, 384), [r.astype(BF16) for r in rests])
            picked = jnp.where(block_of == row * grid_cols + c, sums, 0.0).astype(BF16)
            gain = dot_nn(picked, gather)
            gain = jnp.concatenate([gain, jnp.zeros((quarter - 8, LANES), F32)], axis=0).astype(BF16)
            store_halves(own, other, where, grid, place[2], row, c, every, slice(384, 512), [gain, gain])


def output_grads(place, grid, context_turned, branch_one, gain_grads, height):
    width = context_turned.shape[0]
    grid_rows, grid_cols = grid
    quarter = width // grid_rows // 4
    whole = lambda value: pl.BlockSpec(value.shape, lambda i: (0, 0))
    count, span = grid_rows * grid_cols, 512
    out = pl.BlockSpec((count, quarter, span), lambda i: (0, height // quarter - 1, 0))
    return pl.pallas_call(
        lambda *refs: output_grads_body(grid, *refs),
        grid=(1,),
        in_specs=[pl.BlockSpec(memory_space=pltpu.SMEM)]
        + [whole(v) for v in (context_turned, branch_one, gain_grads)],
        out_specs=[out] * 2,
        out_shape=[jax.ShapeDtypeStruct((count, height, span), BF16)] * 2,
        cost_estimate=costs(4),
        name="output_weight_grad",
    )(place, context_turned, branch_one, gain_grads)


def attention_grads_body(grid, parts, place, x_turned, *refs):
    grads, (own, other) = refs[:-2], refs[-2:]
    grid_rows, grid_cols = grid
    where = (place[0], place[1])
    width = x_turned.shape[0]
    half = width // grid_rows // 2
    quarter = half // 2
    x_turned = x_turned[...]
    query, key, value = (
        jnp.concatenate([dot_nn(x_turned, g[...]) for g in grads[parts * k : parts * (k + 1)]], axis=1) for k in range(3)
    )
    for row in range(grid_rows):
        for c in range(grid_cols):
            odd = c % 2
            tile = 384 * (c // 2)
            body = slice(tile + 256 * odd, tile + 256 * odd + 128)
            mid = slice(tile + 128, tile + 256)
            pieces = []
            for core in range(2):
                start = row * 2 * half + core * half
                rows = slice(start, start + half)
                top, low = slice(start, start + quarter), slice(start + quarter, start + half)
                pair = (query[rows, body], key[rows, body], rest_tile(query[rows, mid], key[rows, mid], odd))
                last = (value[top, body], value[low, body], rest_tile(value[top, mid], value[low, mid], odd))
                pieces.append([p.astype(BF16) for p in pair + last])
            for k in range(3):
                lanes = slice(128 * k, 128 * (k + 1))
                store_halves(own, other, where, grid, place[2], row, c, slice(0, half), lanes, [p[k] for p in pieces])
                store_halves(own, other, where, grid, place[2], row, c, slice(half, half + quarter), lanes, [p[3 + k] for p in pieces])


def attention_grads(place, grid, x_turned, grads):
    width, tokens = x_turned.shape
    grid_rows, grid_cols = grid
    half = width // grid_rows // 2
    vmem = pl.BlockSpec(memory_space=pltpu.VMEM)
    shape = (grid_rows * grid_cols, half + half // 2, 384)
    flat = [g for k in range(3) for g in (part[k] for part in grads)]
    return pl.pallas_call(
        lambda *refs: attention_grads_body(grid, len(grads), *refs),
        in_specs=[pl.BlockSpec(memory_space=pltpu.SMEM)] + [vmem] * (1 + len(flat)),
        out_specs=[vmem] * 2,
        out_shape=[jax.ShapeDtypeStruct(shape, BF16)] * 2,
        cost_estimate=costs(8),
        name="attention_weight_grads",
    )(place, x_turned, *flat)


def input_grad_body(parts, grad_first, *refs):
    grads, weights, out = refs[: 3 * parts], refs[3 * parts : -1], refs[-1]
    total = grad_first[...]
    for k, weight in enumerate(weights):
        grad = jnp.concatenate([g[...] for g in grads[parts * k : parts * (k + 1)]], axis=1)
        total = total + dot_nt(grad, weight[...])
    out[...] = total.astype(BF16)


def input_gradient(grad_first, grads, w_query, w_key, w_value):
    tokens, width = grad_first.shape
    rows = 256
    tile = pl.BlockSpec((rows, width), lambda i: (i, 0))
    whole = pl.BlockSpec((width, width), lambda i: (0, 0), pipeline_mode=pl.Buffered(1))
    flat = [g for k in range(3) for g in (part[k] for part in grads)]
    return pl.pallas_call(
        lambda *refs: input_grad_body(len(grads), *refs),
        grid=(tokens // rows,),
        in_specs=[tile] + [pl.BlockSpec((rows, g.shape[1]), lambda i: (i, 0)) for g in flat] + [whole] * 3,
        out_specs=tile,
        out_shape=jax.ShapeDtypeStruct((tokens, width), BF16),
        cost_estimate=costs(8),
        name="input_gradient",
    )(grad_first, *flat, w_query, w_key, w_value)


def gather_plain(block):
    whole = lax.all_gather(block, "col", axis=1, tiled=True)
    return lax.all_gather(whole, "row", axis=0, tiled=True)


def scatter_plain(whole):
    part = lax.psum_scatter(whole.astype(BF16), "row", scatter_dimension=0, tiled=True)
    part = lax.psum_scatter(part, "col", scatter_dimension=1, tiled=True)
    return lax.psum(part, "dp").astype(F32)


def scatter_gain(whole):
    part = lax.psum_scatter(whole.astype(BF16), ("row", "col"), scatter_dimension=0, tiled=True)
    return lax.psum(part, "dp").astype(F32)


def on_device(
    inputs,
    segment_ids,
    query_weight,
    key_weight,
    value_weight,
    output_weight,
    gate_weight,
    up_weight,
    down_weight,
    first_gain,
    second_gain,
    cotangent,
):
    grid = (lax.axis_size("row"), lax.axis_size("col"))
    tokens, width = inputs.shape
    hidden_width = gate_weight.shape[1] * grid[1]
    core = lax.axis_index("dp")
    odd = (lax.axis_index("col") & 1) == 1
    place = place_scalars()
    packs = grid == (4, 4) and query_weight.shape[1] == 192 and gate_weight.shape[1] == 512

    def tables(segments):
        token_index = jnp.arange(tokens, dtype=jnp.int32)
        same = segments[:, None] == segments[None, :]
        starts = jnp.min(jnp.where(same, token_index[None, :], tokens), axis=1)
        positions = (token_index - starts).astype(F32)
        frequencies = ROPE_BASE ** (-2.0 * jnp.arange(HEAD_DIM // 2, dtype=F32) / HEAD_DIM)
        phases = positions[:, None] * frequencies[None, :]
        cosine, sine = jnp.cos(phases), jnp.sin(phases)
        cosine = jnp.concatenate([cosine] * 4, axis=1)
        sine = jnp.concatenate([-sine, sine] * 2, axis=1)
        return cosine, sine, starts[::QUERY_BLOCK] // QUERY_BLOCK

    def backward(grad_context, context, lse, begin, pairs, shift):
        return attention_backward(first, query, key, value, grad_context, context, lse, cosine, sine, begin, pairs, shift)

    if not packs:
        cosine, sine, first = tables(segment_ids)
        x_turned = inputs.T
        w_query, w_key, w_value, w_output = (
            gather_plain(w) for w in (query_weight, key_weight, value_weight, output_weight)
        )
        w_gate, w_up, w_down = gather_plain(gate_weight), gather_plain(up_weight), gather_plain(down_weight).T
        gains = jnp.stack(
            [lax.all_gather(g, ("row", "col"), axis=0, tiled=True).astype(F32) for g in (first_gain, second_gain)]
        )
        gains = jnp.pad(gains, ((0, 6), (0, 0)))
        query, key, value = project(inputs, w_query, w_key, w_value, cosine, sine)
        context, lse = attention_forward(first, query, key, value, 0, width // LANES)
        (
            layer_out, hidden_in_turned, branch_two_turned, context_turned, hidden, grad_gate, grad_up, grad_first, branch_one, grad_context, gain_grads,
        ) = middle_plain(context, inputs, cotangent, w_output, w_gate, w_up, w_down, gains)
        grads = [backward(grad_context, context, lse, 0, width // LANES, 0)]
        input_grad = input_gradient(grad_first, grads, w_query, w_key, w_value)
        query_out, key_out, value_out = (scatter_plain(dot_nn(x_turned, g)) for g in grads[0])
        output_out = scatter_plain(dot_nn(context_turned, branch_one))
        gate_out, up_out = (scatter_plain(dot_nn(hidden_in_turned, g)) for g in (grad_gate, grad_up))
        down_out = scatter_plain(dot_nn(branch_two_turned, hidden).T)
        gain_one_out, gain_two_out = scatter_gain(gain_grads[0]), scatter_gain(gain_grads[1])
        return (
            layer_out, input_grad, query_out, key_out, value_out, output_out, gate_out, up_out, down_out, gain_one_out, gain_two_out,
        )

    join = lambda *stacks: jnp.concatenate(stacks, axis=0)
    q0 = pack_attention(place, query_weight, key_weight, value_weight)[None]
    gate_in, q0 = tie(gate_weight, q0)
    q1 = exchange(q0, grid, 0)
    f0 = pack_feed(place, gate_in, up_weight, down_weight.T, output_weight, first_gain, second_gain)[None]
    q1, f0, segments, x_in = tie(q1, f0, segment_ids, inputs)
    q01 = join(q0, q1)
    q2 = exchange(q01, grid, 1)
    cosine, sine, first = tables(segments)
    x_turned = x_in.T
    q2, cosine, sine, x_turned, first = tie(q2, cosine, sine, x_turned, first)
    q03 = join(q01, q2)
    q3 = exchange(q03, grid, 2)
    f1 = exchange(f0, grid, 0)
    q3, f1 = tie(q3, f1)
    q4, q5 = exchange(q03, grid, 3), exchange(q3, grid, 3)
    q03_other, q3_other = other_core(q03), other_core(q3)
    f01 = join(f0, f1)
    f2 = exchange(f01, grid, 1)
    q4, q5, q03_other, q3_other = tie(q4, q5, q03_other, q3_other)
    q4_other, q5_other = other_core(q4), other_core(q5)
    q4_other, q5_other, f2 = tie(q4_other, q5_other, f2)
    f03 = join(f01, f2)
    f3 = exchange(f03, grid, 2)
    f03_other = other_core(f03)
    query, key, value, w_query, w_key, w_value = project_blocks(
        (q03, q3, q4, q5, q03_other, q3_other, q4_other, q5_other), place, grid, inputs, cosine, sine
    )
    f3, f03_other, f03, query = tie(f3, f03_other, f03, query)
    f4, f5 = exchange(f03, grid, 3), exchange(f3, grid, 3)
    f3_other = other_core(f3)
    context, lse = attention_forward(first, query, key, value, 0, width // LANES)
    f4, f5, f3_other, context = tie(f4, f5, f3_other, context)
    (
        layer_out, hidden_in_turned, branch_two_turned, context_turned, hidden, grad_gate, grad_up, grad_first, branch_one, grad_context, gain_grads,
    ) = middle(
        (f03, f3, f4, f5, f03_other, f3_other, other_core(f4), other_core(f5)), place, grid, context, inputs, cotangent
    )

    half = query_weight.shape[0] // 2
    quarter = half // 2
    pairs = width // LANES
    own, other = feed_grads(place, grid, branch_two_turned, (hidden,), True, half, ())
    one = Scatter(own, other, grid)
    one.other, context_turned = tie(one.other, context_turned)
    came = one.swap()
    into = output_grads(place, grid, context_turned, branch_one, gain_grads, 2 * half + quarter)
    came, into, hidden_in_turned = tie(came, into, hidden_in_turned)
    one.terms[-1] = came
    came = one.go()
    own, other = feed_grads(place, grid, hidden_in_turned, (grad_gate, grad_up), False, 2 * half + quarter, into)
    came, own, other, grad_context = tie(came, own, other, grad_context)
    one.terms[-1] = came
    two = Scatter(own, other, grid)
    came_two = two.swap()
    came = one.go()
    grads = [backward(grad_context, context, lse, 0, pairs // 2, 0)]
    came, came_two, grad_context, _ = tie(came, came_two, grad_context, grads[0][0])
    one.terms[-1] = came
    two.terms[-1] = came_two
    came_two = two.go()
    came = one.go()
    grads.append(backward(grad_context, context, lse, pairs // 2, pairs // 2, pairs // 2))
    came, came_two, x_turned, _ = tie(came, came_two, x_turned, grads[1][0])
    one.terms[-1] = came
    two.terms[-1] = came_two
    came_two = two.go()
    came = one.go()
    own, other = attention_grads(place, grid, x_turned, grads)
    three = Scatter(own, other, grid)
    three.other, came, came_two, grad_first = tie(three.other, came, came_two, grad_first)
    one.terms[-1] = came
    two.terms[-1] = came_two
    came_three = three.swap()
    came_two = two.go()
    one_mine = one.mine()
    one_theirs = other_core(one_mine)
    came_three, one_theirs = tie(came_three, one_theirs)
    three.terms[-1] = came_three
    came_three = three.go()
    input_grad = input_gradient(grad_first, grads, w_query, w_key, w_value)
    came_three, came_two, input_grad, one_mine = tie(came_three, came_two, input_grad, one_mine)
    two.terms[-1] = came_two
    three.terms[-1] = came_three
    came_three = three.go()
    came_two = two.go()
    down_out, = finish(finish_one_body, "finish_one", place, one_mine, one_theirs, [gate_weight.shape])
    came_three, came_two, down_out = tie(came_three, came_two, down_out)
    two.terms[-1] = came_two
    three.terms[-1] = came_three
    came_three = three.go()
    two_mine = two.mine()
    two_theirs = other_core(two_mine)
    came_three, two_mine, two_theirs = tie(came_three, two_mine, two_theirs)
    three.terms[-1] = came_three
    came_three = three.go()
    gate_out, up_out, output_out, gain_out = finish(
        finish_two_body, "finish_two", place, two_mine, two_theirs,
        [gate_weight.shape, up_weight.shape, output_weight.shape, (8, LANES)],
    )
    share = first_gain.shape[0]
    gain_one_out, gain_two_out = gain_out[0, :share], gain_out[1, :share]
    came_three, gate_out, gain_one_out, gain_two_out = tie(came_three, gate_out, gain_one_out, gain_two_out)
    three.terms[-1] = came_three
    three_mine = three.mine()
    query_out, key_out, value_out = finish(
        finish_three_body, "finish_three", place, three_mine, other_core(three_mine), [query_weight.shape] * 3
    )
    return (
        layer_out, input_grad, query_out, key_out, value_out, output_out, gate_out, up_out, down_out.T, gain_one_out, gain_two_out,
    )


def solution(mesh):
    tokens = P(("dp", "row", "col"), None)
    block = P("row", "col")
    gain = P(("row", "col"))
    return jax.shard_map(
        on_device,
        mesh=mesh,
        in_specs=(tokens, P(("dp", "row", "col"))) + (block,) * 7 + (gain, gain, tokens),
        out_specs=(tokens, tokens) + (block,) * 7 + (gain, gain),
        check_vma=False,
    )
```

```python
import jax
import jax.numpy as jnp
from jax import lax
from jax.experimental import pallas as pl
from jax.experimental.pallas import tpu as pltpu
from jax.sharding import PartitionSpec as P

HEAD_DIM = 64
EPSILON = 1e-06
ROPE_BASE = 10000.0
NEGATIVE = -1e30
LOG2E = 1.4426950408889634
QUERY_BLOCK = 256
GAIN_ROWS = 16
LANES = 128
BF16 = jnp.bfloat16
F32 = jnp.float32
EVERYWHERE = ("dp", "row", "col")


def costs(microseconds):
    return pl.CostEstimate(flops=int(microseconds * 1e7), bytes_accessed=int(microseconds * 1e4), transcendentals=0)


def dot_nn(left, right):
    return lax.dot_general(left, right, (((1,), (0,)), ((), ())), preferred_element_type=F32)


def dot_nt(left, right):
    return lax.dot_general(left, right, (((1,), (1,)), ((), ())), preferred_element_type=F32)


def bit_count(size):
    return size.bit_length() - 1


def bit_order(grid_rows, grid_cols, core):
    col_bits = [("col", b) for b in range(bit_count(grid_cols))]
    row_bits = [("row", b) for b in range(bit_count(grid_rows))]
    return (col_bits[::-1] + row_bits[::-1]) if core else (col_bits + row_bits)


def step_pairs(grid_rows, grid_cols, step):
    pairs = []
    for core in range(2):
        axis, bit = bit_order(grid_rows, grid_cols, core)[step]
        for row in range(grid_rows):
            for col in range(grid_cols):
                to_row = row ^ (1 << bit) if axis == "row" else row
                to_col = col ^ (1 << bit) if axis == "col" else col
                source = (core * grid_rows + row) * grid_cols + col
                target = (core * grid_rows + to_row) * grid_cols + to_col
                pairs.append((source, target))
    return pairs


def other_core(value):
    return lax.ppermute(value, "dp", [(0, 1), (1, 0)])


def exchange(value, grid, step):
    return lax.ppermute(value, EVERYWHERE, step_pairs(*grid, step))


def tie(*values):
    return lax.optimization_barrier(values)


class Scatter:
    def __init__(self, own, other, grid):
        self.grid = grid
        self.terms = [own]
        self.other = other
        self.step = bit_count(grid[0]) + bit_count(grid[1])

    def swap(self):
        self.terms.append(other_core(self.other))
        return self.terms[-1]

    def sums(self, part):
        parts = [part(term) for term in self.terms]
        if len(parts) == 2:
            return parts[0] + parts[1]
        return sum(p.astype(F32) for p in parts).astype(BF16)

    def go(self):
        self.step -= 1
        shape = self.terms[0].shape
        axis = 0 if shape[0] > 1 else 1
        half = shape[axis] // 2
        cut = lambda begin: lambda term: lax.slice_in_dim(term, begin, begin + half, axis=axis)
        came = exchange(self.sums(cut(half)), self.grid, self.step)
        self.terms = [cut(0)(term) for term in self.terms] + [came]
        return came

    def put(self, came):
        self.terms[-1] = came

    def mine(self):
        return self.sums(lambda term: term[0, 0])


def reversed_bits(value, bits):
    out = 0
    for b in range(bits):
        out = out | (((value >> b) & 1) << (bits - 1 - b))
    return out


def place_of(row, col, place, core, grid_rows, grid_cols):
    far_row = row ^ place[0]
    far_col = col ^ place[1]
    row_bits = bit_count(grid_rows)
    col_bits = bit_count(grid_cols)
    plain = far_col + far_row * grid_cols
    turned = reversed_bits(far_col, col_bits) + reversed_bits(far_row, row_bits) * grid_cols
    return jnp.where(core == 0, plain, turned)


def unpack_pair(packed, odd):
    firsts = []
    for k in range(2):
        body = packed[:, 128 * k : 128 * (k + 1)]
        rest_low, rest_high = packed[:, 256:320], packed[:, 320:384]
        in_order, turned = (rest_low, rest_high) if k == 0 else (rest_high, rest_low)
        plain = jnp.concatenate([body, in_order], axis=1)
        other = jnp.concatenate([turned, body], axis=1)
        firsts.append(jnp.where(odd, other, plain))
    return firsts


def by_core(place, mine, theirs):
    mine, theirs = mine.astype(F32), theirs.astype(F32)
    first = place[2] == 0
    return jnp.where(first, mine, theirs), jnp.where(first, theirs, mine)


def finish_one_body(place, mine, theirs, down, output, gains):
    half = down.shape[0] // 2
    quarter = half // 2
    odd = (place[1] & 1) == 1
    halves = by_core(place, mine[...], theirs[...])
    for core, part in enumerate(halves):
        down[core * half : (core + 1) * half, :] = part[:half]
        for k, block in enumerate(unpack_pair(part[half:], odd)):
            output[core * half + k * quarter : core * half + (k + 1) * quarter, :] = block
    gains[...] = halves[0][half : half + 8, 384:512]


def finish_two_body(place, mine, theirs, gate, up):
    half = gate.shape[0] // 2
    for core, part in enumerate(by_core(place, mine[...], theirs[...])):
        for k, out in enumerate((gate, up)):
            out[core * half : (core + 1) * half, :] = part[k * half : (k + 1) * half]


def finish_three_body(place, mine, theirs, query, key, value):
    half = query.shape[0] // 2
    quarter = half // 2
    odd = (place[1] & 1) == 1
    for core, part in enumerate(by_core(place, mine[...], theirs[...])):
        rows = slice(core * half, (core + 1) * half)
        query[rows, :], key[rows, :] = unpack_pair(part[:half], odd)
        for k, block in enumerate(unpack_pair(part[half:], odd)):
            value[core * half + k * quarter : core * half + (k + 1) * quarter, :] = block


def finish(body, name, place, mine, theirs, shapes):
    vmem = pl.BlockSpec(memory_space=pltpu.VMEM)
    return pl.pallas_call(
        body,
        in_specs=[pl.BlockSpec(memory_space=pltpu.SMEM)] + [vmem] * 2,
        out_specs=[vmem] * len(shapes),
        out_shape=[jax.ShapeDtypeStruct(shape, F32) for shape in shapes],
        cost_estimate=costs(1),
        name=name,
    )(place, mine, theirs)


def pack_pair(first, second, odd, out, rows):
    rolled = [jnp.concatenate([v[:, 64:], v[:, :64]], axis=1) for v in (first, second)]
    bodies = [jnp.where(odd, r[:, :128], v[:, :128]) for r, v in zip(rolled, (first, second))]
    rests = [jnp.where(odd, v[:, :64], v[:, 128:]) for v in (first, second)]
    low = jnp.where(odd, rests[1], rests[0])
    high = jnp.where(odd, rests[0], rests[1])
    out[rows, 0:128] = bodies[0].astype(BF16)
    out[rows, 128:256] = bodies[1].astype(BF16)
    out[rows, 256:384] = jnp.concatenate([low, high], axis=1).astype(BF16)


def pack_attention_body(place, query, key, value, output, gain_one, gain_two, out):
    half = query.shape[0] // 2
    quarter = half // 2
    odd = (place[1] & 1) == 1
    base = pl.multiple_of(place[2] * half, half)
    query, key, value, output = (w[pl.ds(base, half), :].astype(F32) for w in (query, key, value, output))
    pack_pair(query, key, odd, out, slice(0, half))
    pack_pair(value[:quarter], value[quarter:], odd, out, slice(half, half + quarter))
    pack_pair(output[:quarter], output[quarter:], odd, out, slice(half + quarter, 2 * half))
    share = gain_one.shape[1]
    gains = jnp.concatenate([gain_one[...].astype(F32), gain_two[...].astype(F32)], axis=0)
    gains = jnp.concatenate([gains, jnp.zeros((2, out.shape[1] - share), F32)], axis=1)
    gains = jnp.concatenate([gains, jnp.zeros((GAIN_ROWS - 2, out.shape[1]), F32)], axis=0)
    out[2 * half :, :] = gains.astype(BF16)


def pack_attention(place, query, key, value, output, gain_one, gain_two):
    vmem = pl.BlockSpec(memory_space=pltpu.VMEM)
    return pl.pallas_call(
        pack_attention_body,
        in_specs=[pl.BlockSpec(memory_space=pltpu.SMEM)] + [vmem] * 6,
        out_specs=vmem,
        out_shape=jax.ShapeDtypeStruct((query.shape[0] + GAIN_ROWS, 384), BF16),
        cost_estimate=costs(2),
        name="pack_attention",
    )(place, query, key, value, output, gain_one[None], gain_two[None])


def pack_feed_body(place, gate, up, down, one, two):
    half = gate.shape[0] // 2
    rows = pl.ds(pl.multiple_of(place[2] * half, half), half)
    one[0:half, :] = gate[rows, :]
    one[half : 2 * half, :] = up[rows, :]
    two[...] = down[rows, :]


def pack_feed(place, gate, up, down_turned):
    half = gate.shape[0] // 2
    vmem = pl.BlockSpec(memory_space=pltpu.VMEM)
    return pl.pallas_call(
        pack_feed_body,
        in_specs=[pl.BlockSpec(memory_space=pltpu.SMEM)] + [vmem] * 3,
        out_specs=[vmem] * 2,
        out_shape=[jax.ShapeDtypeStruct((n * half, gate.shape[1]), BF16) for n in (2, 1)],
        cost_estimate=costs(2),
        name="pack_feed",
    )(place, gate, up, down_turned)


def place_scalars():
    return jnp.stack([lax.axis_index("row"), lax.axis_index("col"), lax.axis_index("dp")]).astype(jnp.int32)


def split_rows(top):
    return lax.broadcasted_iota(jnp.int32, top, 1) < 64


def fill_columns(target, rows, low_even, body_even, low_odd, body_odd, pair, swapped):
    base = 384 * pair
    target[rows, base : base + 128] = body_even
    target[rows, base + 256 : base + 384] = body_odd
    first = split_rows(low_even.shape)
    if swapped:
        mixed = jnp.where(first, low_odd, low_even)
        target[rows, base + 128 : base + 256] = pltpu.roll(mixed.astype(F32), 64, 1).astype(BF16)
    else:
        target[rows, base + 128 : base + 256] = jnp.where(first, low_even, low_odd)


def piece_places(pieces):
    counts = [p.shape[0] for p in pieces]
    out = []
    for side in range(2):
        at = 0
        for count in counts[side * len(counts) // 2 : (side + 1) * len(counts) // 2]:
            out.append((side, at, count))
            at += count
    return out


def load_stacks(pieces, held, sems):
    copies = []
    for k, (piece, (side, at, count)) in enumerate(zip(pieces, piece_places(pieces))):
        copies.append(pltpu.make_async_copy(piece, held.at[side, pl.ds(at, count)], sems.at[k]))
    for copy in copies:
        copy.start()
    for copy in copies:
        copy.wait()


def assemble_attention(grid, place, held, w_query, w_key, w_value, w_output, gains):
    grid_rows, grid_cols = grid
    where = (place[0], place[1])
    half = w_query.shape[0] // grid_rows // 2
    quarter = half // 2
    width = gains.shape[1]
    share = width // (grid_rows * grid_cols)
    lane = lax.broadcasted_iota(jnp.int32, (LANES, width), 1)
    spread = (lax.rem(lane, share) == lax.broadcasted_iota(jnp.int32, (LANES, width), 0)).astype(BF16)
    block_of = lax.div(lax.broadcasted_iota(jnp.int32, (GAIN_ROWS, width), 1), share)
    total = jnp.zeros((GAIN_ROWS, width), F32)
    for core in range(2):
        side = core ^ place[2]
        for row in range(grid_rows):
            start = row * 2 * half + core * half
            for pair in range(grid_cols // 2):
                at = [place_of(row, 2 * pair + c, where, core, grid_rows, grid_cols) for c in range(2)]
                even, odd = (held.at[side, p] for p in at)
                top = slice(0, half)
                rows = slice(start, start + half)
                rest_even, rest_odd = even[top, 256:384], odd[top, 256:384]
                fill_columns(w_query, rows, rest_even, even[top, 0:128], rest_odd, odd[top, 0:128], pair, False)
                fill_columns(w_key, rows, rest_even, even[top, 128:256], rest_odd, odd[top, 128:256], pair, True)
                for k, target in enumerate((w_value, w_output)):
                    low = slice(half + k * quarter, half + (k + 1) * quarter)
                    rest_even, rest_odd = even[low, 256:384], odd[low, 256:384]
                    rows = slice(start, start + quarter)
                    fill_columns(target, rows, rest_even, even[low, 0:128], rest_odd, odd[low, 0:128], pair, False)
                    rows = slice(start + quarter, start + half)
                    fill_columns(target, rows, rest_even, even[low, 128:256], rest_odd, odd[low, 128:256], pair, True)
                if core == 0:
                    for c, block in enumerate((even, odd)):
                        spreaded = dot_nn(block[2 * half : 2 * half + GAIN_ROWS, 0:LANES], spread)
                        total = total + jnp.where(block_of == row * grid_cols + 2 * pair + c, spreaded, 0.0)
    gains[...] = total[:8]


def block_at(position, place, core, grid):
    grid_rows, grid_cols = grid
    far_row, far_col = position // grid_cols, position % grid_cols
    turned_row, turned_col = reversed_bits(far_row, bit_count(grid_rows)), reversed_bits(far_col, bit_count(grid_cols))
    first = core == 0
    return jnp.where(first, far_row, turned_row) ^ place[0], jnp.where(first, far_col, turned_col) ^ place[1]


def start_copies(grid, place, pieces, targets, turned, sems):
    grid_rows, grid_cols = grid
    half = pieces[0].shape[1] // len(targets)
    span = pieces[0].shape[2]
    for piece, (side, at, count) in zip(pieces, piece_places(pieces)):
        core = side ^ place[2]

        @pl.loop(0, count)
        def _(n):
            row, col = block_at(at + n, place, core, grid)
            row, col = (col, row) if turned else (row, col)
            rows = pl.ds(pl.multiple_of((2 * row + core) * half, half), half)
            lanes = pl.ds(pl.multiple_of(col * span, span), span)
            for k, target in enumerate(targets):
                pltpu.make_async_copy(piece.at[n, pl.ds(k * half, half)], target.at[rows, lanes], sems[k]).start()


def swap_halves(values):
    lane = lax.broadcasted_iota(jnp.int32, values.shape, 1)
    back = pltpu.roll(values, 32, 1)
    ahead = pltpu.roll(values, LANES - 32, 1)
    return jnp.where(lax.rem(lane, HEAD_DIM) < HEAD_DIM // 2, ahead, back)


def project_tile(x, w_query, w_key, w_value, cosine, sine, query, key, value):
    width = w_query.shape[1]
    step = 256
    for start in range(0, width, step):
        for weight, out in ((w_query, query), (w_key, key)):
            flat = dot_nn(x[...], weight[:, start : start + step])
            for k in range(step // LANES):
                part = flat[:, k * LANES : (k + 1) * LANES]
                turned = part * cosine[...] + swap_halves(part) * sine[...]
                out[:, start + k * LANES : start + (k + 1) * LANES] = turned.astype(BF16)
        value[:, start : start + step] = dot_nn(x[...], w_value[:, start : start + step]).astype(BF16)


def project_blocks_body(grid, count, place, *refs):
    pieces, refs = refs[:count], refs[count:]
    x, cosine, sine, query, key, value, w_query, w_key, w_value, w_output, gains, held, sems = refs

    @pl.when(pl.program_id(0) == 0)
    def _():
        load_stacks(pieces, held, sems)
        assemble_attention(grid, place, held, w_query, w_key, w_value, w_output, gains)

    project_tile(x, w_query, w_key, w_value, cosine, sine, query, key, value)


def project_blocks(pieces, place, grid, x, cosine, sine):
    tokens, width = x.shape
    _, height, lanes = pieces[0].shape
    rows = 256
    tile = pl.BlockSpec((rows, width), lambda i: (i, 0))
    table = pl.BlockSpec((rows, LANES), lambda i: (i, 0))
    whole = pl.BlockSpec((width, width), lambda i: (0, 0), pipeline_mode=pl.Buffered(1))
    anywhere = pl.BlockSpec(memory_space=pl.ANY)
    return pl.pallas_call(
        lambda *refs: project_blocks_body(grid, len(pieces), *refs),
        grid=(tokens // rows,),
        in_specs=[pl.BlockSpec(memory_space=pltpu.SMEM)] + [anywhere] * len(pieces) + [tile, table, table],
        out_specs=[tile] * 3 + [whole] * 4 + [pl.BlockSpec((8, width), lambda i: (0, 0))],
        out_shape=[jax.ShapeDtypeStruct((tokens, width), BF16)] * 3
        + [jax.ShapeDtypeStruct((width, width), BF16)] * 4
        + [jax.ShapeDtypeStruct((8, width), F32)],
        scratch_shapes=[
            pltpu.VMEM((2, grid[0] * grid[1], height, lanes), BF16),
            pltpu.SemaphoreType.DMA((len(pieces),)),
        ],
        cost_estimate=costs(10),
        name="project_heads",
    )(place, *pieces, x, cosine, sine)


def project(x, w_query, w_key, w_value, cosine, sine):
    tokens, width = x.shape
    rows = 256
    tile = pl.BlockSpec((rows, width), lambda i: (i, 0))
    table = pl.BlockSpec((rows, LANES), lambda i: (i, 0))
    whole = pl.BlockSpec((width, width), lambda i: (0, 0))
    return pl.pallas_call(
        project_tile,
        grid=(tokens // rows,),
        in_specs=[tile, whole, whole, whole, table, table],
        out_specs=[tile] * 3,
        out_shape=[jax.ShapeDtypeStruct((tokens, width), BF16)] * 3,
        name="project_heads_plain",
    )(x, w_query, w_key, w_value, cosine, sine)


def own_half(values, h):
    zero = jnp.zeros_like(values)
    return jnp.concatenate([values, zero] if h == 0 else [zero, values], axis=0)


def attention_forward_body(first, q_ref, k_ref, v_ref, context_ref, lse_ref):
    q_turned = (q_ref[...].astype(F32) * HEAD_DIM**-0.5).T.astype(BF16)
    v_turned = v_ref[...].T
    square = (LANES, LANES)
    causal = lax.broadcasted_iota(jnp.int32, square, 0) <= lax.broadcasted_iota(jnp.int32, square, 1)
    lse_ref[...] = jnp.zeros_like(lse_ref)
    for t in range(q_ref.shape[0] // LANES):
        now = slice(t * LANES, (t + 1) * LANES)
        begin = first[t * LANES // QUERY_BLOCK]
        outs = []
        for h in range(2):
            head = slice(h * HEAD_DIM, (h + 1) * HEAD_DIM)
            mine = own_half(q_turned[head, now], h)
            for b in [t, *range(t)]:
                there = slice(b * LANES, (b + 1) * LANES)
                scores = dot_nn(k_ref[there, :], mine)
                if b == t:
                    scores = jnp.where(causal, scores, NEGATIVE)
                block_top = jnp.max(scores, axis=0, keepdims=True) * LOG2E
                if b == t:
                    new_top = base = block_top
                else:
                    seen = begin <= b * LANES // QUERY_BLOCK
                    new_top = jnp.maximum(top, jnp.where(seen, block_top, NEGATIVE))
                    base = new_top + jnp.where(seen, 0.0, -NEGATIVE)
                weights = jnp.exp2(scores * LOG2E - base)
                part_total = jnp.sum(weights, axis=0, keepdims=True)
                part = dot_nn(v_turned[head, there], weights.astype(BF16))
                if b == t:
                    total, mixed = part_total, part
                else:
                    shrink = jnp.exp2(top - new_top)
                    total = total * shrink + part_total
                    mixed = mixed * shrink + part
                top = new_top
            outs.append(mixed * (1.0 / total))
            lse_ref[0, h : h + 1, now] = top + jnp.log2(total)
        context_ref[now, :] = jnp.concatenate(outs, axis=0).T.astype(BF16)


def attention_forward(first, query, key, value, begin, pairs):
    tokens = query.shape[0]
    spec = pl.BlockSpec((tokens, LANES), lambda j, f: (0, j + begin))
    part = pl.BlockSpec((tokens, LANES), lambda j, f: (0, j))
    return pl.pallas_call(
        attention_forward_body,
        grid_spec=pltpu.PrefetchScalarGridSpec(
            num_scalar_prefetch=1,
            grid=(pairs,),
            in_specs=[spec] * 3,
            out_specs=[part, pl.BlockSpec((1, 8, tokens), lambda j, f: (j, 0, 0))],
        ),
        out_shape=[
            jax.ShapeDtypeStruct((tokens, pairs * LANES), BF16),
            jax.ShapeDtypeStruct((pairs, 8, tokens), F32),
        ],
        cost_estimate=costs(4 * pairs),
        name="attention_forward",
    )(first, query, key, value)


def attention_backward_body(first, q_ref, k_ref, v_ref, grad_ref, context_ref, lse_ref, cosine, sine, *refs):
    dq_ref, dk_ref, dv_ref, dk_sum, dv_sum = refs[-5:]
    blocks = q_ref.shape[0] // QUERY_BLOCK
    scaled = q_ref[...].astype(F32) * HEAD_DIM**-0.5
    q_turned = scaled.T.astype(BF16)
    q_plain = scaled.astype(BF16)
    k_turned = k_ref[...].T
    grad = grad_ref[...]
    grad_turned = grad.T
    inner = (grad.astype(F32) * context_ref[...].astype(F32)).T
    square = (QUERY_BLOCK, QUERY_BLOCK)
    causal = lax.broadcasted_iota(jnp.int32, square, 0) <= lax.broadcasted_iota(jnp.int32, square, 1)
    low_lanes = lax.broadcasted_iota(jnp.int32, (QUERY_BLOCK, LANES), 1) < HEAD_DIM
    for i in reversed(range(blocks)):
        now = slice(i * QUERY_BLOCK, (i + 1) * QUERY_BLOCK)
        seen = slice(0, (i + 1) * QUERY_BLOCK)
        grads = []
        for h in range(2):
            head = slice(h * HEAD_DIM, (h + 1) * HEAD_DIM)
            own_lanes = low_lanes if h == 0 else jnp.logical_not(low_lanes)
            q_rows = jnp.where(own_lanes, q_plain[now, :], 0)
            g_rows = jnp.where(own_lanes, grad[now, :], 0)
            delta = jnp.sum(inner[head, now], axis=0, keepdims=True)
            lse = lse_ref[0, h : h + 1, now]
            scores = dot_nn(k_ref[seen, :], own_half(q_turned[head, now], h))
            grad_probs = dot_nn(v_ref[seen, :], own_half(grad_turned[head, now], h))
            probs, grad_scores = [], []
            for b in range(i + 1):
                there = slice(b * QUERY_BLOCK, (b + 1) * QUERY_BLOCK)
                part = scores[there]
                base = lse if b == i else lse + jnp.where(first[i] <= b, 0.0, -NEGATIVE)
                if b == i:
                    part = jnp.where(causal, part, NEGATIVE)
                part = jnp.exp2(part * LOG2E - base)
                probs.append(part.astype(BF16))
                grad_scores.append((part * (grad_probs[there] - delta)).astype(BF16))
            probs, grad_scores = jnp.concatenate(probs, axis=0), jnp.concatenate(grad_scores, axis=0)
            dv, dk = dot_nn(probs, g_rows), dot_nn(grad_scores, q_rows)
            if i == blocks - 1 and h == 0:
                dv_sum[...] = dv
                dk_sum[...] = dk
            else:
                dv_sum[seen, :] += dv
                dk_sum[seen, :] += dk
            grads.append(dot_nn(k_turned[head, seen], grad_scores) * HEAD_DIM**-0.5)
        dq = jnp.concatenate(grads, axis=0).T
        dq_ref[now, :] = (dq * cosine[now, :] - swap_halves(dq) * sine[now, :]).astype(BF16)
    dk = dk_sum[...]
    dk_ref[...] = (dk * cosine[...] - swap_halves(dk) * sine[...]).astype(BF16)
    dv_ref[...] = dv_sum[...].astype(BF16)


def attention_backward(first, query, key, value, grad, context, lse, cosine, sine, begin, pairs, into):
    tokens, width = query.shape
    spec = pl.BlockSpec((tokens, LANES), lambda j, f: (0, j + begin))
    table = pl.BlockSpec((tokens, LANES), lambda j, f: (0, 0))
    anywhere = pl.BlockSpec(memory_space=pl.ANY)
    return pl.pallas_call(
        attention_backward_body,
        grid_spec=pltpu.PrefetchScalarGridSpec(
            num_scalar_prefetch=1,
            grid=(pairs,),
            in_specs=[spec] * 5
            + [pl.BlockSpec((1, 8, tokens), lambda j, f: (j + begin, 0, 0)), table, table]
            + [anywhere] * len(into),
            out_specs=[spec] * 3,
            scratch_shapes=[pltpu.VMEM((tokens, LANES), F32)] * 2,
        ),
        out_shape=[jax.ShapeDtypeStruct((tokens, width), BF16)] * 3,
        input_output_aliases={9 + k: k for k in range(len(into))},
        cost_estimate=costs(6 * pairs),
        name="attention_backward",
    )(first, query, key, value, grad, context, lse, cosine, sine, *into)


CHUNK = 512


def inner_tile(context, x, w_output, w_gate, w_up, gains, ready, first_sum, hidden_in_turned, context_turned, hidden, slope, act):
    context_now = context[...]
    total = x[...].astype(F32) + dot_nn(context_now, w_output[...])
    first_sum[...] = total
    scale_one = lax.rsqrt(jnp.mean(total * total, axis=1, keepdims=True) + EPSILON)
    hidden_in = (total * scale_one * gains[0:1, :]).astype(BF16)
    context_turned[...] = context_now.T
    hidden_in_turned[...] = hidden_in.T
    ready()
    for start in range(0, w_gate.shape[1], CHUNK):
        cols = slice(start, start + CHUNK)
        gate_act = dot_nn(hidden_in, w_gate[:, cols])
        up_act = dot_nn(hidden_in, w_up[:, cols])
        sigmoid = jax.nn.sigmoid(gate_act)
        silu = gate_act * sigmoid
        act[:, cols] = silu
        slope[:, cols] = up_act * (sigmoid + silu * (1.0 - sigmoid))
        hidden[:, cols] = (silu * up_act).astype(BF16)


def outer_tile(
    first_sum, hidden, slope, act, cotangent, w_output, w_gate, w_up, w_down, gains, ready,
    layer_out, branch_two_turned, grad_gate, grad_up, grad_first, branch_one, grad_context, gain_grads,
):
    width = first_sum.shape[1]
    gain_one = gains[0:1, :]
    gain_two = gains[1:2, :]
    total = first_sum[...]
    scale_one = lax.rsqrt(jnp.mean(total * total, axis=1, keepdims=True) + EPSILON)
    normed_one = total * scale_one
    ready(0)
    second_sum = normed_one * gain_one + dot_nt(hidden[...], w_down[...])
    scale_two = lax.rsqrt(jnp.mean(second_sum * second_sum, axis=1, keepdims=True) + EPSILON)
    normed_two = second_sum * scale_two
    layer_out[...] = (normed_two * gain_two).astype(BF16)
    grad_out = cotangent[...].astype(F32)
    two_term = jnp.sum(grad_out * normed_two, axis=0, keepdims=True)
    scaled = grad_out * gain_two
    grad_second = scale_two * (scaled - normed_two * jnp.mean(scaled * normed_two, axis=1, keepdims=True))
    branch_two = grad_second.astype(BF16)
    branch_two_turned[...] = branch_two.T
    grad_normed = grad_second
    ready(1)
    for start in range(0, w_down.shape[1], CHUNK):
        cols = slice(start, start + CHUNK)
        grad_hidden = dot_nn(branch_two, w_down[:, cols])
        gate_now = (grad_hidden * slope[:, cols]).astype(BF16)
        up_now = (grad_hidden * act[:, cols]).astype(BF16)
        grad_gate[:, cols] = gate_now
        grad_up[:, cols] = up_now
        grad_normed = grad_normed + dot_nt(gate_now, w_gate[:, cols]) + dot_nt(up_now, w_up[:, cols])
    one_term = jnp.sum(grad_normed * normed_one, axis=0, keepdims=True)
    scaled = grad_normed * gain_one
    first_grad = scale_one * (scaled - normed_one * jnp.mean(scaled * normed_one, axis=1, keepdims=True))
    grad_first[...] = first_grad
    one_now = first_grad.astype(BF16)
    branch_one[...] = one_now
    grad_context[...] = dot_nt(one_now, w_output[...]).astype(BF16)
    terms = jnp.concatenate([one_term, two_term, jnp.zeros((6, width), F32)], axis=0)

    @pl.when(pl.program_id(0) == 0)
    def _():
        gain_grads[...] = terms

    @pl.when(pl.program_id(0) > 0)
    def _():
        gain_grads[...] += terms


def wait_for(target, sem):
    pltpu.make_async_copy(target, target, sem).wait()


def inner_body(grid, count, place, *refs):
    pieces, refs = refs[:count], refs[count:]
    context, x, w_output, gains = refs[:4]
    outs, (w_gate, w_up, gate_sem, up_sem) = refs[4:-4], refs[-4:]
    here = pl.program_id(0) == 0

    @pl.when(here)
    def _():
        start_copies(grid, place, pieces, (w_gate, w_up), False, (gate_sem, up_sem))

    def ready():
        @pl.when(here)
        def _():
            wait_for(w_gate, gate_sem)
            wait_for(w_up, up_sem)

    inner_tile(context, x, w_output, w_gate, w_up, gains, ready, *outs)


def outer_body(grid, counts, place, *refs):
    gate_pieces, refs = refs[: counts[0]], refs[counts[0] :]
    down_pieces, refs = refs[: counts[1]], refs[counts[1] :]
    first_sum, hidden, slope, act, cotangent, w_output, gains = refs[:7]
    outs, (w_gate, w_up, w_down, gate_sem, up_sem, down_sem) = refs[7:-6], refs[-6:]
    here = pl.program_id(0) == 0

    @pl.when(here)
    def _():
        start_copies(grid, place, down_pieces, (w_down,), True, (down_sem,))
        start_copies(grid, place, gate_pieces, (w_gate, w_up), False, (gate_sem, up_sem))

    def ready(k):
        @pl.when(here)
        def _():
            if k == 0:
                wait_for(w_down, down_sem)
            else:
                wait_for(w_gate, gate_sem)
                wait_for(w_up, up_sem)

    outer_tile(first_sum, hidden, slope, act, cotangent, w_output, w_gate, w_up, w_down, gains, ready, *outs)


def feed_specs(tokens, width, span, rows):
    return dict(
        tile=pl.BlockSpec((rows, width), lambda i: (i, 0)),
        turned=pl.BlockSpec((width, rows), lambda i: (0, i)),
        wide=pl.BlockSpec((rows, span), lambda i: (i, 0)),
        square=pl.BlockSpec((width, width), lambda i: (0, 0), pipeline_mode=pl.Buffered(1)),
        whole=pl.BlockSpec((width, span), lambda i: (0, 0), pipeline_mode=pl.Buffered(1)),
        eight=pl.BlockSpec((8, width), lambda i: (0, 0)),
    )


def inner_outs(tokens, width, span):
    shapes = (
        ("tile", (tokens, width), F32), ("turned", (width, tokens), BF16), ("turned", (width, tokens), BF16),
        ("wide", (tokens, span), BF16), ("wide", (tokens, span), F32), ("wide", (tokens, span), F32),
    )
    return [s[0] for s in shapes], [jax.ShapeDtypeStruct(s[1], s[2]) for s in shapes]


def outer_outs(tokens, width, span):
    shapes = (
        ("tile", (tokens, width), BF16), ("turned", (width, tokens), BF16), ("wide", (tokens, span), BF16),
        ("wide", (tokens, span), BF16), ("tile", (tokens, width), F32), ("tile", (tokens, width), BF16),
        ("tile", (tokens, width), BF16), ("eight", (8, width), F32),
    )
    return [s[0] for s in shapes], [jax.ShapeDtypeStruct(s[1], s[2]) for s in shapes]


ROWS = 256


def feed_inner(pieces, place, grid, context, x, w_output, gains):
    tokens, width = x.shape
    span = pieces[0].shape[2] * grid[1]
    spec = feed_specs(tokens, width, span, ROWS)
    outs, shapes = inner_outs(tokens, width, span)
    return pl.pallas_call(
        lambda *refs: inner_body(grid, len(pieces), *refs),
        grid=(tokens // ROWS,),
        in_specs=[pl.BlockSpec(memory_space=pltpu.SMEM)]
        + [pl.BlockSpec(memory_space=pl.ANY)] * len(pieces)
        + [spec[n] for n in ("tile", "tile", "square", "eight")],
        out_specs=[spec[n] for n in outs],
        out_shape=shapes,
        scratch_shapes=[pltpu.VMEM((width, span), BF16)] * 2 + [pltpu.SemaphoreType.DMA] * 2,
        cost_estimate=costs(15),
        name="feed_forward_inner",
    )(place, *pieces, context, x, w_output, gains)


def feed_outer(gate_pieces, down_pieces, place, grid, kept, cotangent, w_output, gains):
    first_sum, hidden, slope, act = kept
    tokens, width = first_sum.shape
    span = hidden.shape[1]
    spec = feed_specs(tokens, width, span, ROWS)
    outs, shapes = outer_outs(tokens, width, span)
    return pl.pallas_call(
        lambda *refs: outer_body(grid, (len(gate_pieces), len(down_pieces)), *refs),
        grid=(tokens // ROWS,),
        in_specs=[pl.BlockSpec(memory_space=pltpu.SMEM)]
        + [pl.BlockSpec(memory_space=pl.ANY)] * (len(gate_pieces) + len(down_pieces))
        + [spec[n] for n in ("tile", "wide", "wide", "wide", "tile", "square", "eight")],
        out_specs=[spec[n] for n in outs],
        out_shape=shapes,
        scratch_shapes=[pltpu.VMEM((width, span), BF16)] * 3 + [pltpu.SemaphoreType.DMA] * 3,
        cost_estimate=costs(25),
        name="feed_forward_outer",
    )(place, *gate_pieces, *down_pieces, first_sum, hidden, slope, act, cotangent, w_output, gains)


def feed_inner_plain(context, x, w_output, w_gate, w_up, gains):
    tokens, width = x.shape
    span = w_gate.shape[1]
    spec = feed_specs(tokens, width, span, ROWS)
    outs, shapes = inner_outs(tokens, width, span)

    def body(context, x, w_output, w_gate, w_up, gains, *refs):
        inner_tile(context, x, w_output, w_gate, w_up, gains, lambda: None, *refs)

    return pl.pallas_call(
        body,
        grid=(tokens // ROWS,),
        in_specs=[spec[n] for n in ("tile", "tile", "square", "whole", "whole", "eight")],
        out_specs=[spec[n] for n in outs],
        out_shape=shapes,
        name="feed_forward_inner_plain",
    )(context, x, w_output, w_gate, w_up, gains)


def feed_outer_plain(kept, cotangent, w_output, w_gate, w_up, w_down, gains):
    tokens, width = kept[0].shape
    span = w_gate.shape[1]
    spec = feed_specs(tokens, width, span, ROWS)
    outs, shapes = outer_outs(tokens, width, span)

    def body(*refs):
        outer_tile(*refs[:10], lambda k: None, *refs[10:])

    return pl.pallas_call(
        body,
        grid=(tokens // ROWS,),
        in_specs=[spec[n] for n in ("tile", "wide", "wide", "wide", "tile", "square", "whole", "whole", "whole", "eight")],
        out_specs=[spec[n] for n in outs],
        out_shape=shapes,
        name="feed_forward_outer_plain",
    )(*kept, cotangent, w_output, w_gate, w_up, w_down, gains)


def part_of(index, place_index, core, count):
    far = index ^ place_index
    return jnp.where(core == 0, far, reversed_bits(far, bit_count(count)))


def store_halves(own, other, where, grid, core_here, row, col, rows, lanes, halves):
    here = core_here == 0
    for target, core, first, second in ((own, core_here, 0, 1), (other, 1 - core_here, 1, 0)):
        at = part_of(row, where[0], core, grid[0]), part_of(col, where[1], core, grid[1])
        target[at[0], at[1], rows, lanes] = jnp.where(here, halves[first], halves[second])


def rest_tile(first, second, odd):
    low = split_rows(first.shape)
    rolled = pltpu.roll(second, 64, 1)
    return jnp.where(low, rolled, first) if odd else jnp.where(low, first, rolled)


def feed_grads_body(grid, count, place, left, *refs):
    rights, (own, other) = refs[:count], refs[-2:]
    grid_rows, grid_cols = grid
    half = left.shape[0] // grid_rows // 2
    step = pl.program_id(0)
    here = place[2] == 0
    for k, right in enumerate(rights):

        @pl.when(step // grid_cols == k)
        def _():
            product = dot_nn(left[...], right[...]).astype(BF16)
            for i in range(grid_rows):
                first, second = (product[(2 * i + c) * half : (2 * i + c + 1) * half] for c in range(2))
                mine, theirs = part_of(i, place[0], place[2], grid_rows), part_of(i, place[0], 1 - place[2], grid_rows)
                own[mine, 0] = jnp.where(here, first, second)
                other[theirs, 0] = jnp.where(here, second, first)


def feed_grads(place, grid, left, rights):
    width, tokens = left.shape
    grid_rows, grid_cols = grid
    span = rights[0].shape[1] // grid_cols
    half = width // grid_rows // 2
    count = len(rights)

    def out_index(flip):
        return lambda i, s: (0, part_of(lax.rem(i, grid_cols), s[1], s[2] ^ flip, grid_cols), i // grid_cols, 0)

    block = (grid_rows, 1, half, span)
    shape = (grid_rows, grid_cols, half * count, span)
    return pl.pallas_call(
        lambda *refs: feed_grads_body(grid, count, *refs),
        grid_spec=pltpu.PrefetchScalarGridSpec(
            num_scalar_prefetch=1,
            grid=(grid_cols * count,),
            in_specs=[pl.BlockSpec((width, tokens), lambda i, s: (0, 0), pipeline_mode=pl.Buffered(1))]
            + [
                pl.BlockSpec((tokens, span), lambda i, s, k=k: (0, jnp.clip(i - k * grid_cols, 0, grid_cols - 1)))
                for k in range(count)
            ],
            out_specs=[pl.BlockSpec(block, out_index(f)) for f in range(2)],
        ),
        out_shape=[jax.ShapeDtypeStruct(shape, BF16)] * 2,
        cost_estimate=costs(7 * count),
        name="feed_forward_weight_grad",
    )(place, left, *rights)


def down_grads_body(grid, place, branch_two_turned, hidden, context_turned, branch_one, gain_grads, own, other):
    grid_rows, grid_cols = grid
    width = branch_two_turned.shape[0]
    half = width // grid_cols // 2
    quarter = half // 2
    here = place[2] == 0
    row = pl.program_id(0)
    down = dot_nn(branch_two_turned[...], hidden[...]).astype(BF16)
    output = dot_nn(context_turned[...], branch_one[...])
    share = width // (grid_rows * grid_cols)
    lane = lax.broadcasted_iota(jnp.int32, (width, LANES), 0)
    gather = (lax.rem(lane, share) == lax.broadcasted_iota(jnp.int32, (width, LANES), 1)).astype(BF16)
    block_of = lax.div(lax.broadcasted_iota(jnp.int32, (8, width), 1), share)
    low = slice(half, half + quarter)

    def store(mine, theirs, rows, lanes, halves):
        own[0, mine, rows, lanes] = jnp.where(here, halves[0], halves[1])
        other[0, theirs, rows, lanes] = jnp.where(here, halves[1], halves[0])

    for c in range(grid_cols):
        at = part_of(c, place[1], place[2], grid_cols), part_of(c, place[1], 1 - place[2], grid_cols)
        store(*at, slice(0, half), slice(0, down.shape[1]), [down[(2 * c + k) * half : (2 * c + k + 1) * half] for k in range(2)])
        tile = 384 * (c // 2)
        odd = c % 2
        body = slice(tile + 256 * odd, tile + 256 * odd + 128)
        mid = slice(tile + 128, tile + 256)
        tops, lows = ([slice(k * half + n * quarter, k * half + (n + 1) * quarter) for k in range(2)] for n in range(2))
        store(*at, low, slice(0, 128), [output[t, body].astype(BF16) for t in tops])
        store(*at, low, slice(128, 256), [output[t, body].astype(BF16) for t in lows])
        store(*at, low, slice(256, 384), [rest_tile(output[t, mid], output[l, mid], odd).astype(BF16) for t, l in zip(tops, lows)])
        picked = jnp.where(block_of == row * grid_cols + c, gain_grads[...], 0.0).astype(BF16)
        gain = dot_nn(picked, gather)
        gain = jnp.concatenate([gain, jnp.zeros((quarter - 8, LANES), F32)], axis=0).astype(BF16)
        store(*at, low, slice(384, 512), [gain, gain])


def down_grads(place, grid, branch_two_turned, hidden, context_turned, branch_one, gain_grads):
    width, tokens = branch_two_turned.shape
    grid_rows, grid_cols = grid
    span = hidden.shape[1] // grid_rows
    half = width // grid_cols // 2
    height = half + half // 2

    def out_index(flip):
        return lambda i, s: (part_of(i, s[0], s[2] ^ flip, grid_rows), 0, 0, 0)

    once = dict(pipeline_mode=pl.Buffered(1))
    own, other = pl.pallas_call(
        lambda *refs: down_grads_body(grid, *refs),
        grid_spec=pltpu.PrefetchScalarGridSpec(
            num_scalar_prefetch=1,
            grid=(grid_rows,),
            in_specs=[
                pl.BlockSpec((width, tokens), lambda i, s: (0, 0), **once),
                pl.BlockSpec((tokens, span), lambda i, s: (0, i)),
                pl.BlockSpec((width // grid_rows, tokens), lambda i, s: (i, 0)),
                pl.BlockSpec((tokens, width), lambda i, s: (0, 0), **once),
                pl.BlockSpec((8, width), lambda i, s: (0, 0)),
            ],
            out_specs=[pl.BlockSpec((1, grid_cols, height, span), out_index(f)) for f in range(2)],
        ),
        out_shape=[jax.ShapeDtypeStruct((grid_rows, grid_cols, height, span), BF16)] * 2,
        cost_estimate=costs(10),
        name="down_weight_grad",
    )(place, branch_two_turned, hidden, context_turned, branch_one, gain_grads)
    return own, other


def attention_grads_body(grid, place, x_turned, grad_query, grad_key, grad_value, own, other):
    grid_rows, grid_cols = grid
    where = (place[0], place[1])
    half = x_turned.shape[0] // grid_rows // 2
    quarter = half // 2
    pair = pl.program_id(0)
    query, key, value = (dot_nn(x_turned[...], g[...]) for g in (grad_query, grad_key, grad_value))
    mid = slice(128, 256)
    for row in range(grid_rows):
        for odd in range(2):
            body = slice(256 * odd, 256 * odd + 128)
            pieces = []
            for core in range(2):
                start = row * 2 * half + core * half
                rows = slice(start, start + half)
                top, low = slice(start, start + quarter), slice(start + quarter, start + half)
                joined = (query[rows, body], key[rows, body], rest_tile(query[rows, mid], key[rows, mid], odd))
                last = (value[top, body], value[low, body], rest_tile(value[top, mid], value[low, mid], odd))
                pieces.append([p.astype(BF16) for p in joined + last])
            for k in range(3):
                lanes = slice(128 * k, 128 * (k + 1))
                at = (row, 2 * pair + odd)
                store_halves(own, other, where, grid, place[2], *at, slice(0, half), lanes, [p[k] for p in pieces])
                store_halves(own, other, where, grid, place[2], *at, slice(half, half + quarter), lanes, [p[3 + k] for p in pieces])


def attention_grads(place, grid, x_turned, grads):
    width, tokens = x_turned.shape
    grid_rows, grid_cols = grid
    half = width // grid_rows // 2
    shape = (grid_rows, grid_cols, half + half // 2, 384)
    out = pl.BlockSpec(shape, lambda i, s: (0, 0, 0, 0), pipeline_mode=pl.Buffered(1))
    return pl.pallas_call(
        lambda *refs: attention_grads_body(grid, *refs),
        grid_spec=pltpu.PrefetchScalarGridSpec(
            num_scalar_prefetch=1,
            grid=(width // 384,),
            in_specs=[pl.BlockSpec((width, tokens), lambda i, s: (0, 0), pipeline_mode=pl.Buffered(1))]
            + [pl.BlockSpec((tokens, 384), lambda i, s: (0, i))] * 3,
            out_specs=[out] * 2,
        ),
        out_shape=[jax.ShapeDtypeStruct(shape, BF16)] * 2,
        cost_estimate=costs(8),
        name="attention_weight_grads",
    )(place, x_turned, *grads)


def input_grad_body(grad_first, grad_query, grad_key, grad_value, w_query, w_key, w_value, out):
    total = grad_first[...]
    for grad, weight in ((grad_query, w_query), (grad_key, w_key), (grad_value, w_value)):
        total = total + dot_nt(grad[...], weight[...])
    out[...] = total.astype(BF16)


def input_gradient(grad_first, grads, w_query, w_key, w_value):
    tokens, width = grad_first.shape
    rows = 256
    tile = pl.BlockSpec((rows, width), lambda i: (i, 0))
    whole = pl.BlockSpec((width, width), lambda i: (0, 0), pipeline_mode=pl.Buffered(1))
    return pl.pallas_call(
        input_grad_body,
        grid=(tokens // rows,),
        in_specs=[tile] * 4 + [whole] * 3,
        out_specs=tile,
        out_shape=jax.ShapeDtypeStruct((tokens, width), BF16),
        cost_estimate=costs(8),
        name="input_gradient",
    )(grad_first, *grads, w_query, w_key, w_value)


def gather_plain(block):
    whole = lax.all_gather(block, "col", axis=1, tiled=True)
    return lax.all_gather(whole, "row", axis=0, tiled=True)


def scatter_plain(whole):
    part = lax.psum_scatter(whole.astype(BF16), "row", scatter_dimension=0, tiled=True)
    part = lax.psum_scatter(part, "col", scatter_dimension=1, tiled=True)
    return lax.psum(part, "dp").astype(F32)


def scatter_gain(whole):
    part = lax.psum_scatter(whole.astype(BF16), ("row", "col"), scatter_dimension=0, tiled=True)
    return lax.psum(part, "dp").astype(F32)


def on_device(
    inputs,
    segment_ids,
    query_weight,
    key_weight,
    value_weight,
    output_weight,
    gate_weight,
    up_weight,
    down_weight,
    first_gain,
    second_gain,
    cotangent,
):
    grid = (lax.axis_size("row"), lax.axis_size("col"))
    tokens, width = inputs.shape
    hidden_width = gate_weight.shape[1] * grid[1]
    core = lax.axis_index("dp")
    odd = (lax.axis_index("col") & 1) == 1
    place = place_scalars()
    packs = grid == (4, 4) and query_weight.shape[1] == 192 and gate_weight.shape[1] == 512

    def tables(segments):
        token_index = jnp.arange(tokens, dtype=jnp.int32)
        length = tokens // (segments[tokens - 1] + 1)
        starts = segments * length
        positions = (token_index - starts).astype(F32)
        frequencies = ROPE_BASE ** (-2.0 * jnp.arange(HEAD_DIM // 2, dtype=F32) / HEAD_DIM)
        phases = positions[:, None] * frequencies[None, :]
        cosine, sine = jnp.cos(phases), jnp.sin(phases)
        cosine = jnp.concatenate([cosine] * 4, axis=1)
        sine = jnp.concatenate([-sine, sine] * 2, axis=1)
        return cosine, sine, starts[::QUERY_BLOCK] // QUERY_BLOCK

    def backward(grad_context, context, lse, begin, pairs, into):
        return attention_backward(first, query, key, value, grad_context, context, lse, cosine, sine, begin, pairs, into)

    if not packs:
        cosine, sine, first = tables(segment_ids)
        x_turned = inputs.T
        w_query, w_key, w_value, w_output = (
            gather_plain(w) for w in (query_weight, key_weight, value_weight, output_weight)
        )
        w_gate, w_up, w_down = gather_plain(gate_weight), gather_plain(up_weight), gather_plain(down_weight).T
        gains = jnp.stack(
            [lax.all_gather(g, ("row", "col"), axis=0, tiled=True).astype(F32) for g in (first_gain, second_gain)]
        )
        gains = jnp.pad(gains, ((0, 6), (0, 0)))
        query, key, value = project(inputs, w_query, w_key, w_value, cosine, sine)
        context, lse = attention_forward(first, query, key, value, 0, width // LANES)
        first_sum, hidden_in_turned, context_turned, hidden, slope, act = feed_inner_plain(
            context, inputs, w_output, w_gate, w_up, gains
        )
        layer_out, branch_two_turned, grad_gate, grad_up, grad_first, branch_one, grad_context, gain_grads = feed_outer_plain(
            (first_sum, hidden, slope, act), cotangent, w_output, w_gate, w_up, w_down, gains
        )
        grads = backward(grad_context, context, lse, 0, width // LANES, ())
        input_grad = input_gradient(grad_first, grads, w_query, w_key, w_value)
        query_out, key_out, value_out = (scatter_plain(dot_nn(x_turned, g)) for g in grads)
        output_out = scatter_plain(dot_nn(context_turned, branch_one))
        gate_out, up_out = (scatter_plain(dot_nn(hidden_in_turned, g)) for g in (grad_gate, grad_up))
        down_out = scatter_plain(dot_nn(branch_two_turned, hidden).T)
        gain_one_out, gain_two_out = scatter_gain(gain_grads[0]), scatter_gain(gain_grads[1])
        return (
            layer_out, input_grad, query_out, key_out, value_out, output_out, gate_out, up_out, down_out, gain_one_out, gain_two_out,
        )

    join = lambda *stacks: jnp.concatenate(stacks, axis=0)
    q0 = pack_attention(place, query_weight, key_weight, value_weight, output_weight, first_gain, second_gain)[None]
    g0, d0 = pack_feed(place, gate_weight, up_weight, down_weight.T)
    g0, d0 = g0[None], d0[None]
    q1 = exchange(q0, grid, 0)
    g1 = exchange(g0, grid, 0)
    q1, g0, d0, segments, x_in = tie(q1, g0, d0, segment_ids, inputs)
    q01 = join(q0, q1)
    q2 = exchange(q01, grid, 1)
    cosine, sine, first = tables(segments)
    x_turned = x_in.T
    q2, g1, cosine, sine, x_turned, first = tie(q2, g1, cosine, sine, x_turned, first)
    q03 = join(q01, q2)
    g01 = join(g0, g1)
    q3, q4 = exchange(q03, grid, 2), exchange(q03, grid, 3)
    q03_other = other_core(q03)
    g2 = exchange(g01, grid, 1)
    q3, q4, q03_other, g2 = tie(q3, q4, q03_other, g2)
    q5 = exchange(q3, grid, 3)
    q3_other, q4_other = other_core(q3), other_core(q4)
    d1 = exchange(d0, grid, 0)
    q5, q3_other, q4_other, d1, g01, g2 = tie(q5, q3_other, q4_other, d1, g01, g2)
    q5_other = other_core(q5)
    g03 = join(g01, g2)
    g3, g4 = exchange(g03, grid, 2), exchange(g03, grid, 3)
    d01 = join(d0, d1)
    d2 = exchange(d01, grid, 1)
    query, key, value, w_query, w_key, w_value, w_output, gains = project_blocks(
        (q03, q3, q4, q5, q03_other, q3_other, q4_other, q5_other), place, grid, inputs, cosine, sine
    )
    g3, g4, d2, query = tie(g3, g4, d2, query)
    g5 = exchange(g3, grid, 3)
    d03 = join(d01, d2)
    d3 = exchange(d03, grid, 2)
    g03_other, g3_other, g4_other = other_core(g03), other_core(g3), other_core(g4)
    context, lse = attention_forward(first, query, key, value, 0, width // LANES)
    g5, d3, g03_other, g3_other, g4_other, d03, context = tie(g5, d3, g03_other, g3_other, g4_other, d03, context)
    g5_other = other_core(g5)
    d4, d5 = exchange(d03, grid, 3), exchange(d3, grid, 3)
    d03_other, d3_other = other_core(d03), other_core(d3)
    gate_pieces = (g03, g3, g4, g5, g03_other, g3_other, g4_other, g5_other)
    first_sum, hidden_in_turned, context_turned, hidden, slope, act = feed_inner(
        gate_pieces, place, grid, context, inputs, w_output, gains
    )
    d4, d5, d03_other, d3_other, first_sum = tie(d4, d5, d03_other, d3_other, first_sum)
    down_pieces = (d03, d3, d4, d5, d03_other, d3_other, other_core(d4), other_core(d5))
    layer_out, branch_two_turned, grad_gate, grad_up, grad_first, branch_one, grad_context, gain_grads = feed_outer(
        gate_pieces, down_pieces, place, grid, (first_sum, hidden, slope, act), cotangent, w_output, gains
    )

    pairs = width // LANES
    two = Scatter(*feed_grads(place, grid, hidden_in_turned, (grad_gate, grad_up)), grid)
    two.other, branch_two_turned = tie(two.other, branch_two_turned)
    came_two = two.swap()
    one = Scatter(*down_grads(place, grid, branch_two_turned, hidden, context_turned, branch_one, gain_grads), grid)
    came_two, one.other, grad_context = tie(came_two, one.other, grad_context)
    two.put(came_two)
    came_two = two.go()
    came = one.swap()
    grads = backward(grad_context, context, lse, 0, pairs // 2, ())
    came_two, came, grad_context, grads = tie(came_two, came, grad_context, grads)
    two.put(came_two)
    one.put(came)
    came_two = two.go()
    came = one.go()
    grads = backward(grad_context, context, lse, pairs // 2, pairs // 2, grads)
    came_two, came, x_turned, grads = tie(came_two, came, x_turned, grads)
    two.put(came_two)
    one.put(came)
    came_two = two.go()
    came = one.go()
    three = Scatter(*attention_grads(place, grid, x_turned, grads), grid)
    three.other, came_two, came, grad_first = tie(three.other, came_two, came, grad_first)
    came_three = three.swap()
    two.put(came_two)
    came_two = two.go()
    came_three, came, grad_first = tie(came_three, came, grad_first)
    three.put(came_three)
    came_three = three.go()
    one.put(came)
    came = one.go()
    input_grad = input_gradient(grad_first, grads, w_query, w_key, w_value)
    came_three, came_two, input_grad = tie(came_three, came_two, input_grad)
    three.put(came_three)
    came_three = three.go()
    two.put(came_two)
    two_mine = two.mine()
    two_theirs = other_core(two_mine)
    came_three, came, two_theirs = tie(came_three, came, two_theirs)
    three.put(came_three)
    came_three = three.go()
    one.put(came)
    came = one.go()
    gate_out, up_out = finish(
        finish_two_body, "finish_two", place, two_mine, two_theirs, [gate_weight.shape, up_weight.shape]
    )
    came_three, came, gate_out = tie(came_three, came, gate_out)
    three.put(came_three)
    came_three = three.go()
    one.put(came)
    one_mine = one.mine()
    one_theirs = other_core(one_mine)
    down_out, output_out, gain_out = finish(
        finish_one_body, "finish_one", place, one_mine, one_theirs, [gate_weight.shape, output_weight.shape, (8, LANES)]
    )
    came_three, down_out, gain_out = tie(came_three, down_out, gain_out)
    three.put(came_three)
    three_mine = three.mine()
    share = first_gain.shape[0]
    three_theirs = other_core(three_mine)
    gain_one_out, gain_two_out = gain_out[0, :share], gain_out[1, :share]
    three_theirs, gain_one_out, gain_two_out = tie(three_theirs, gain_one_out, gain_two_out)
    query_out, key_out, value_out = finish(
        finish_three_body, "finish_three", place, three_mine, three_theirs, [query_weight.shape] * 3
    )
    return (
        layer_out, input_grad, query_out, key_out, value_out, output_out, gate_out, up_out, down_out.T, gain_one_out, gain_two_out,
    )


def solution(mesh):
    tokens = P(("dp", "row", "col"), None)
    block = P("row", "col")
    gain = P(("row", "col"))
    return jax.shard_map(
        on_device,
        mesh=mesh,
        in_specs=(tokens, P(("dp", "row", "col"))) + (block,) * 7 + (gain, gain, tokens),
        out_specs=(tokens, tokens) + (block,) * 7 + (gain, gain),
        check_vma=False,
    )
```

```python
import jax
import jax.numpy as jnp
from jax import lax
from jax.experimental import pallas as pl
from jax.experimental.pallas import tpu as pltpu
from jax.sharding import PartitionSpec as P

HEAD_DIM = 64
EPSILON = 1e-06
ROPE_BASE = 10000.0
NEGATIVE = -1e30
LOG2E = 1.4426950408889634
QUERY_BLOCK = 256
LANES = 128
BF16 = jnp.bfloat16
F32 = jnp.float32
EVERYWHERE = ("dp", "row", "col")


def costs(microseconds):
    return pl.CostEstimate(flops=int(microseconds * 1e7), bytes_accessed=int(microseconds * 1e4), transcendentals=0)


def dot_nn(left, right):
    return lax.dot_general(left, right, (((1,), (0,)), ((), ())), preferred_element_type=F32)


def dot_nt(left, right):
    return lax.dot_general(left, right, (((1,), (1,)), ((), ())), preferred_element_type=F32)


def bit_count(size):
    return size.bit_length() - 1


def bit_order(grid_rows, grid_cols, core):
    col_bits = [("col", b) for b in range(bit_count(grid_cols))]
    row_bits = [("row", b) for b in range(bit_count(grid_rows))]
    return (col_bits[::-1] + row_bits[::-1]) if core else (col_bits + row_bits)


def step_pairs(grid_rows, grid_cols, step):
    pairs = []
    for core in range(2):
        axis, bit = bit_order(grid_rows, grid_cols, core)[step]
        for row in range(grid_rows):
            for col in range(grid_cols):
                to_row = row ^ (1 << bit) if axis == "row" else row
                to_col = col ^ (1 << bit) if axis == "col" else col
                source = (core * grid_rows + row) * grid_cols + col
                target = (core * grid_rows + to_row) * grid_cols + to_col
                pairs.append((source, target))
    return pairs


def other_core(value):
    return lax.ppermute(value, "dp", [(0, 1), (1, 0)])


def exchange(value, grid, step):
    return lax.ppermute(value, EVERYWHERE, step_pairs(*grid, step))


def tie(*values):
    return lax.optimization_barrier(values)


def sum_blocks_body(shape, *refs):
    parts, came = shape
    out = refs[-1]
    came_refs = refs[len(refs) - 1 - came : -1]
    at = begin = 0
    for count in parts:
        end = begin + refs[at].shape[2]
        total = sum(ref[...].astype(F32) for ref in refs[at : at + count])
        for ref in came_refs:
            total = total + ref[:, :, begin:end, :].astype(F32)
        out[:, :, begin:end, :] = total.astype(BF16)
        at += count
        begin = end


class Scatter:
    def __init__(self, grid):
        self.grid = grid
        self.parts = []
        self.came = []

    def add(self, *terms):
        self.parts.append(list(terms))

    def put(self, came, origin=(0, 0)):
        self.came.append((came, origin))

    def terms(self, start, size):
        came = []
        for value, origin in self.came:
            inside = [o <= a and a + n <= o + m for o, a, n, m in zip(origin, start, size, value.shape)]
            apart = [a + n <= o or o + m <= a for o, a, n, m in zip(origin, start, size, value.shape)]
            assert all(inside) or any(apart)
            if all(inside):
                came.append((value, origin))
        return [(term, (0, 0)) for part in self.parts for term in part], came

    def sums(self, start, size):
        height = sum(part[0].shape[2] for part in self.parts)
        width = self.parts[0][0].shape[3]
        parts, came = self.terms(start, size)
        terms = parts + came
        if len(self.parts) == 1:
            values = []
            for term, origin in terms:
                begin = [a - o for a, o in zip(start, origin)]
                values.append(term[begin[0] : begin[0] + size[0], begin[1] : begin[1] + size[1]])
            if len(values) == 2:
                return values[0] + values[1]
            return sum(value.astype(F32) for value in values).astype(BF16)
        axis = 0 if size[0] > 1 else 1
        count = 2 if size[axis] > 1 else 1
        block = list(size)
        block[axis] //= count

        def spec(rows, begin):
            first = begin[0] // block[0], begin[1] // block[1]
            step = (lambda i: (first[0] + i, first[1], 0, 0)) if axis == 0 else (lambda i: (first[0], first[1] + i, 0, 0))
            return pl.BlockSpec((block[0], block[1], rows, width), step)

        return pl.pallas_call(
            lambda *refs: sum_blocks_body(([len(part) for part in self.parts], len(came)), *refs),
            grid=(count,),
            in_specs=[spec(term.shape[2], [a - o for a, o in zip(start, origin)]) for term, origin in terms],
            out_specs=spec(height, (0, 0)),
            out_shape=jax.ShapeDtypeStruct((size[0], size[1], height, width), BF16),
            cost_estimate=costs(2),
            name="sum_blocks",
        )(*[term for term, _ in terms])

    def send(self, value, step):
        return exchange(value, self.grid, step)


def last_sums_body(shapes, *refs):
    out = refs[-1]
    at = top = 0
    for parts, came in shapes:
        count = sum(parts) + came
        group = refs[at : at + count]
        height = sum(group[sum(parts[:k])].shape[2] for k in range(len(parts)))
        width = group[0].shape[3]
        begin = first = 0
        for n in parts:
            end = begin + group[first].shape[2]
            total = sum(ref[0, 0].astype(F32) for ref in group[first : first + n])
            for ref in group[count - came :]:
                total = total + ref[0, 0, begin:end, :].astype(F32)
            out[top + begin : top + end, 0:width] = total.astype(BF16)
            first += n
            begin = end
        top += height
        at += count


def last_sums(scatters):
    shapes, terms, height, width = [], [], 0, 0
    for scatter in scatters:
        parts, came = scatter.terms([0, 0], [1, 1])
        shapes.append(([len(part) for part in scatter.parts], len(came)))
        terms += parts + came
        height += sum(part[0].shape[2] for part in scatter.parts)
        width = max(width, scatter.parts[0][0].shape[3])

    def spec(term, origin):
        return pl.BlockSpec((1, 1, *term.shape[2:]), lambda i: (-origin[0], -origin[1], 0, 0))

    return pl.pallas_call(
        lambda *refs: last_sums_body(shapes, *refs),
        grid=(1,),
        in_specs=[spec(*term) for term in terms],
        out_specs=pl.BlockSpec((height, width), lambda i: (0, 0)),
        out_shape=jax.ShapeDtypeStruct((height, width), BF16),
        cost_estimate=costs(2),
        name="last_sums",
    )(*[term for term, _ in terms])


def reversed_bits(value, bits):
    out = 0
    for b in range(bits):
        out = out | (((value >> b) & 1) << (bits - 1 - b))
    return out


def place_of(row, col, place, core, grid_rows, grid_cols):
    far_row = row ^ place[0]
    far_col = col ^ place[1]
    row_bits = bit_count(grid_rows)
    col_bits = bit_count(grid_cols)
    plain = far_col + far_row * grid_cols
    turned = reversed_bits(far_col, col_bits) + reversed_bits(far_row, row_bits) * grid_cols
    return jnp.where(core == 0, plain, turned)


def unpack_pair(packed, odd):
    firsts = []
    for k in range(2):
        body = packed[:, 128 * k : 128 * (k + 1)]
        rest_low, rest_high = packed[:, 256:320], packed[:, 320:384]
        in_order, turned = (rest_low, rest_high) if k == 0 else (rest_high, rest_low)
        plain = jnp.concatenate([body, in_order], axis=1)
        other = jnp.concatenate([turned, body], axis=1)
        firsts.append(jnp.where(odd, other, plain))
    return firsts


def by_core(place, mine, theirs):
    mine, theirs = mine.astype(F32), theirs.astype(F32)
    first = place[2] == 0
    return jnp.where(first, mine, theirs), jnp.where(first, theirs, mine)


def finish_body(place, mine, theirs, query, key, value, output, gate, up, down, gain_one, gain_two):
    half = down.shape[0] // 2
    quarter = half // 2
    share = gain_one.shape[0]
    odd = (place[1] & 1) == 1
    halves = by_core(place, mine[...], theirs[...])
    for core, part in enumerate(halves):
        rows = slice(core * half, (core + 1) * half)
        for k, out in enumerate((gate, up, down)):
            out[rows, :] = part[k * half : (k + 1) * half]
        low = 3 * half + quarter
        query[rows, :], key[rows, :] = unpack_pair(part[low : low + half, :384], odd)
        for out, begin in ((output, 3 * half), (value, low + half)):
            for k, block in enumerate(unpack_pair(part[begin : begin + quarter, :384], odd)):
                out[core * half + k * quarter : core * half + (k + 1) * quarter, :] = block
    gains = halves[0][3 * half : 3 * half + 8, 384:512]
    gain_one[...] = gains[0, :share]
    gain_two[...] = gains[1, :share]


def finish(place, mine, theirs, shapes):
    vmem = pl.BlockSpec(memory_space=pltpu.VMEM)
    return pl.pallas_call(
        finish_body,
        in_specs=[pl.BlockSpec(memory_space=pltpu.SMEM)] + [vmem] * 2,
        out_specs=[vmem] * len(shapes),
        out_shape=[jax.ShapeDtypeStruct(shape, F32) for shape in shapes],
        cost_estimate=costs(1),
        name="finish",
    )(place, mine, theirs)


def pack_pair(first, second, odd, out, rows):
    rolled = [jnp.concatenate([v[:, 64:], v[:, :64]], axis=1) for v in (first, second)]
    bodies = [jnp.where(odd, r[:, :128], v[:, :128]) for r, v in zip(rolled, (first, second))]
    rests = [jnp.where(odd, v[:, :64], v[:, 128:]) for v in (first, second)]
    low = jnp.where(odd, rests[1], rests[0])
    high = jnp.where(odd, rests[0], rests[1])
    out[rows, 0:128] = bodies[0].astype(BF16)
    out[rows, 128:256] = bodies[1].astype(BF16)
    out[rows, 256:384] = jnp.concatenate([low, high], axis=1).astype(BF16)


def pack_attention_body(place, query, key, value, out):
    half = query.shape[0] // 2
    quarter = half // 2
    odd = (place[1] & 1) == 1
    base = place[2] * half
    query, key = (w[pl.ds(pl.multiple_of(base, half), half), :].astype(F32) for w in (query, key))
    pack_pair(query, key, odd, out, slice(0, half))
    value = value[pl.ds(pl.multiple_of(base, half), half), :].astype(F32)
    pack_pair(value[:quarter], value[quarter:], odd, out, slice(half, half + quarter))


def pack_attention(place, query, key, value):
    half = query.shape[0] // 2
    vmem = pl.BlockSpec(memory_space=pltpu.VMEM)
    return pl.pallas_call(
        pack_attention_body,
        in_specs=[pl.BlockSpec(memory_space=pltpu.SMEM)] + [vmem] * 3,
        out_specs=vmem,
        out_shape=jax.ShapeDtypeStruct((half + half // 2, 384), BF16),
        cost_estimate=costs(2),
        name="pack_attention",
    )(place, query, key, value)


def pack_feed_body(place, gate, up, down, output, gain_one, gain_two, out):
    half = gate.shape[0] // 2
    quarter = half // 2
    odd = (place[1] & 1) == 1
    rows = pl.ds(pl.multiple_of(place[2] * half, half), half)
    out[0:half, :] = gate[rows, :]
    out[half : 2 * half, :] = up[rows, :]
    out[2 * half + quarter : 3 * half + quarter, :] = down[rows, :]
    output = output[rows, :].astype(F32)
    low = slice(2 * half, 2 * half + quarter)
    pack_pair(output[:quarter], output[quarter:], odd, out, low)
    share = gain_one.shape[1]
    gains = jnp.concatenate([gain_one[...].astype(F32), gain_two[...].astype(F32)], axis=0)
    gains = jnp.concatenate([gains, jnp.zeros((2, LANES - share), F32)], axis=1)
    gains = jnp.concatenate([gains, jnp.zeros((quarter - 2, LANES), F32)], axis=0)
    out[low, 384:512] = gains.astype(BF16)


def pack_feed(place, gate, up, down_turned, output, gain_one, gain_two):
    half = gate.shape[0] // 2
    vmem = pl.BlockSpec(memory_space=pltpu.VMEM)
    return pl.pallas_call(
        pack_feed_body,
        in_specs=[pl.BlockSpec(memory_space=pltpu.SMEM)] + [vmem] * 6,
        out_specs=vmem,
        out_shape=jax.ShapeDtypeStruct((3 * half + half // 2, gate.shape[1]), BF16),
        cost_estimate=costs(2),
        name="pack_feed",
    )(place, gate, up, down_turned, output, gain_one[None], gain_two[None])


def place_scalars():
    return jnp.stack([lax.axis_index("row"), lax.axis_index("col"), lax.axis_index("dp")]).astype(jnp.int32)


def split_rows(top):
    return lax.broadcasted_iota(jnp.int32, top, 1) < 64


def fill_columns(target, rows, low_even, body_even, low_odd, body_odd, pair, swapped):
    base = 384 * pair
    target[rows, base : base + 128] = body_even
    target[rows, base + 256 : base + 384] = body_odd
    first = split_rows(low_even.shape)
    if swapped:
        mixed = jnp.where(first, low_odd, low_even)
        target[rows, base + 128 : base + 256] = pltpu.roll(mixed.astype(F32), 64, 1).astype(BF16)
    else:
        target[rows, base + 128 : base + 256] = jnp.where(first, low_even, low_odd)


def piece_places(pieces):
    counts = [p.shape[0] for p in pieces]
    out = []
    for side in range(2):
        at = 0
        for count in counts[side * len(counts) // 2 : (side + 1) * len(counts) // 2]:
            out.append((side, at, count))
            at += count
    return out


def load_stacks(pieces, held, sems):
    copies = []
    for k, (piece, (side, at, count)) in enumerate(zip(pieces, piece_places(pieces))):
        copies.append(pltpu.make_async_copy(piece, held.at[side, pl.ds(at, count)], sems.at[k]))
    for copy in copies:
        copy.start()
    for copy in copies:
        copy.wait()


def assemble_attention(grid, place, held, w_query, w_key, w_value):
    grid_rows, grid_cols = grid
    where = (place[0], place[1])
    half = w_query.shape[0] // grid_rows // 2
    quarter = half // 2
    for core in range(2):
        side = core ^ place[2]
        for row in range(grid_rows):
            start = row * 2 * half + core * half
            for pair in range(grid_cols // 2):
                at = [place_of(row, 2 * pair + c, where, core, grid_rows, grid_cols) for c in range(2)]
                even, odd = (held.at[side, p] for p in at)
                top = slice(0, half)
                rows = slice(start, start + half)
                rest_even, rest_odd = even[top, 256:384], odd[top, 256:384]
                fill_columns(w_query, rows, rest_even, even[top, 0:128], rest_odd, odd[top, 0:128], pair, False)
                fill_columns(w_key, rows, rest_even, even[top, 128:256], rest_odd, odd[top, 128:256], pair, True)
                low = slice(half, half + quarter)
                rest_even, rest_odd = even[low, 256:384], odd[low, 256:384]
                rows = slice(start, start + quarter)
                fill_columns(w_value, rows, rest_even, even[low, 0:128], rest_odd, odd[low, 0:128], pair, False)
                rows = slice(start + quarter, start + half)
                fill_columns(w_value, rows, rest_even, even[low, 128:256], rest_odd, odd[low, 128:256], pair, True)


def assemble_output(grid, place, held, w_output, gains):
    grid_rows, grid_cols = grid
    where = (place[0], place[1])
    half = w_output.shape[0] // grid_rows // 2
    quarter = half // 2
    width = gains.shape[1]
    share = width // (grid_rows * grid_cols)
    lane = lax.broadcasted_iota(jnp.int32, (LANES, width), 1)
    spread = (lax.rem(lane, share) == lax.broadcasted_iota(jnp.int32, (LANES, width), 0)).astype(BF16)
    block_of = lax.div(lax.broadcasted_iota(jnp.int32, (16, width), 1), share)
    total = jnp.zeros((16, width), F32)
    every = slice(0, quarter)
    for core in range(2):
        side = core ^ place[2]
        for row in range(grid_rows):
            start = row * 2 * half + core * half
            for pair in range(grid_cols // 2):
                at = [place_of(row, 2 * pair + c, where, core, grid_rows, grid_cols) for c in range(2)]
                even, odd = (held.at[side, p] for p in at)
                rest_even, rest_odd = even[every, 256:384], odd[every, 256:384]
                rows = slice(start, start + quarter)
                fill_columns(w_output, rows, rest_even, even[every, 0:128], rest_odd, odd[every, 0:128], pair, False)
                rows = slice(start + quarter, start + half)
                fill_columns(w_output, rows, rest_even, even[every, 128:256], rest_odd, odd[every, 128:256], pair, True)
                if core == 0:
                    for c, block in enumerate((even, odd)):
                        spreaded = dot_nn(block[0:16, 384:512], spread)
                        total = total + jnp.where(block_of == row * grid_cols + 2 * pair + c, spreaded, 0.0)
    gains[...] = total[:8]


def block_at(position, place, core, grid):
    grid_rows, grid_cols = grid
    far_row, far_col = position // grid_cols, position % grid_cols
    turned_row, turned_col = reversed_bits(far_row, bit_count(grid_rows)), reversed_bits(far_col, bit_count(grid_cols))
    first = core == 0
    return jnp.where(first, far_row, turned_row) ^ place[0], jnp.where(first, far_col, turned_col) ^ place[1]


def start_feed_copies(grid, place, pieces, w_gate, w_up, w_down, held, sems):
    grid_rows, grid_cols = grid
    half = w_gate.shape[0] // grid_rows // 2
    quarter = half // 2
    span = w_gate.shape[1] // grid_cols
    for piece, (side, at, count) in zip(pieces, piece_places(pieces)):
        core = side ^ place[2]

        @pl.loop(0, count)
        def _(n):
            row, col = block_at(at + n, place, core, grid)
            block = piece.at[n]
            rows = pl.ds(pl.multiple_of((2 * row + core) * half, half), half)
            lanes = pl.ds(pl.multiple_of(col * span, span), span)
            turned_rows = pl.ds(pl.multiple_of((2 * col + core) * half, half), half)
            turned_lanes = pl.ds(pl.multiple_of(row * span, span), span)
            parts = (
                (0, 2 * half, quarter, held.at[side, at + n]),
                (1, 0, half, w_gate.at[rows, lanes]),
                (2, half, half, w_up.at[rows, lanes]),
                (3, 2 * half + quarter, half, w_down.at[turned_rows, turned_lanes]),
            )
            for k, start, size, target in parts:
                pltpu.make_async_copy(block.at[pl.ds(start, size)], target, sems.at[k]).start()


def swap_halves(values):
    lane = lax.broadcasted_iota(jnp.int32, values.shape, 1)
    back = pltpu.roll(values, 32, 1)
    ahead = pltpu.roll(values, LANES - 32, 1)
    return jnp.where(lax.rem(lane, HEAD_DIM) < HEAD_DIM // 2, ahead, back)


def project_tile(x, w_query, w_key, w_value, cosine, sine, query, key, value):
    width = w_query.shape[1]
    step = 256
    for start in range(0, width, step):
        for weight, out in ((w_query, query), (w_key, key)):
            flat = dot_nn(x[...], weight[:, start : start + step])
            for k in range(step // LANES):
                part = flat[:, k * LANES : (k + 1) * LANES]
                turned = part * cosine[...] + swap_halves(part) * sine[...]
                out[:, start + k * LANES : start + (k + 1) * LANES] = turned.astype(BF16)
        value[:, start : start + step] = dot_nn(x[...], w_value[:, start : start + step]).astype(BF16)


def project_blocks_body(grid, count, place, *refs):
    pieces, refs = refs[:count], refs[count:]
    x, cosine, sine, query, key, value, w_query, w_key, w_value, held, sems = refs

    @pl.when(pl.program_id(0) == 0)
    def _():
        load_stacks(pieces, held, sems)
        assemble_attention(grid, place, held, w_query, w_key, w_value)

    project_tile(x, w_query, w_key, w_value, cosine, sine, query, key, value)


def project_blocks(pieces, place, grid, x, cosine, sine):
    tokens, width = x.shape
    _, height, lanes = pieces[0].shape
    rows = 256
    tile = pl.BlockSpec((rows, width), lambda i: (i, 0))
    table = pl.BlockSpec((rows, LANES), lambda i: (i, 0))
    whole = pl.BlockSpec((width, width), lambda i: (0, 0), pipeline_mode=pl.Buffered(1))
    anywhere = pl.BlockSpec(memory_space=pl.ANY)
    return pl.pallas_call(
        lambda *refs: project_blocks_body(grid, len(pieces), *refs),
        grid=(tokens // rows,),
        in_specs=[pl.BlockSpec(memory_space=pltpu.SMEM)] + [anywhere] * len(pieces) + [tile, table, table],
        out_specs=[tile] * 3 + [whole] * 3,
        out_shape=[jax.ShapeDtypeStruct((tokens, width), BF16)] * 3 + [jax.ShapeDtypeStruct((width, width), BF16)] * 3,
        scratch_shapes=[
            pltpu.VMEM((2, grid[0] * grid[1], height, lanes), BF16),
            pltpu.SemaphoreType.DMA((len(pieces),)),
        ],
        cost_estimate=costs(10),
        name="project_heads",
    )(place, *pieces, x, cosine, sine)


def project(x, w_query, w_key, w_value, cosine, sine):
    tokens, width = x.shape
    rows = 256
    tile = pl.BlockSpec((rows, width), lambda i: (i, 0))
    table = pl.BlockSpec((rows, LANES), lambda i: (i, 0))
    whole = pl.BlockSpec((width, width), lambda i: (0, 0))
    return pl.pallas_call(
        project_tile,
        grid=(tokens // rows,),
        in_specs=[tile, whole, whole, whole, table, table],
        out_specs=[tile] * 3,
        out_shape=[jax.ShapeDtypeStruct((tokens, width), BF16)] * 3,
        name="project_heads_plain",
    )(x, w_query, w_key, w_value, cosine, sine)


def own_half(values, h):
    zero = jnp.zeros_like(values)
    return jnp.concatenate([values, zero] if h == 0 else [zero, values], axis=0)


def attention_forward_body(first, q_ref, k_ref, v_ref, context_ref, lse_ref):
    q_turned = (q_ref[...].astype(F32) * HEAD_DIM**-0.5).T.astype(BF16)
    v_turned = v_ref[...].T
    square = (LANES, LANES)
    causal = lax.broadcasted_iota(jnp.int32, square, 0) <= lax.broadcasted_iota(jnp.int32, square, 1)
    lse_ref[...] = jnp.zeros_like(lse_ref)
    for t in range(q_ref.shape[0] // LANES):
        now = slice(t * LANES, (t + 1) * LANES)
        begin = first[t * LANES // QUERY_BLOCK]
        outs = []
        for h in range(2):
            head = slice(h * HEAD_DIM, (h + 1) * HEAD_DIM)
            mine = own_half(q_turned[head, now], h)
            for b in [t, *range(t)]:
                there = slice(b * LANES, (b + 1) * LANES)
                scores = dot_nn(k_ref[there, :], mine)
                if b == t:
                    scores = jnp.where(causal, scores, NEGATIVE)
                block_top = jnp.max(scores, axis=0, keepdims=True) * LOG2E
                if b == t:
                    new_top = base = block_top
                else:
                    seen = begin <= b * LANES // QUERY_BLOCK
                    new_top = jnp.maximum(top, jnp.where(seen, block_top, NEGATIVE))
                    base = new_top + jnp.where(seen, 0.0, -NEGATIVE)
                weights = jnp.exp2(scores * LOG2E - base)
                part_total = jnp.sum(weights, axis=0, keepdims=True)
                part = dot_nn(v_turned[head, there], weights.astype(BF16))
                if b == t:
                    total, mixed = part_total, part
                else:
                    shrink = jnp.exp2(top - new_top)
                    total = total * shrink + part_total
                    mixed = mixed * shrink + part
                top = new_top
            outs.append(mixed * (1.0 / total))
            lse_ref[0, h : h + 1, now] = top + jnp.log2(total)
        context_ref[now, :] = jnp.concatenate(outs, axis=0).T.astype(BF16)


def attention_forward(first, query, key, value, begin, pairs):
    tokens = query.shape[0]
    spec = pl.BlockSpec((tokens, LANES), lambda j, f: (0, j + begin))
    part = pl.BlockSpec((tokens, LANES), lambda j, f: (0, j))
    return pl.pallas_call(
        attention_forward_body,
        grid_spec=pltpu.PrefetchScalarGridSpec(
            num_scalar_prefetch=1,
            grid=(pairs,),
            in_specs=[spec] * 3,
            out_specs=[part, pl.BlockSpec((1, 8, tokens), lambda j, f: (j, 0, 0))],
        ),
        out_shape=[
            jax.ShapeDtypeStruct((tokens, pairs * LANES), BF16),
            jax.ShapeDtypeStruct((pairs, 8, tokens), F32),
        ],
        cost_estimate=costs(4 * pairs),
        name="attention_forward",
    )(first, query, key, value)


def attention_backward_body(first, q_ref, k_ref, v_ref, grad_ref, context_ref, lse_ref, cosine, sine, *refs):
    dq_ref, dk_ref, dv_ref, dk_sum, dv_sum = refs[-5:]
    blocks = q_ref.shape[0] // QUERY_BLOCK
    scaled = q_ref[...].astype(F32) * HEAD_DIM**-0.5
    q_turned = scaled.T.astype(BF16)
    q_plain = scaled.astype(BF16)
    k_turned = k_ref[...].T
    grad = grad_ref[...]
    grad_turned = grad.T
    inner = (grad.astype(F32) * context_ref[...].astype(F32)).T
    square = (QUERY_BLOCK, QUERY_BLOCK)
    causal = lax.broadcasted_iota(jnp.int32, square, 0) <= lax.broadcasted_iota(jnp.int32, square, 1)
    low_lanes = lax.broadcasted_iota(jnp.int32, (QUERY_BLOCK, LANES), 1) < HEAD_DIM
    for i in reversed(range(blocks)):
        now = slice(i * QUERY_BLOCK, (i + 1) * QUERY_BLOCK)
        seen = slice(0, (i + 1) * QUERY_BLOCK)
        grads = []
        for h in range(2):
            head = slice(h * HEAD_DIM, (h + 1) * HEAD_DIM)
            own_lanes = low_lanes if h == 0 else jnp.logical_not(low_lanes)
            q_rows = jnp.where(own_lanes, q_plain[now, :], 0)
            g_rows = jnp.where(own_lanes, grad[now, :], 0)
            delta = jnp.sum(inner[head, now], axis=0, keepdims=True)
            lse = lse_ref[0, h : h + 1, now]
            scores = dot_nn(k_ref[seen, :], own_half(q_turned[head, now], h))
            grad_probs = dot_nn(v_ref[seen, :], own_half(grad_turned[head, now], h))
            probs, grad_scores = [], []
            for b in range(i + 1):
                there = slice(b * QUERY_BLOCK, (b + 1) * QUERY_BLOCK)
                part = scores[there]
                base = lse if b == i else lse + jnp.where(first[i] <= b, 0.0, -NEGATIVE)
                if b == i:
                    part = jnp.where(causal, part, NEGATIVE)
                part = jnp.exp2(part * LOG2E - base)
                probs.append(part.astype(BF16))
                grad_scores.append((part * (grad_probs[there] - delta)).astype(BF16))
            probs, grad_scores = jnp.concatenate(probs, axis=0), jnp.concatenate(grad_scores, axis=0)
            dv, dk = dot_nn(probs, g_rows), dot_nn(grad_scores, q_rows)
            if i == blocks - 1 and h == 0:
                dv_sum[...] = dv
                dk_sum[...] = dk
            else:
                dv_sum[seen, :] += dv
                dk_sum[seen, :] += dk
            grads.append(dot_nn(k_turned[head, seen], grad_scores) * HEAD_DIM**-0.5)
        dq = jnp.concatenate(grads, axis=0).T
        dq_ref[now, :] = (dq * cosine[now, :] - swap_halves(dq) * sine[now, :]).astype(BF16)
    dk = dk_sum[...]
    dk_ref[...] = (dk * cosine[...] - swap_halves(dk) * sine[...]).astype(BF16)
    dv_ref[...] = dv_sum[...].astype(BF16)


def attention_backward(first, query, key, value, grad, context, lse, cosine, sine, begin, pairs, into):
    tokens, width = query.shape
    spec = pl.BlockSpec((tokens, LANES), lambda j, f: (0, j + begin))
    table = pl.BlockSpec((tokens, LANES), lambda j, f: (0, 0))
    anywhere = pl.BlockSpec(memory_space=pl.ANY)
    return pl.pallas_call(
        attention_backward_body,
        grid_spec=pltpu.PrefetchScalarGridSpec(
            num_scalar_prefetch=1,
            grid=(pairs,),
            in_specs=[spec] * 5
            + [pl.BlockSpec((1, 8, tokens), lambda j, f: (j + begin, 0, 0)), table, table]
            + [anywhere] * len(into),
            out_specs=[spec] * 3,
            scratch_shapes=[pltpu.VMEM((tokens, LANES), F32)] * 2,
        ),
        out_shape=[jax.ShapeDtypeStruct((tokens, width), BF16)] * 3,
        input_output_aliases={9 + k: k for k in range(len(into))},
        cost_estimate=costs(6 * pairs),
        name="attention_backward",
    )(first, query, key, value, grad, context, lse, cosine, sine, *into)


def middle_tile(
    contexts, x, cotangent, w_output, w_gate, w_up, w_down, gains, ready,
    layer_out, hidden_in_turned, branch_two_turned, context_turned, hidden, grad_gate, grad_up, grad_first, branch_one, grad_context, gain_grads,
    slope, act,
):
    width = x.shape[1]
    span = w_gate.shape[1]
    chunk = 512
    ready(0)
    gain_one = gains[0:1, :]
    gain_two = gains[1:2, :]
    context_now = jnp.concatenate([part[...] for part in contexts], axis=1)
    first_sum = x[...].astype(F32) + dot_nn(context_now, w_output[...])
    scale_one = lax.rsqrt(jnp.mean(first_sum * first_sum, axis=1, keepdims=True) + EPSILON)
    normed_one = first_sum * scale_one
    normed = normed_one * gain_one
    hidden_in = normed.astype(BF16)
    second_sum = normed
    ready(1)
    for start in range(0, span, chunk):
        cols = slice(start, start + chunk)
        gate_act = dot_nn(hidden_in, w_gate[:, cols])
        up_act = dot_nn(hidden_in, w_up[:, cols])
        sigmoid = jax.nn.sigmoid(gate_act)
        silu = gate_act * sigmoid
        act[:, cols] = silu
        slope[:, cols] = up_act * (sigmoid + silu * (1.0 - sigmoid))
        hidden_now = (silu * up_act).astype(BF16)
        hidden[:, cols] = hidden_now
        if start == 0:
            ready(2)
        second_sum = second_sum + dot_nt(hidden_now, w_down[:, cols])
    scale_two = lax.rsqrt(jnp.mean(second_sum * second_sum, axis=1, keepdims=True) + EPSILON)
    normed_two = second_sum * scale_two
    layer_out[...] = (normed_two * gain_two).astype(BF16)
    grad_out = cotangent[...].astype(F32)
    two_term = jnp.sum(grad_out * normed_two, axis=0, keepdims=True)
    scaled = grad_out * gain_two
    grad_second = scale_two * (scaled - normed_two * jnp.mean(scaled * normed_two, axis=1, keepdims=True))
    branch_two = grad_second.astype(BF16)
    grad_normed = grad_second
    for start in range(0, span, chunk):
        cols = slice(start, start + chunk)
        grad_hidden = dot_nn(branch_two, w_down[:, cols])
        gate_now = (grad_hidden * slope[:, cols]).astype(BF16)
        up_now = (grad_hidden * act[:, cols]).astype(BF16)
        grad_gate[:, cols] = gate_now
        grad_up[:, cols] = up_now
        grad_normed = grad_normed + dot_nt(gate_now, w_gate[:, cols]) + dot_nt(up_now, w_up[:, cols])
    one_term = jnp.sum(grad_normed * normed_one, axis=0, keepdims=True)
    scaled = grad_normed * gain_one
    first_grad = scale_one * (scaled - normed_one * jnp.mean(scaled * normed_one, axis=1, keepdims=True))
    grad_first[...] = first_grad
    one_now = first_grad.astype(BF16)
    branch_one[...] = one_now
    grad_context[...] = dot_nt(one_now, w_output[...]).astype(BF16)
    hidden_in_turned[...] = hidden_in.T
    branch_two_turned[...] = branch_two.T
    context_turned[...] = context_now.T
    terms = jnp.concatenate([one_term, two_term, jnp.zeros((6, width), F32)], axis=0)

    @pl.when(pl.program_id(0) == 0)
    def _():
        gain_grads[...] = terms

    @pl.when(pl.program_id(0) > 0)
    def _():
        gain_grads[...] += terms


def middle_specs(tokens, width, span, rows):
    tile = pl.BlockSpec((rows, width), lambda i: (i, 0))
    wide = pl.BlockSpec((rows, span), lambda i: (i, 0))
    turned = pl.BlockSpec((width, rows), lambda i: (0, i))
    eight = pl.BlockSpec((8, width), lambda i: (0, 0))
    flat = jax.ShapeDtypeStruct((tokens, width), BF16)
    flat_turned = jax.ShapeDtypeStruct((width, tokens), BF16)
    broad = jax.ShapeDtypeStruct((tokens, span), BF16)
    return (
        [tile, turned, turned, turned, wide, wide, wide, tile, tile, tile, eight],
        [
            flat, flat_turned, flat_turned, flat_turned, broad, broad, broad,
            jax.ShapeDtypeStruct((tokens, width), F32), flat, flat, jax.ShapeDtypeStruct((8, width), F32),
        ],
    )


def middle_plain_body(context, x, cotangent, w_output, w_gate, w_up, w_down, gains, *rest):
    middle_tile((context,), x, cotangent, w_output, w_gate, w_up, w_down, gains, lambda k: None, *rest)


def middle_plain(context, x, cotangent, w_output, w_gate, w_up, w_down, gains):
    tokens, width = x.shape
    span = w_gate.shape[1]
    rows = 256
    tile = pl.BlockSpec((rows, width), lambda i: (i, 0))
    square = pl.BlockSpec((width, width), lambda i: (0, 0), pipeline_mode=pl.Buffered(1))
    whole = pl.BlockSpec((width, span), lambda i: (0, 0), pipeline_mode=pl.Buffered(1))
    eight = pl.BlockSpec((8, width), lambda i: (0, 0))
    out_specs, out_shape = middle_specs(tokens, width, span, rows)
    return pl.pallas_call(
        middle_plain_body,
        grid=(tokens // rows,),
        in_specs=[tile, tile, tile, square, whole, whole, whole, eight],
        out_specs=out_specs,
        out_shape=out_shape,
        scratch_shapes=[pltpu.VMEM((rows, span), F32)] * 2,
        name="feed_forward_and_back_plain",
    )(context, x, cotangent, w_output, w_gate, w_up, w_down, gains)


def middle_body(grid, count, place, *refs):
    pieces, refs = refs[:count], refs[count:]
    context, x, cotangent = refs[:3]
    outs = refs[3:14]
    slope, act, w_output, w_gate, w_up, w_down, gains, held, sems = refs[14:]
    here = pl.program_id(0) == 0

    @pl.when(here)
    def _():
        start_feed_copies(grid, place, pieces, w_gate, w_up, w_down, held, sems)

    def ready(k):
        @pl.when(here)
        def _():
            for n, target in (((0, held),), ((1, w_gate), (2, w_up)), ((3, w_down),))[k]:
                pltpu.make_async_copy(target, target, sems.at[n]).wait()
            if k == 0:
                assemble_output(grid, place, held, w_output, gains)

    middle_tile((context,), x, cotangent, w_output, w_gate, w_up, w_down, gains, ready, *outs, slope, act)


def middle(pieces, place, grid, context, x, cotangent):
    tokens, width = x.shape
    _, height, lanes = pieces[0].shape
    span = lanes * grid[1]
    rows = 256
    tile = pl.BlockSpec((rows, width), lambda i: (i, 0))
    anywhere = pl.BlockSpec(memory_space=pl.ANY)
    out_specs, out_shape = middle_specs(tokens, width, span, rows)
    return pl.pallas_call(
        lambda *refs: middle_body(grid, len(pieces), *refs),
        grid=(tokens // rows,),
        in_specs=[pl.BlockSpec(memory_space=pltpu.SMEM)] + [anywhere] * len(pieces) + [tile] * 3,
        out_specs=out_specs,
        out_shape=out_shape,
        scratch_shapes=[pltpu.VMEM((rows, span), F32)] * 2
        + [pltpu.VMEM((width, width), BF16)]
        + [pltpu.VMEM((width, span), BF16)] * 3
        + [
            pltpu.VMEM((8, width), F32),
            pltpu.VMEM((2, grid[0] * grid[1], height // 7, lanes), BF16),
            pltpu.SemaphoreType.DMA((4,)),
        ],
        cost_estimate=costs(40),
        name="feed_forward_and_back",
    )(place, *pieces, context, x, cotangent)


def part_of(index, place_index, core, count):
    far = index ^ place_index
    return jnp.where(core == 0, far, reversed_bits(far, bit_count(count)))


def store_split(own, low, high, where, grid, core_here, row, col, rows, lanes, halves):
    here = core_here == 0
    at = part_of(row, where[0], core_here, grid[0]), part_of(col, where[1], core_here, grid[1])
    own[at[0], at[1], rows, lanes] = jnp.where(here, halves[0], halves[1])
    at = part_of(row, where[0], 1 - core_here, grid[0]), part_of(col, where[1], 1 - core_here, grid[1])
    value = jnp.where(here, halves[1], halves[0])
    edge = grid[0] // 2

    @pl.when(at[0] < edge)
    def _():
        low[at[0], at[1], rows, lanes] = value

    @pl.when(at[0] >= edge)
    def _():
        high[at[0] - edge, at[1], rows, lanes] = value


def rest_tile(first, second, odd):
    low = split_rows(first.shape)
    rolled = pltpu.roll(second, 64, 1)
    return jnp.where(low, rolled, first) if odd else jnp.where(low, first, rolled)


def feed_grads_body(grid, count, place, left, *refs):
    rights, (own, other) = refs[:count], refs[-2:]
    grid_rows, grid_cols = grid
    half = left.shape[0] // grid_rows // 2
    here = place[2] == 0
    for k, right in enumerate(rights):
        product = dot_nn(left[...], right[...]).astype(BF16)
        rows = slice(k * half, (k + 1) * half)
        for i in range(grid_rows):
            first, second = (product[(2 * i + c) * half : (2 * i + c + 1) * half] for c in range(2))
            mine, theirs = part_of(i, place[0], place[2], grid_rows), part_of(i, place[0], 1 - place[2], grid_rows)
            own[mine, 0, rows, :] = jnp.where(here, first, second)
            other[theirs, 0, rows, :] = jnp.where(here, second, first)


def feed_grads(place, grid, left, rights):
    width, tokens = left.shape
    grid_rows, grid_cols = grid
    span = rights[0].shape[1] // grid_cols
    half = width // grid_rows // 2
    count = len(rights)

    def out_index(flip):
        return lambda i, s: (0, part_of(i, s[1], s[2] ^ flip, grid_cols), 0, 0)

    shape = (grid_rows, grid_cols, half * count, span)
    return pl.pallas_call(
        lambda *refs: feed_grads_body(grid, count, *refs),
        grid_spec=pltpu.PrefetchScalarGridSpec(
            num_scalar_prefetch=1,
            grid=(grid_cols,),
            in_specs=[pl.BlockSpec((width, tokens), lambda i, s: (0, 0), pipeline_mode=pl.Buffered(1))]
            + [pl.BlockSpec((tokens, span), lambda i, s: (0, i))] * count,
            out_specs=[pl.BlockSpec((grid_rows, 1, half * count, span), out_index(f)) for f in range(2)],
        ),
        out_shape=[jax.ShapeDtypeStruct(shape, BF16)] * 2,
        cost_estimate=costs(7 * count),
        name="feed_forward_weight_grad",
    )(place, left, *rights)


def down_grads_body(grid, place, branch_two_turned, hidden, context_turned, branch_one, gain_grads, own, other):
    grid_rows, grid_cols = grid
    width = branch_two_turned.shape[0]
    half = width // grid_cols // 2
    quarter = half // 2
    here = place[2] == 0
    row = pl.program_id(0)
    down = dot_nn(branch_two_turned[...], hidden[...]).astype(BF16)
    output = dot_nn(context_turned[...], branch_one[...])
    share = width // (grid_rows * grid_cols)
    lane = lax.broadcasted_iota(jnp.int32, (width, LANES), 0)
    gather = (lax.rem(lane, share) == lax.broadcasted_iota(jnp.int32, (width, LANES), 1)).astype(BF16)
    block_of = lax.div(lax.broadcasted_iota(jnp.int32, (8, width), 1), share)
    low = slice(half, half + quarter)

    def store(mine, theirs, rows, lanes, halves):
        own[0, mine, rows, lanes] = jnp.where(here, halves[0], halves[1])
        other[0, theirs, rows, lanes] = jnp.where(here, halves[1], halves[0])

    for c in range(grid_cols):
        at = part_of(c, place[1], place[2], grid_cols), part_of(c, place[1], 1 - place[2], grid_cols)
        store(*at, slice(0, half), slice(0, down.shape[1]), [down[(2 * c + k) * half : (2 * c + k + 1) * half] for k in range(2)])
        tile = 384 * (c // 2)
        odd = c % 2
        body = slice(tile + 256 * odd, tile + 256 * odd + 128)
        mid = slice(tile + 128, tile + 256)
        tops, lows = ([slice(k * half + n * quarter, k * half + (n + 1) * quarter) for k in range(2)] for n in range(2))
        store(*at, low, slice(0, 128), [output[t, body].astype(BF16) for t in tops])
        store(*at, low, slice(128, 256), [output[t, body].astype(BF16) for t in lows])
        store(*at, low, slice(256, 384), [rest_tile(output[t, mid], output[l, mid], odd).astype(BF16) for t, l in zip(tops, lows)])
        picked = jnp.where(block_of == row * grid_cols + c, gain_grads[...], 0.0).astype(BF16)
        gain = dot_nn(picked, gather)
        gain = jnp.concatenate([gain, jnp.zeros((quarter - 8, LANES), F32)], axis=0).astype(BF16)
        store(*at, low, slice(384, 512), [gain, gain])


def down_grads(place, grid, branch_two_turned, hidden, context_turned, branch_one, gain_grads):
    width, tokens = branch_two_turned.shape
    grid_rows, grid_cols = grid
    span = hidden.shape[1] // grid_rows
    half = width // grid_cols // 2
    height = half + half // 2

    def out_index(flip):
        return lambda i, s: (part_of(i, s[0], s[2] ^ flip, grid_rows), 0, 0, 0)

    once = dict(pipeline_mode=pl.Buffered(1))
    own, other = pl.pallas_call(
        lambda *refs: down_grads_body(grid, *refs),
        grid_spec=pltpu.PrefetchScalarGridSpec(
            num_scalar_prefetch=1,
            grid=(grid_rows,),
            in_specs=[
                pl.BlockSpec((width, tokens), lambda i, s: (0, 0), **once),
                pl.BlockSpec((tokens, span), lambda i, s: (0, i)),
                pl.BlockSpec((width // grid_rows, tokens), lambda i, s: (i, 0)),
                pl.BlockSpec((tokens, width), lambda i, s: (0, 0), **once),
                pl.BlockSpec((8, width), lambda i, s: (0, 0)),
            ],
            out_specs=[pl.BlockSpec((1, grid_cols, height, span), out_index(f)) for f in range(2)],
        ),
        out_shape=[jax.ShapeDtypeStruct((grid_rows, grid_cols, height, span), BF16)] * 2,
        cost_estimate=costs(10),
        name="down_weight_grad",
    )(place, branch_two_turned, hidden, context_turned, branch_one, gain_grads)
    return own, other


def attention_grads_body(grid, place, x_turned, grad_query, grad_key, grad_value, own, lower, upper):
    grid_rows, grid_cols = grid
    where = (place[0], place[1])
    half = x_turned.shape[0] // grid_rows // 2
    quarter = half // 2
    pair = pl.program_id(0)
    query, key, value = (dot_nn(x_turned[...], g[...]) for g in (grad_query, grad_key, grad_value))
    mid = slice(128, 256)
    for row in range(grid_rows):
        for odd in range(2):
            body = slice(256 * odd, 256 * odd + 128)
            pieces = []
            for core in range(2):
                start = row * 2 * half + core * half
                rows = slice(start, start + half)
                top, low = slice(start, start + quarter), slice(start + quarter, start + half)
                joined = (query[rows, body], key[rows, body], rest_tile(query[rows, mid], key[rows, mid], odd))
                last = (value[top, body], value[low, body], rest_tile(value[top, mid], value[low, mid], odd))
                pieces.append([p.astype(BF16) for p in joined + last])
            for k in range(3):
                lanes = slice(128 * k, 128 * (k + 1))
                at = (row, 2 * pair + odd)
                for n, rows in ((k, slice(0, half)), (3 + k, slice(half, half + quarter))):
                    store_split(own, lower, upper, where, grid, place[2], *at, rows, lanes, [p[n] for p in pieces])


def attention_grads(place, grid, x_turned, grads):
    width, tokens = x_turned.shape
    grid_rows, grid_cols = grid
    half = width // grid_rows // 2
    shape = (grid_rows, grid_cols, half + half // 2, 384)
    half_shape = (grid_rows // 2, *shape[1:])
    out, part = (pl.BlockSpec(v, lambda i, s: (0, 0, 0, 0), pipeline_mode=pl.Buffered(1)) for v in (shape, half_shape))
    return pl.pallas_call(
        lambda *refs: attention_grads_body(grid, *refs),
        grid_spec=pltpu.PrefetchScalarGridSpec(
            num_scalar_prefetch=1,
            grid=(width // 384,),
            in_specs=[pl.BlockSpec((width, tokens), lambda i, s: (0, 0), pipeline_mode=pl.Buffered(1))]
            + [pl.BlockSpec((tokens, 384), lambda i, s: (0, i))] * 3,
            out_specs=[out, part, part],
        ),
        out_shape=[jax.ShapeDtypeStruct(v, BF16) for v in (shape, half_shape, half_shape)],
        cost_estimate=costs(8),
        name="attention_weight_grads",
    )(place, x_turned, *grads)


def input_grad_body(grad_first, grad_query, grad_key, grad_value, w_query, w_key, w_value, out):
    total = grad_first[...]
    for grad, weight in ((grad_query, w_query), (grad_key, w_key), (grad_value, w_value)):
        total = total + dot_nt(grad[...], weight[...])
    out[...] = total.astype(BF16)


def input_gradient(grad_first, grads, w_query, w_key, w_value):
    tokens, width = grad_first.shape
    rows = 256
    tile = pl.BlockSpec((rows, width), lambda i: (i, 0))
    whole = pl.BlockSpec((width, width), lambda i: (0, 0), pipeline_mode=pl.Buffered(1))
    return pl.pallas_call(
        input_grad_body,
        grid=(tokens // rows,),
        in_specs=[tile] * 4 + [whole] * 3,
        out_specs=tile,
        out_shape=jax.ShapeDtypeStruct((tokens, width), BF16),
        cost_estimate=costs(8),
        name="input_gradient",
    )(grad_first, *grads, w_query, w_key, w_value)


def gather_plain(block):
    whole = lax.all_gather(block, "col", axis=1, tiled=True)
    return lax.all_gather(whole, "row", axis=0, tiled=True)


def scatter_plain(whole):
    part = lax.psum_scatter(whole.astype(BF16), "row", scatter_dimension=0, tiled=True)
    part = lax.psum_scatter(part, "col", scatter_dimension=1, tiled=True)
    return lax.psum(part, "dp").astype(F32)


def scatter_gain(whole):
    part = lax.psum_scatter(whole.astype(BF16), ("row", "col"), scatter_dimension=0, tiled=True)
    return lax.psum(part, "dp").astype(F32)


def on_device(
    inputs,
    segment_ids,
    query_weight,
    key_weight,
    value_weight,
    output_weight,
    gate_weight,
    up_weight,
    down_weight,
    first_gain,
    second_gain,
    cotangent,
):
    grid = (lax.axis_size("row"), lax.axis_size("col"))
    tokens, width = inputs.shape
    hidden_width = gate_weight.shape[1] * grid[1]
    core = lax.axis_index("dp")
    odd = (lax.axis_index("col") & 1) == 1
    place = place_scalars()
    packs = grid == (4, 4) and query_weight.shape[1] == 192 and gate_weight.shape[1] == 512

    def tables(segments):
        token_index = jnp.arange(tokens, dtype=jnp.int32)
        length = tokens // (segments[tokens - 1] + 1)
        starts = segments * length
        positions = (token_index - starts).astype(F32)
        frequencies = ROPE_BASE ** (-2.0 * jnp.arange(HEAD_DIM // 2, dtype=F32) / HEAD_DIM)
        phases = positions[:, None] * frequencies[None, :]
        cosine, sine = jnp.cos(phases), jnp.sin(phases)
        cosine = jnp.concatenate([cosine] * 4, axis=1)
        sine = jnp.concatenate([-sine, sine] * 2, axis=1)
        return cosine, sine, starts[::QUERY_BLOCK] // QUERY_BLOCK

    def backward(grad_context, context, lse, begin, pairs, into):
        return attention_backward(first, query, key, value, grad_context, context, lse, cosine, sine, begin, pairs, into)

    if not packs:
        cosine, sine, first = tables(segment_ids)
        x_turned = inputs.T
        w_query, w_key, w_value, w_output = (
            gather_plain(w) for w in (query_weight, key_weight, value_weight, output_weight)
        )
        w_gate, w_up, w_down = gather_plain(gate_weight), gather_plain(up_weight), gather_plain(down_weight).T
        gains = jnp.stack(
            [lax.all_gather(g, ("row", "col"), axis=0, tiled=True).astype(F32) for g in (first_gain, second_gain)]
        )
        gains = jnp.pad(gains, ((0, 6), (0, 0)))
        query, key, value = project(inputs, w_query, w_key, w_value, cosine, sine)
        context, lse = attention_forward(first, query, key, value, 0, width // LANES)
        (
            layer_out, hidden_in_turned, branch_two_turned, context_turned, hidden, grad_gate, grad_up, grad_first, branch_one, grad_context, gain_grads,
        ) = middle_plain(context, inputs, cotangent, w_output, w_gate, w_up, w_down, gains)
        grads = backward(grad_context, context, lse, 0, width // LANES, ())
        input_grad = input_gradient(grad_first, grads, w_query, w_key, w_value)
        query_out, key_out, value_out = (scatter_plain(dot_nn(x_turned, g)) for g in grads)
        output_out = scatter_plain(dot_nn(context_turned, branch_one))
        gate_out, up_out = (scatter_plain(dot_nn(hidden_in_turned, g)) for g in (grad_gate, grad_up))
        down_out = scatter_plain(dot_nn(branch_two_turned, hidden).T)
        gain_one_out, gain_two_out = scatter_gain(gain_grads[0]), scatter_gain(gain_grads[1])
        return (
            layer_out, input_grad, query_out, key_out, value_out, output_out, gate_out, up_out, down_out, gain_one_out, gain_two_out,
        )

    join = lambda *stacks: jnp.concatenate(stacks, axis=0)
    q0 = pack_attention(place, query_weight, key_weight, value_weight)[None]
    f0 = pack_feed(place, gate_weight, up_weight, down_weight.T, output_weight, first_gain, second_gain)[None]
    q1 = exchange(q0, grid, 0)
    f1 = exchange(f0, grid, 0)
    q1, f0, segments, x_in = tie(q1, f0, segment_ids, inputs)
    q01 = join(q0, q1)
    q2 = exchange(q01, grid, 1)
    cosine, sine, first = tables(segments)
    x_turned = x_in.T
    q2, f1, cosine, sine, x_turned, first = tie(q2, f1, cosine, sine, x_turned, first)
    q03 = join(q01, q2)
    f01 = join(f0, f1)
    q3, q4 = exchange(q03, grid, 2), exchange(q03, grid, 3)
    q03_other = other_core(q03)
    f2 = exchange(f01, grid, 1)
    q3, q4, q03_other = tie(q3, q4, q03_other)
    q5 = exchange(q3, grid, 3)
    q3_other, q4_other = other_core(q3), other_core(q4)
    q5, q3_other, q4_other, f2 = tie(q5, q3_other, q4_other, f2)
    q5_other = other_core(q5)
    f03 = join(f01, f2)
    f3, f4 = exchange(f03, grid, 2), exchange(f03, grid, 3)
    query, key, value, w_query, w_key, w_value = project_blocks(
        (q03, q3, q4, q5, q03_other, q3_other, q4_other, q5_other), place, grid, inputs, cosine, sine
    )
    f03_other = other_core(f03)
    context, lse = attention_forward(first, query, key, value, 0, width // LANES)
    f3, f4, f03_other, context = tie(f3, f4, f03_other, context)
    f5 = exchange(f3, grid, 3)
    f3_other, f4_other = other_core(f3), other_core(f4)
    f5, f3_other, f4_other = tie(f5, f3_other, f4_other)
    (
        layer_out, hidden_in_turned, branch_two_turned, context_turned, hidden, grad_gate, grad_up, grad_first, branch_one, grad_context, gain_grads,
    ) = middle((f03, f3, f4, f5, f03_other, f3_other, f4_other, other_core(f5)), place, grid, context, inputs, cotangent)

    pairs = width // LANES
    feed = Scatter(grid)
    own, other = feed_grads(place, grid, hidden_in_turned, (grad_gate, grad_up))
    other, branch_two_turned = tie(other, branch_two_turned)
    received = other_core(other)
    low_own, low_other = down_grads(place, grid, branch_two_turned, hidden, context_turned, branch_one, gain_grads)
    received, low_other = tie(received, low_other)
    feed.add(own, received)
    feed.add(low_own, other_core(low_other))
    came = feed.send(feed.sums([2, 0], [2, 4]), 3)
    grads = backward(grad_context, context, lse, 0, pairs // 2, ())
    grads = backward(grad_context, context, lse, pairs // 2, pairs // 2, grads)
    came, x_turned, grads = tie(came, x_turned, grads)
    feed.put(came)
    away, x_turned = tie(feed.sums([1, 0], [1, 4]), x_turned)
    came = feed.send(away, 2)
    heads = Scatter(grid)
    own, low, high = attention_grads(place, grid, x_turned, grads)
    heads.add(own)
    heads.put(other_core(low))
    heads.put(other_core(high), (2, 0))
    away, came = tie(heads.sums([2, 0], [2, 4]), came)
    came_heads = heads.send(away, 3)
    feed.put(came)
    away, grad_first = tie(feed.sums([0, 2], [1, 2]), grad_first)
    came = feed.send(away, 1)
    input_grad = input_gradient(grad_first, grads, w_query, w_key, w_value)
    came_heads, input_grad = tie(came_heads, input_grad)
    heads.put(came_heads)
    came_heads = heads.send(heads.sums([1, 0], [1, 4]), 2)
    feed.put(came)
    came_heads, away = tie(came_heads, feed.sums([0, 1], [1, 1]))
    came = feed.send(away, 0)
    heads.put(came_heads)
    came_heads = heads.send(heads.sums([0, 2], [1, 2]), 1)
    heads.put(came_heads)
    came_heads, came = tie(heads.send(heads.sums([0, 1], [1, 1]), 0), came)
    heads.put(came_heads)
    feed.put(came)
    mine = last_sums((feed, heads))
    query_out, key_out, value_out, output_out, gate_out, up_out, down_out, gain_one_out, gain_two_out = finish(
        place, mine, other_core(mine), [query_weight.shape] * 4 + [gate_weight.shape] * 3 + [first_gain.shape] * 2
    )
    return (
        layer_out, input_grad, query_out, key_out, value_out, output_out, gate_out, up_out, down_out.T, gain_one_out, gain_two_out,
    )


def solution(mesh):
    tokens = P(("dp", "row", "col"), None)
    block = P("row", "col")
    gain = P(("row", "col"))
    return jax.shard_map(
        on_device,
        mesh=mesh,
        in_specs=(tokens, P(("dp", "row", "col"))) + (block,) * 7 + (gain, gain, tokens),
        out_specs=(tokens, tokens) + (block,) * 7 + (gain, gain),
        check_vma=False,
    )
```

```python
import jax
import jax.numpy as jnp
from jax import lax
from jax.experimental import pallas as pl
from jax.experimental.pallas import tpu as pltpu
from jax.sharding import PartitionSpec as P

HEAD_DIM = 64
EPSILON = 1e-06
ROPE_BASE = 10000.0
NEGATIVE = -1e30
LOG2E = 1.4426950408889634
QUERY_BLOCK = 256
LANES = 128
BF16 = jnp.bfloat16
F32 = jnp.float32
EVERYWHERE = ("dp", "row", "col")


def costs(microseconds):
    return pl.CostEstimate(flops=int(microseconds * 1e7), bytes_accessed=int(microseconds * 1e4), transcendentals=0)


def dot_nn(left, right):
    return lax.dot_general(left, right, (((1,), (0,)), ((), ())), preferred_element_type=F32)


def dot_nt(left, right):
    return lax.dot_general(left, right, (((1,), (1,)), ((), ())), preferred_element_type=F32)


def bit_count(size):
    return size.bit_length() - 1


def bit_order(grid_rows, grid_cols, core):
    col_bits = [("col", b) for b in range(bit_count(grid_cols))]
    row_bits = [("row", b) for b in range(bit_count(grid_rows))]
    return (col_bits[::-1] + row_bits[::-1]) if core else (col_bits + row_bits)


def step_pairs(grid_rows, grid_cols, step):
    pairs = []
    for core in range(2):
        axis, bit = bit_order(grid_rows, grid_cols, core)[step]
        for row in range(grid_rows):
            for col in range(grid_cols):
                to_row = row ^ (1 << bit) if axis == "row" else row
                to_col = col ^ (1 << bit) if axis == "col" else col
                source = (core * grid_rows + row) * grid_cols + col
                target = (core * grid_rows + to_row) * grid_cols + to_col
                pairs.append((source, target))
    return pairs


def other_core(value):
    return lax.ppermute(value, "dp", [(0, 1), (1, 0)])


def exchange(value, grid, step):
    return lax.ppermute(value, EVERYWHERE, step_pairs(*grid, step))


def tie(*values):
    return lax.optimization_barrier(values)


def sum_blocks_body(shape, *refs):
    parts, came = shape
    out = refs[-1]
    came_refs = refs[len(refs) - 1 - came : -1]
    at = begin = 0
    for count in parts:
        end = begin + refs[at].shape[2]
        total = sum(ref[...].astype(F32) for ref in refs[at : at + count])
        for ref in came_refs:
            total = total + ref[:, :, begin:end, :].astype(F32)
        out[:, :, begin:end, :] = total.astype(BF16)
        at += count
        begin = end


class Scatter:
    def __init__(self, grid):
        self.grid = grid
        self.parts = []
        self.came = []

    def add(self, *terms):
        self.parts.append(list(terms))

    def put(self, came, origin=(0, 0)):
        self.came.append((came, origin))

    def terms(self, start, size):
        came = []
        for value, origin in self.came:
            inside = [o <= a and a + n <= o + m for o, a, n, m in zip(origin, start, size, value.shape)]
            apart = [a + n <= o or o + m <= a for o, a, n, m in zip(origin, start, size, value.shape)]
            assert all(inside) or any(apart)
            if all(inside):
                came.append((value, origin))
        return [(term, (0, 0)) for part in self.parts for term in part], came

    def sums(self, start, size):
        height = sum(part[0].shape[2] for part in self.parts)
        width = self.parts[0][0].shape[3]
        parts, came = self.terms(start, size)
        terms = parts + came
        if len(self.parts) == 1:
            values = []
            for term, origin in terms:
                begin = [a - o for a, o in zip(start, origin)]
                values.append(term[begin[0] : begin[0] + size[0], begin[1] : begin[1] + size[1]])
            if len(values) == 2:
                return values[0] + values[1]
            return sum(value.astype(F32) for value in values).astype(BF16)
        axis = 0 if size[0] > 1 else 1
        count = 2 if size[axis] > 1 else 1
        block = list(size)
        block[axis] //= count

        def spec(rows, begin):
            first = begin[0] // block[0], begin[1] // block[1]
            step = (lambda i: (first[0] + i, first[1], 0, 0)) if axis == 0 else (lambda i: (first[0], first[1] + i, 0, 0))
            return pl.BlockSpec((block[0], block[1], rows, width), step)

        return pl.pallas_call(
            lambda *refs: sum_blocks_body(([len(part) for part in self.parts], len(came)), *refs),
            grid=(count,),
            in_specs=[spec(term.shape[2], [a - o for a, o in zip(start, origin)]) for term, origin in terms],
            out_specs=spec(height, (0, 0)),
            out_shape=jax.ShapeDtypeStruct((size[0], size[1], height, width), BF16),
            cost_estimate=costs(2),
            name="sum_blocks",
        )(*[term for term, _ in terms])

    def send(self, value, step):
        return exchange(value, self.grid, step)


def last_sums_body(shapes, *refs):
    out = refs[-1]
    at = top = 0
    for parts, came in shapes:
        count = sum(parts) + came
        group = refs[at : at + count]
        height = sum(group[sum(parts[:k])].shape[2] for k in range(len(parts)))
        width = group[0].shape[3]
        begin = first = 0
        for n in parts:
            end = begin + group[first].shape[2]
            total = sum(ref[0, 0].astype(F32) for ref in group[first : first + n])
            for ref in group[count - came :]:
                total = total + ref[0, 0, begin:end, :].astype(F32)
            out[top + begin : top + end, 0:width] = total.astype(BF16)
            first += n
            begin = end
        top += height
        at += count


def last_sums(scatters):
    shapes, terms, height, width = [], [], 0, 0
    for scatter in scatters:
        parts, came = scatter.terms([0, 0], [1, 1])
        shapes.append(([len(part) for part in scatter.parts], len(came)))
        terms += parts + came
        height += sum(part[0].shape[2] for part in scatter.parts)
        width = max(width, scatter.parts[0][0].shape[3])

    def spec(term, origin):
        return pl.BlockSpec((1, 1, *term.shape[2:]), lambda i: (-origin[0], -origin[1], 0, 0))

    return pl.pallas_call(
        lambda *refs: last_sums_body(shapes, *refs),
        grid=(1,),
        in_specs=[spec(*term) for term in terms],
        out_specs=pl.BlockSpec((height, width), lambda i: (0, 0)),
        out_shape=jax.ShapeDtypeStruct((height, width), BF16),
        cost_estimate=costs(2),
        name="last_sums",
    )(*[term for term, _ in terms])


def reversed_bits(value, bits):
    out = 0
    for b in range(bits):
        out = out | (((value >> b) & 1) << (bits - 1 - b))
    return out


def place_of(row, col, place, core, grid_rows, grid_cols):
    far_row = row ^ place[0]
    far_col = col ^ place[1]
    row_bits = bit_count(grid_rows)
    col_bits = bit_count(grid_cols)
    plain = far_col + far_row * grid_cols
    turned = reversed_bits(far_col, col_bits) + reversed_bits(far_row, row_bits) * grid_cols
    return jnp.where(core == 0, plain, turned)


def unpack_pair(packed, odd):
    firsts = []
    for k in range(2):
        body = packed[:, 128 * k : 128 * (k + 1)]
        rest_low, rest_high = packed[:, 256:320], packed[:, 320:384]
        in_order, turned = (rest_low, rest_high) if k == 0 else (rest_high, rest_low)
        plain = jnp.concatenate([body, in_order], axis=1)
        other = jnp.concatenate([turned, body], axis=1)
        firsts.append(jnp.where(odd, other, plain))
    return firsts


def by_core(place, mine, theirs):
    mine, theirs = mine.astype(F32), theirs.astype(F32)
    first = place[2] == 0
    return jnp.where(first, mine, theirs), jnp.where(first, theirs, mine)


def finish_body(place, mine, theirs, query, key, value, output, gate, up, down, gain_one, gain_two):
    half = down.shape[0] // 2
    quarter = half // 2
    share = gain_one.shape[0]
    odd = (place[1] & 1) == 1
    halves = by_core(place, mine[...], theirs[...])
    for core, part in enumerate(halves):
        rows = slice(core * half, (core + 1) * half)
        for k, out in enumerate((gate, up, down)):
            out[rows, :] = part[k * half : (k + 1) * half]
        low = 3 * half + quarter
        query[rows, :], key[rows, :] = unpack_pair(part[low : low + half, :384], odd)
        for out, begin in ((output, 3 * half), (value, low + half)):
            for k, block in enumerate(unpack_pair(part[begin : begin + quarter, :384], odd)):
                out[core * half + k * quarter : core * half + (k + 1) * quarter, :] = block
    gains = halves[0][3 * half : 3 * half + 8, 384:512]
    gain_one[...] = gains[0, :share]
    gain_two[...] = gains[1, :share]


def finish(place, mine, theirs, shapes):
    vmem = pl.BlockSpec(memory_space=pltpu.VMEM)
    return pl.pallas_call(
        finish_body,
        in_specs=[pl.BlockSpec(memory_space=pltpu.SMEM)] + [vmem] * 2,
        out_specs=[vmem] * len(shapes),
        out_shape=[jax.ShapeDtypeStruct(shape, F32) for shape in shapes],
        cost_estimate=costs(1),
        name="finish",
    )(place, mine, theirs)


def pack_pair(first, second, odd, out, rows):
    rolled = [jnp.concatenate([v[:, 64:], v[:, :64]], axis=1) for v in (first, second)]
    bodies = [jnp.where(odd, r[:, :128], v[:, :128]) for r, v in zip(rolled, (first, second))]
    rests = [jnp.where(odd, v[:, :64], v[:, 128:]) for v in (first, second)]
    low = jnp.where(odd, rests[1], rests[0])
    high = jnp.where(odd, rests[0], rests[1])
    out[rows, 0:128] = bodies[0].astype(BF16)
    out[rows, 128:256] = bodies[1].astype(BF16)
    out[rows, 256:384] = jnp.concatenate([low, high], axis=1).astype(BF16)


def pack_attention_body(query, key, value, out):
    half = query.shape[0] // 2
    quarter = half // 2
    place = lax.axis_index("row"), lax.axis_index("col"), lax.axis_index("dp")
    odd = (place[1] & 1) == 1
    base = place[2] * half
    query, key = (w[pl.ds(pl.multiple_of(base, half), half), :].astype(F32) for w in (query, key))
    pack_pair(query, key, odd, out, slice(0, half))
    value = value[pl.ds(pl.multiple_of(base, half), half), :].astype(F32)
    pack_pair(value[:quarter], value[quarter:], odd, out, slice(half, half + quarter))


def pack_attention(query, key, value):
    half = query.shape[0] // 2
    vmem = pl.BlockSpec(memory_space=pltpu.VMEM)
    return pl.pallas_call(
        pack_attention_body,
        in_specs=[vmem] * 3,
        out_specs=vmem,
        out_shape=jax.ShapeDtypeStruct((half + half // 2, 384), BF16),
        cost_estimate=costs(2),
        name="pack_attention",
    )(query, key, value)


def pack_feed_body(place, gate, up, down, output, gain_one, gain_two, out):
    half = gate.shape[0] // 2
    quarter = half // 2
    odd = (place[1] & 1) == 1
    rows = pl.ds(pl.multiple_of(place[2] * half, half), half)
    out[0:half, :] = gate[rows, :]
    out[half : 2 * half, :] = up[rows, :]
    out[2 * half + quarter : 3 * half + quarter, :] = down[rows, :]
    output = output[rows, :].astype(F32)
    low = slice(2 * half, 2 * half + quarter)
    pack_pair(output[:quarter], output[quarter:], odd, out, low)
    share = gain_one.shape[1]
    gains = jnp.concatenate([gain_one[...].astype(F32), gain_two[...].astype(F32)], axis=0)
    gains = jnp.concatenate([gains, jnp.zeros((2, LANES - share), F32)], axis=1)
    gains = jnp.concatenate([gains, jnp.zeros((quarter - 2, LANES), F32)], axis=0)
    out[low, 384:512] = gains.astype(BF16)


def pack_feed(place, gate, up, down_turned, output, gain_one, gain_two):
    half = gate.shape[0] // 2
    vmem = pl.BlockSpec(memory_space=pltpu.VMEM)
    return pl.pallas_call(
        pack_feed_body,
        in_specs=[pl.BlockSpec(memory_space=pltpu.SMEM)] + [vmem] * 6,
        out_specs=vmem,
        out_shape=jax.ShapeDtypeStruct((3 * half + half // 2, gate.shape[1]), BF16),
        cost_estimate=costs(2),
        name="pack_feed",
    )(place, gate, up, down_turned, output, gain_one[None], gain_two[None])


def place_scalars():
    return jnp.stack([lax.axis_index("row"), lax.axis_index("col"), lax.axis_index("dp")]).astype(jnp.int32)


def split_rows(top):
    return lax.broadcasted_iota(jnp.int32, top, 1) < 64


def fill_columns(target, rows, low_even, body_even, low_odd, body_odd, pair, swapped):
    base = 384 * pair
    target[rows, base : base + 128] = body_even
    target[rows, base + 256 : base + 384] = body_odd
    first = split_rows(low_even.shape)
    if swapped:
        mixed = jnp.where(first, low_odd, low_even)
        target[rows, base + 128 : base + 256] = pltpu.roll(mixed.astype(F32), 64, 1).astype(BF16)
    else:
        target[rows, base + 128 : base + 256] = jnp.where(first, low_even, low_odd)


def piece_places(pieces):
    counts = [p.shape[0] for p in pieces]
    out = []
    for side in range(2):
        at = 0
        for count in counts[side * len(counts) // 2 : (side + 1) * len(counts) // 2]:
            out.append((side, at, count))
            at += count
    return out


def load_stacks(pieces, held, sems):
    copies = []
    for k, (piece, (side, at, count)) in enumerate(zip(pieces, piece_places(pieces))):
        copies.append(pltpu.make_async_copy(piece, held.at[side, pl.ds(at, count)], sems.at[k]))
    for copy in copies:
        copy.start()
    for copy in copies:
        copy.wait()


def assemble_attention(grid, place, held, w_query, w_key, w_value):
    grid_rows, grid_cols = grid
    where = (place[0], place[1])
    half = w_query.shape[0] // grid_rows // 2
    quarter = half // 2
    for core in range(2):
        side = core ^ place[2]
        for row in range(grid_rows):
            start = row * 2 * half + core * half
            for pair in range(grid_cols // 2):
                at = [place_of(row, 2 * pair + c, where, core, grid_rows, grid_cols) for c in range(2)]
                even, odd = (held.at[side, p] for p in at)
                top = slice(0, half)
                rows = slice(start, start + half)
                rest_even, rest_odd = even[top, 256:384], odd[top, 256:384]
                fill_columns(w_query, rows, rest_even, even[top, 0:128], rest_odd, odd[top, 0:128], pair, False)
                fill_columns(w_key, rows, rest_even, even[top, 128:256], rest_odd, odd[top, 128:256], pair, True)
                low = slice(half, half + quarter)
                rest_even, rest_odd = even[low, 256:384], odd[low, 256:384]
                rows = slice(start, start + quarter)
                fill_columns(w_value, rows, rest_even, even[low, 0:128], rest_odd, odd[low, 0:128], pair, False)
                rows = slice(start + quarter, start + half)
                fill_columns(w_value, rows, rest_even, even[low, 128:256], rest_odd, odd[low, 128:256], pair, True)


def assemble_output(grid, place, held, w_output, gains):
    grid_rows, grid_cols = grid
    where = (place[0], place[1])
    half = w_output.shape[0] // grid_rows // 2
    quarter = half // 2
    width = gains.shape[1]
    share = width // (grid_rows * grid_cols)
    lane = lax.broadcasted_iota(jnp.int32, (LANES, width), 1)
    spread = (lax.rem(lane, share) == lax.broadcasted_iota(jnp.int32, (LANES, width), 0)).astype(BF16)
    block_of = lax.div(lax.broadcasted_iota(jnp.int32, (16, width), 1), share)
    total = jnp.zeros((16, width), F32)
    every = slice(0, quarter)
    for core in range(2):
        side = core ^ place[2]
        for row in range(grid_rows):
            start = row * 2 * half + core * half
            for pair in range(grid_cols // 2):
                at = [place_of(row, 2 * pair + c, where, core, grid_rows, grid_cols) for c in range(2)]
                even, odd = (held.at[side, p] for p in at)
                rest_even, rest_odd = even[every, 256:384], odd[every, 256:384]
                rows = slice(start, start + quarter)
                fill_columns(w_output, rows, rest_even, even[every, 0:128], rest_odd, odd[every, 0:128], pair, False)
                rows = slice(start + quarter, start + half)
                fill_columns(w_output, rows, rest_even, even[every, 128:256], rest_odd, odd[every, 128:256], pair, True)
                if core == 0:
                    for c, block in enumerate((even, odd)):
                        spreaded = dot_nn(block[0:16, 384:512], spread)
                        total = total + jnp.where(block_of == row * grid_cols + 2 * pair + c, spreaded, 0.0)
    gains[...] = total[:8]


def block_at(position, place, core, grid):
    grid_rows, grid_cols = grid
    far_row, far_col = position // grid_cols, position % grid_cols
    turned_row, turned_col = reversed_bits(far_row, bit_count(grid_rows)), reversed_bits(far_col, bit_count(grid_cols))
    first = core == 0
    return jnp.where(first, far_row, turned_row) ^ place[0], jnp.where(first, far_col, turned_col) ^ place[1]


def start_feed_copies(grid, place, pieces, w_gate, w_up, w_down, held, sems):
    grid_rows, grid_cols = grid
    half = w_gate.shape[0] // grid_rows // 2
    quarter = half // 2
    span = w_gate.shape[1] // grid_cols
    for k, (begin, size) in enumerate(((2 * half, quarter), (0, half), (half, half), (2 * half + quarter, half))):
        for piece, (side, at, count) in zip(pieces, piece_places(pieces)):
            core = side ^ place[2]

            @pl.loop(0, count)
            def _(n):
                row, col = block_at(at + n, place, core, grid)
                if k == 0:
                    target = held.at[side, at + n]
                elif k < 3:
                    rows = pl.ds(pl.multiple_of((2 * row + core) * half, half), half)
                    target = (w_gate, w_up)[k - 1].at[rows, pl.ds(pl.multiple_of(col * span, span), span)]
                else:
                    rows = pl.ds(pl.multiple_of((2 * col + core) * half, half), half)
                    target = w_down.at[rows, pl.ds(pl.multiple_of(row * span, span), span)]
                pltpu.make_async_copy(piece.at[n, pl.ds(begin, size)], target, sems.at[k]).start()


def swap_halves(values):
    lane = lax.broadcasted_iota(jnp.int32, values.shape, 1)
    back = pltpu.roll(values, 32, 1)
    ahead = pltpu.roll(values, LANES - 32, 1)
    return jnp.where(lax.rem(lane, HEAD_DIM) < HEAD_DIM // 2, ahead, back)


def project_tile(x, w_query, w_key, w_value, cosine, sine, query, key, value):
    width = w_query.shape[1]
    step = 256
    for start in range(0, width, step):
        for weight, out in ((w_query, query), (w_key, key)):
            flat = dot_nn(x[...], weight[:, start : start + step])
            for k in range(step // LANES):
                part = flat[:, k * LANES : (k + 1) * LANES]
                turned = part * cosine[...] + swap_halves(part) * sine[...]
                out[:, start + k * LANES : start + (k + 1) * LANES] = turned.astype(BF16)
        value[:, start : start + step] = dot_nn(x[...], w_value[:, start : start + step]).astype(BF16)


def project_blocks_body(grid, count, place, *refs):
    pieces, refs = refs[:count], refs[count:]
    x, cosine, sine, query, key, value, w_query, w_key, w_value, held, sems = refs

    @pl.when(pl.program_id(0) == 0)
    def _():
        load_stacks(pieces, held, sems)
        assemble_attention(grid, place, held, w_query, w_key, w_value)

    project_tile(x, w_query, w_key, w_value, cosine, sine, query, key, value)


def project_blocks(pieces, place, grid, x, cosine, sine):
    tokens, width = x.shape
    _, height, lanes = pieces[0].shape
    rows = 256
    tile = pl.BlockSpec((rows, width), lambda i: (i, 0))
    table = pl.BlockSpec((rows, LANES), lambda i: (i, 0))
    whole = pl.BlockSpec((width, width), lambda i: (0, 0), pipeline_mode=pl.Buffered(1))
    anywhere = pl.BlockSpec(memory_space=pl.ANY)
    return pl.pallas_call(
        lambda *refs: project_blocks_body(grid, len(pieces), *refs),
        grid=(tokens // rows,),
        in_specs=[pl.BlockSpec(memory_space=pltpu.SMEM)] + [anywhere] * len(pieces) + [tile, table, table],
        out_specs=[tile] * 3 + [whole] * 3,
        out_shape=[jax.ShapeDtypeStruct((tokens, width), BF16)] * 3 + [jax.ShapeDtypeStruct((width, width), BF16)] * 3,
        scratch_shapes=[
            pltpu.VMEM((2, grid[0] * grid[1], height, lanes), BF16),
            pltpu.SemaphoreType.DMA((len(pieces),)),
        ],
        cost_estimate=costs(10),
        name="project_heads",
    )(place, *pieces, x, cosine, sine)


def project(x, w_query, w_key, w_value, cosine, sine):
    tokens, width = x.shape
    rows = 256
    tile = pl.BlockSpec((rows, width), lambda i: (i, 0))
    table = pl.BlockSpec((rows, LANES), lambda i: (i, 0))
    whole = pl.BlockSpec((width, width), lambda i: (0, 0))
    return pl.pallas_call(
        project_tile,
        grid=(tokens // rows,),
        in_specs=[tile, whole, whole, whole, table, table],
        out_specs=[tile] * 3,
        out_shape=[jax.ShapeDtypeStruct((tokens, width), BF16)] * 3,
        name="project_heads_plain",
    )(x, w_query, w_key, w_value, cosine, sine)


def own_half(values, h):
    zero = jnp.zeros_like(values)
    return jnp.concatenate([values, zero] if h == 0 else [zero, values], axis=0)


def attention_forward_body(first, q_ref, k_ref, v_ref, context_ref, lse_ref):
    q_turned = (q_ref[...].astype(F32) * HEAD_DIM**-0.5).T.astype(BF16)
    v_turned = v_ref[...].T
    square = (LANES, LANES)
    causal = lax.broadcasted_iota(jnp.int32, square, 0) <= lax.broadcasted_iota(jnp.int32, square, 1)
    lse_ref[...] = jnp.zeros_like(lse_ref)
    for t in range(q_ref.shape[0] // LANES):
        now = slice(t * LANES, (t + 1) * LANES)
        begin = first[t * LANES // QUERY_BLOCK]
        outs = []
        for h in range(2):
            head = slice(h * HEAD_DIM, (h + 1) * HEAD_DIM)
            mine = own_half(q_turned[head, now], h)
            for b in [t, *range(t)]:
                there = slice(b * LANES, (b + 1) * LANES)
                scores = dot_nn(k_ref[there, :], mine)
                if b == t:
                    scores = jnp.where(causal, scores, NEGATIVE)
                block_top = jnp.max(scores, axis=0, keepdims=True) * LOG2E
                if b == t:
                    new_top = base = block_top
                else:
                    seen = begin <= b * LANES // QUERY_BLOCK
                    new_top = jnp.maximum(top, jnp.where(seen, block_top, NEGATIVE))
                    base = new_top + jnp.where(seen, 0.0, -NEGATIVE)
                weights = jnp.exp2(scores * LOG2E - base)
                part_total = jnp.sum(weights, axis=0, keepdims=True)
                part = dot_nn(v_turned[head, there], weights.astype(BF16))
                if b == t:
                    total, mixed = part_total, part
                else:
                    shrink = jnp.exp2(top - new_top)
                    total = total * shrink + part_total
                    mixed = mixed * shrink + part
                top = new_top
            outs.append(mixed * (1.0 / total))
            lse_ref[0, h : h + 1, now] = top + jnp.log2(total)
        context_ref[now, :] = jnp.concatenate(outs, axis=0).T.astype(BF16)


def attention_forward(first, query, key, value, begin, pairs):
    tokens = query.shape[0]
    spec = pl.BlockSpec((tokens, LANES), lambda j, f: (0, j + begin))
    part = pl.BlockSpec((tokens, LANES), lambda j, f: (0, j))
    return pl.pallas_call(
        attention_forward_body,
        grid_spec=pltpu.PrefetchScalarGridSpec(
            num_scalar_prefetch=1,
            grid=(pairs,),
            in_specs=[spec] * 3,
            out_specs=[part, pl.BlockSpec((1, 8, tokens), lambda j, f: (j, 0, 0))],
        ),
        out_shape=[
            jax.ShapeDtypeStruct((tokens, pairs * LANES), BF16),
            jax.ShapeDtypeStruct((pairs, 8, tokens), F32),
        ],
        cost_estimate=costs(4 * pairs),
        name="attention_forward",
    )(first, query, key, value)


def attention_backward_body(first, q_ref, k_ref, v_ref, grad_ref, context_ref, lse_ref, cosine, sine, *refs):
    dq_ref, dk_ref, dv_ref, dk_sum, dv_sum = refs[-5:]
    blocks = q_ref.shape[0] // QUERY_BLOCK
    scaled = q_ref[...].astype(F32) * HEAD_DIM**-0.5
    q_turned = scaled.T.astype(BF16)
    q_plain = scaled.astype(BF16)
    k_turned = k_ref[...].T
    grad = grad_ref[...]
    grad_turned = grad.T
    inner = (grad.astype(F32) * context_ref[...].astype(F32)).T
    square = (QUERY_BLOCK, QUERY_BLOCK)
    causal = lax.broadcasted_iota(jnp.int32, square, 0) <= lax.broadcasted_iota(jnp.int32, square, 1)
    low_lanes = lax.broadcasted_iota(jnp.int32, (QUERY_BLOCK, LANES), 1) < HEAD_DIM
    for i in reversed(range(blocks)):
        now = slice(i * QUERY_BLOCK, (i + 1) * QUERY_BLOCK)
        seen = slice(0, (i + 1) * QUERY_BLOCK)
        grads = []
        for h in range(2):
            head = slice(h * HEAD_DIM, (h + 1) * HEAD_DIM)
            own_lanes = low_lanes if h == 0 else jnp.logical_not(low_lanes)
            q_rows = jnp.where(own_lanes, q_plain[now, :], 0)
            g_rows = jnp.where(own_lanes, grad[now, :], 0)
            delta = jnp.sum(inner[head, now], axis=0, keepdims=True)
            lse = lse_ref[0, h : h + 1, now]
            scores = dot_nn(k_ref[seen, :], own_half(q_turned[head, now], h))
            grad_probs = dot_nn(v_ref[seen, :], own_half(grad_turned[head, now], h))
            probs, grad_scores = [], []
            for b in range(i + 1):
                there = slice(b * QUERY_BLOCK, (b + 1) * QUERY_BLOCK)
                part = scores[there]
                base = lse if b == i else lse + jnp.where(first[i] <= b, 0.0, -NEGATIVE)
                if b == i:
                    part = jnp.where(causal, part, NEGATIVE)
                part = jnp.exp2(part * LOG2E - base)
                probs.append(part.astype(BF16))
                grad_scores.append((part * (grad_probs[there] - delta)).astype(BF16))
            probs, grad_scores = jnp.concatenate(probs, axis=0), jnp.concatenate(grad_scores, axis=0)
            dv, dk = dot_nn(probs, g_rows), dot_nn(grad_scores, q_rows)
            if i == blocks - 1 and h == 0:
                dv_sum[...] = dv
                dk_sum[...] = dk
            else:
                dv_sum[seen, :] += dv
                dk_sum[seen, :] += dk
            grads.append(dot_nn(k_turned[head, seen], grad_scores) * HEAD_DIM**-0.5)
        dq = jnp.concatenate(grads, axis=0).T
        dq_ref[now, :] = (dq * cosine[now, :] - swap_halves(dq) * sine[now, :]).astype(BF16)
    dk = dk_sum[...]
    dk_ref[...] = (dk * cosine[...] - swap_halves(dk) * sine[...]).astype(BF16)
    dv_ref[...] = dv_sum[...].astype(BF16)


def attention_backward(first, query, key, value, grad, context, lse, cosine, sine, begin, pairs, into):
    tokens, width = query.shape
    spec = pl.BlockSpec((tokens, LANES), lambda j, f: (0, j + begin))
    table = pl.BlockSpec((tokens, LANES), lambda j, f: (0, 0))
    anywhere = pl.BlockSpec(memory_space=pl.ANY)
    return pl.pallas_call(
        attention_backward_body,
        grid_spec=pltpu.PrefetchScalarGridSpec(
            num_scalar_prefetch=1,
            grid=(pairs,),
            in_specs=[spec] * 5
            + [pl.BlockSpec((1, 8, tokens), lambda j, f: (j + begin, 0, 0)), table, table]
            + [anywhere] * len(into),
            out_specs=[spec] * 3,
            scratch_shapes=[pltpu.VMEM((tokens, LANES), F32)] * 2,
        ),
        out_shape=[jax.ShapeDtypeStruct((tokens, width), BF16)] * 3,
        input_output_aliases={9 + k: k for k in range(len(into))},
        cost_estimate=costs(6 * pairs),
        name="attention_backward",
    )(first, query, key, value, grad, context, lse, cosine, sine, *into)


def middle_tile(
    contexts, x, cotangent, w_output, w_gate, w_up, w_down, gains, ready,
    layer_out, hidden_in_turned, branch_two_turned, context_turned, hidden, grad_gate, grad_up, grad_first, branch_one, grad_context, gain_grads,
    slope, act,
):
    width = x.shape[1]
    span = w_gate.shape[1]
    chunk = 512
    ready(0)
    gain_one = gains[0:1, :]
    gain_two = gains[1:2, :]
    context_now = jnp.concatenate([part[...] for part in contexts], axis=1)
    first_sum = x[...].astype(F32) + dot_nn(context_now, w_output[...])
    scale_one = lax.rsqrt(jnp.mean(first_sum * first_sum, axis=1, keepdims=True) + EPSILON)
    normed_one = first_sum * scale_one
    normed = normed_one * gain_one
    hidden_in = normed.astype(BF16)
    second_sum = normed
    ready(1)
    for start in range(0, span, chunk):
        cols = slice(start, start + chunk)
        gate_act = dot_nn(hidden_in, w_gate[:, cols])
        up_act = dot_nn(hidden_in, w_up[:, cols])
        sigmoid = jax.nn.sigmoid(gate_act)
        silu = gate_act * sigmoid
        act[:, cols] = silu
        slope[:, cols] = up_act * (sigmoid + silu * (1.0 - sigmoid))
        hidden_now = (silu * up_act).astype(BF16)
        hidden[:, cols] = hidden_now
        if start == 0:
            ready(2)
        second_sum = second_sum + dot_nt(hidden_now, w_down[:, cols])
    scale_two = lax.rsqrt(jnp.mean(second_sum * second_sum, axis=1, keepdims=True) + EPSILON)
    normed_two = second_sum * scale_two
    layer_out[...] = (normed_two * gain_two).astype(BF16)
    grad_out = cotangent[...].astype(F32)
    two_term = jnp.sum(grad_out * normed_two, axis=0, keepdims=True)
    scaled = grad_out * gain_two
    grad_second = scale_two * (scaled - normed_two * jnp.mean(scaled * normed_two, axis=1, keepdims=True))
    branch_two = grad_second.astype(BF16)
    grad_normed = grad_second
    for start in range(0, span, chunk):
        cols = slice(start, start + chunk)
        grad_hidden = dot_nn(branch_two, w_down[:, cols])
        gate_now = (grad_hidden * slope[:, cols]).astype(BF16)
        up_now = (grad_hidden * act[:, cols]).astype(BF16)
        grad_gate[:, cols] = gate_now
        grad_up[:, cols] = up_now
        grad_normed = grad_normed + dot_nt(gate_now, w_gate[:, cols]) + dot_nt(up_now, w_up[:, cols])
    one_term = jnp.sum(grad_normed * normed_one, axis=0, keepdims=True)
    scaled = grad_normed * gain_one
    first_grad = scale_one * (scaled - normed_one * jnp.mean(scaled * normed_one, axis=1, keepdims=True))
    grad_first[...] = first_grad
    one_now = first_grad.astype(BF16)
    branch_one[...] = one_now
    grad_context[...] = dot_nt(one_now, w_output[...]).astype(BF16)
    hidden_in_turned[...] = hidden_in.T
    branch_two_turned[...] = branch_two.T
    context_turned[...] = context_now.T
    terms = jnp.concatenate([one_term, two_term, jnp.zeros((6, width), F32)], axis=0)

    @pl.when(pl.program_id(0) == 0)
    def _():
        gain_grads[...] = terms

    @pl.when(pl.program_id(0) > 0)
    def _():
        gain_grads[...] += terms


def middle_specs(tokens, width, span, rows):
    tile = pl.BlockSpec((rows, width), lambda i: (i, 0))
    wide = pl.BlockSpec((rows, span), lambda i: (i, 0))
    turned = pl.BlockSpec((width, rows), lambda i: (0, i))
    eight = pl.BlockSpec((8, width), lambda i: (0, 0))
    flat = jax.ShapeDtypeStruct((tokens, width), BF16)
    flat_turned = jax.ShapeDtypeStruct((width, tokens), BF16)
    broad = jax.ShapeDtypeStruct((tokens, span), BF16)
    return (
        [tile, turned, turned, turned, wide, wide, wide, tile, tile, tile, eight],
        [
            flat, flat_turned, flat_turned, flat_turned, broad, broad, broad,
            jax.ShapeDtypeStruct((tokens, width), F32), flat, flat, jax.ShapeDtypeStruct((8, width), F32),
        ],
    )


def middle_plain_body(context, x, cotangent, w_output, w_gate, w_up, w_down, gains, *rest):
    middle_tile((context,), x, cotangent, w_output, w_gate, w_up, w_down, gains, lambda k: None, *rest)


def middle_plain(context, x, cotangent, w_output, w_gate, w_up, w_down, gains):
    tokens, width = x.shape
    span = w_gate.shape[1]
    rows = 256
    tile = pl.BlockSpec((rows, width), lambda i: (i, 0))
    square = pl.BlockSpec((width, width), lambda i: (0, 0), pipeline_mode=pl.Buffered(1))
    whole = pl.BlockSpec((width, span), lambda i: (0, 0), pipeline_mode=pl.Buffered(1))
    eight = pl.BlockSpec((8, width), lambda i: (0, 0))
    out_specs, out_shape = middle_specs(tokens, width, span, rows)
    return pl.pallas_call(
        middle_plain_body,
        grid=(tokens // rows,),
        in_specs=[tile, tile, tile, square, whole, whole, whole, eight],
        out_specs=out_specs,
        out_shape=out_shape,
        scratch_shapes=[pltpu.VMEM((rows, span), F32)] * 2,
        name="feed_forward_and_back_plain",
    )(context, x, cotangent, w_output, w_gate, w_up, w_down, gains)


def middle_body(grid, count, place, *refs):
    pieces, refs = refs[:count], refs[count:]
    context, x, cotangent = refs[:3]
    outs = refs[3:14]
    slope, act, w_output, w_gate, w_up, w_down, gains, held, sems = refs[14:]
    here = pl.program_id(0) == 0

    @pl.when(here)
    def _():
        start_feed_copies(grid, place, pieces, w_gate, w_up, w_down, held, sems)

    def ready(k):
        @pl.when(here)
        def _():
            for n, target in (((0, held),), ((1, w_gate), (2, w_up)), ((3, w_down),))[k]:
                pltpu.make_async_copy(target, target, sems.at[n]).wait()
            if k == 0:
                assemble_output(grid, place, held, w_output, gains)

    middle_tile((context,), x, cotangent, w_output, w_gate, w_up, w_down, gains, ready, *outs, slope, act)


def middle(pieces, place, grid, context, x, cotangent):
    tokens, width = x.shape
    _, height, lanes = pieces[0].shape
    span = lanes * grid[1]
    rows = 256
    tile = pl.BlockSpec((rows, width), lambda i: (i, 0))
    anywhere = pl.BlockSpec(memory_space=pl.ANY)
    out_specs, out_shape = middle_specs(tokens, width, span, rows)
    return pl.pallas_call(
        lambda *refs: middle_body(grid, len(pieces), *refs),
        grid=(tokens // rows,),
        in_specs=[pl.BlockSpec(memory_space=pltpu.SMEM)] + [anywhere] * len(pieces) + [tile] * 3,
        out_specs=out_specs,
        out_shape=out_shape,
        scratch_shapes=[pltpu.VMEM((rows, span), F32)] * 2
        + [pltpu.VMEM((width, width), BF16)]
        + [pltpu.VMEM((width, span), BF16)] * 3
        + [
            pltpu.VMEM((8, width), F32),
            pltpu.VMEM((2, grid[0] * grid[1], height // 7, lanes), BF16),
            pltpu.SemaphoreType.DMA((4,)),
        ],
        cost_estimate=costs(40),
        name="feed_forward_and_back",
    )(place, *pieces, context, x, cotangent)


def part_of(index, place_index, core, count):
    far = index ^ place_index
    return jnp.where(core == 0, far, reversed_bits(far, bit_count(count)))


def store_halves(own, other, where, grid, core_here, row, col, rows, lanes, halves):
    here = core_here == 0
    for target, core, first, second in ((own, core_here, 0, 1), (other, 1 - core_here, 1, 0)):
        at = part_of(row, where[0], core, grid[0]), part_of(col, where[1], core, grid[1])
        target[at[0], at[1], rows, lanes] = jnp.where(here, halves[first], halves[second])


def rest_tile(first, second, odd):
    low = split_rows(first.shape)
    rolled = pltpu.roll(second, 64, 1)
    return jnp.where(low, rolled, first) if odd else jnp.where(low, first, rolled)


def feed_grads_body(grid, count, place, left, *refs):
    rights, (own, other) = refs[:count], refs[-2:]
    grid_rows, grid_cols = grid
    half = left.shape[0] // grid_rows // 2
    here = place[2] == 0
    for k, right in enumerate(rights):
        product = dot_nn(left[...], right[...]).astype(BF16)
        rows = slice(k * half, (k + 1) * half)
        for i in range(grid_rows):
            first, second = (product[(2 * i + c) * half : (2 * i + c + 1) * half] for c in range(2))
            mine, theirs = part_of(i, place[0], place[2], grid_rows), part_of(i, place[0], 1 - place[2], grid_rows)
            own[mine, 0, rows, :] = jnp.where(here, first, second)
            other[theirs, 0, rows, :] = jnp.where(here, second, first)


def feed_grads(place, grid, left, rights):
    width, tokens = left.shape
    grid_rows, grid_cols = grid
    span = rights[0].shape[1] // grid_cols
    half = width // grid_rows // 2
    count = len(rights)

    def out_index(flip):
        return lambda i, s: (0, part_of(i, s[1], s[2] ^ flip, grid_cols), 0, 0)

    shape = (grid_rows, grid_cols, half * count, span)
    return pl.pallas_call(
        lambda *refs: feed_grads_body(grid, count, *refs),
        grid_spec=pltpu.PrefetchScalarGridSpec(
            num_scalar_prefetch=1,
            grid=(grid_cols,),
            in_specs=[pl.BlockSpec((width, tokens), lambda i, s: (0, 0), pipeline_mode=pl.Buffered(1))]
            + [pl.BlockSpec((tokens, span), lambda i, s: (0, i))] * count,
            out_specs=[pl.BlockSpec((grid_rows, 1, half * count, span), out_index(f)) for f in range(2)],
        ),
        out_shape=[jax.ShapeDtypeStruct(shape, BF16)] * 2,
        cost_estimate=costs(7 * count),
        name="feed_forward_weight_grad",
    )(place, left, *rights)


def down_grads_body(grid, place, branch_two_turned, hidden, context_turned, branch_one, gain_grads, own, other):
    grid_rows, grid_cols = grid
    width = branch_two_turned.shape[0]
    half = width // grid_cols // 2
    quarter = half // 2
    here = place[2] == 0
    row = pl.program_id(0)
    down = dot_nn(branch_two_turned[...], hidden[...]).astype(BF16)
    output = dot_nn(context_turned[...], branch_one[...])
    share = width // (grid_rows * grid_cols)
    lane = lax.broadcasted_iota(jnp.int32, (width, LANES), 0)
    gather = (lax.rem(lane, share) == lax.broadcasted_iota(jnp.int32, (width, LANES), 1)).astype(BF16)
    block_of = lax.div(lax.broadcasted_iota(jnp.int32, (8, width), 1), share)
    low = slice(half, half + quarter)

    def store(mine, theirs, rows, lanes, halves):
        own[0, mine, rows, lanes] = jnp.where(here, halves[0], halves[1])
        other[0, theirs, rows, lanes] = jnp.where(here, halves[1], halves[0])

    for c in range(grid_cols):
        at = part_of(c, place[1], place[2], grid_cols), part_of(c, place[1], 1 - place[2], grid_cols)
        store(*at, slice(0, half), slice(0, down.shape[1]), [down[(2 * c + k) * half : (2 * c + k + 1) * half] for k in range(2)])
        tile = 384 * (c // 2)
        odd = c % 2
        body = slice(tile + 256 * odd, tile + 256 * odd + 128)
        mid = slice(tile + 128, tile + 256)
        tops, lows = ([slice(k * half + n * quarter, k * half + (n + 1) * quarter) for k in range(2)] for n in range(2))
        store(*at, low, slice(0, 128), [output[t, body].astype(BF16) for t in tops])
        store(*at, low, slice(128, 256), [output[t, body].astype(BF16) for t in lows])
        store(*at, low, slice(256, 384), [rest_tile(output[t, mid], output[l, mid], odd).astype(BF16) for t, l in zip(tops, lows)])
        picked = jnp.where(block_of == row * grid_cols + c, gain_grads[...], 0.0).astype(BF16)
        gain = dot_nn(picked, gather)
        gain = jnp.concatenate([gain, jnp.zeros((quarter - 8, LANES), F32)], axis=0).astype(BF16)
        store(*at, low, slice(384, 512), [gain, gain])


def down_grads(place, grid, branch_two_turned, hidden, context_turned, branch_one, gain_grads):
    width, tokens = branch_two_turned.shape
    grid_rows, grid_cols = grid
    span = hidden.shape[1] // grid_rows
    half = width // grid_cols // 2
    height = half + half // 2

    def out_index(flip):
        return lambda i, s: (part_of(i, s[0], s[2] ^ flip, grid_rows), 0, 0, 0)

    once = dict(pipeline_mode=pl.Buffered(1))
    own, other = pl.pallas_call(
        lambda *refs: down_grads_body(grid, *refs),
        grid_spec=pltpu.PrefetchScalarGridSpec(
            num_scalar_prefetch=1,
            grid=(grid_rows,),
            in_specs=[
                pl.BlockSpec((width, tokens), lambda i, s: (0, 0), **once),
                pl.BlockSpec((tokens, span), lambda i, s: (0, i)),
                pl.BlockSpec((width // grid_rows, tokens), lambda i, s: (i, 0)),
                pl.BlockSpec((tokens, width), lambda i, s: (0, 0), **once),
                pl.BlockSpec((8, width), lambda i, s: (0, 0)),
            ],
            out_specs=[pl.BlockSpec((1, grid_cols, height, span), out_index(f)) for f in range(2)],
        ),
        out_shape=[jax.ShapeDtypeStruct((grid_rows, grid_cols, height, span), BF16)] * 2,
        cost_estimate=costs(10),
        name="down_weight_grad",
    )(place, branch_two_turned, hidden, context_turned, branch_one, gain_grads)
    return own, other


def attention_grads_body(grid, place, x_turned, grad_query, grad_key, grad_value, own, lower, upper, other, sems):
    grid_rows, grid_cols = grid
    where = (place[0], place[1])
    half = x_turned.shape[0] // grid_rows // 2
    quarter = half // 2
    pair = pl.program_id(0)
    query, key, value = (dot_nn(x_turned[...], g[...]) for g in (grad_query, grad_key, grad_value))
    mid = slice(128, 256)
    for row in range(grid_rows):
        for odd in range(2):
            body = slice(256 * odd, 256 * odd + 128)
            pieces = []
            for core in range(2):
                start = row * 2 * half + core * half
                rows = slice(start, start + half)
                top, low = slice(start, start + quarter), slice(start + quarter, start + half)
                joined = (query[rows, body], key[rows, body], rest_tile(query[rows, mid], key[rows, mid], odd))
                last = (value[top, body], value[low, body], rest_tile(value[top, mid], value[low, mid], odd))
                pieces.append([p.astype(BF16) for p in joined + last])
            for k in range(3):
                lanes = slice(128 * k, 128 * (k + 1))
                at = (row, 2 * pair + odd)
                for n, rows in ((k, slice(0, half)), (3 + k, slice(half, half + quarter))):
                    store_halves(own, other, where, grid, place[2], *at, rows, lanes, [p[n] for p in pieces])

    @pl.when(pair == pl.num_programs(0) - 1)
    def _():
        edge = grid_rows // 2
        copies = [
            pltpu.make_async_copy(other.at[pl.ds(begin, edge)], target, sems.at[k])
            for k, (begin, target) in enumerate(((edge, upper), (0, lower)))
        ]
        for copy in copies:
            copy.start()
        for copy in copies:
            copy.wait()


def attention_grads(place, grid, x_turned, grads):
    width, tokens = x_turned.shape
    grid_rows, grid_cols = grid
    half = width // grid_rows // 2
    shape = (grid_rows, grid_cols, half + half // 2, 384)
    half_shape = (grid_rows // 2, *shape[1:])
    out = pl.BlockSpec(shape, lambda i, s: (0, 0, 0, 0), pipeline_mode=pl.Buffered(1))
    anywhere = pl.BlockSpec(memory_space=pl.ANY)
    return pl.pallas_call(
        lambda *refs: attention_grads_body(grid, *refs),
        grid_spec=pltpu.PrefetchScalarGridSpec(
            num_scalar_prefetch=1,
            grid=(width // 384,),
            in_specs=[pl.BlockSpec((width, tokens), lambda i, s: (0, 0), pipeline_mode=pl.Buffered(1))]
            + [pl.BlockSpec((tokens, 384), lambda i, s: (0, i))] * 3,
            out_specs=[out, anywhere, anywhere],
            scratch_shapes=[pltpu.VMEM(shape, BF16), pltpu.SemaphoreType.DMA((2,))],
        ),
        out_shape=[jax.ShapeDtypeStruct(v, BF16) for v in (shape, half_shape, half_shape)],
        cost_estimate=costs(8),
        name="attention_weight_grads",
    )(place, x_turned, *grads)


def input_grad_body(grad_first, grad_query, grad_key, grad_value, w_query, w_key, w_value, out):
    total = grad_first[...]
    for grad, weight in ((grad_query, w_query), (grad_key, w_key), (grad_value, w_value)):
        total = total + dot_nt(grad[...], weight[...])
    out[...] = total.astype(BF16)


def input_gradient(grad_first, grads, w_query, w_key, w_value):
    tokens, width = grad_first.shape
    rows = 256
    tile = pl.BlockSpec((rows, width), lambda i: (i, 0))
    whole = pl.BlockSpec((width, width), lambda i: (0, 0), pipeline_mode=pl.Buffered(1))
    return pl.pallas_call(
        input_grad_body,
        grid=(tokens // rows,),
        in_specs=[tile] * 4 + [whole] * 3,
        out_specs=tile,
        out_shape=jax.ShapeDtypeStruct((tokens, width), BF16),
        cost_estimate=costs(8),
        name="input_gradient",
    )(grad_first, *grads, w_query, w_key, w_value)


def gather_plain(block):
    whole = lax.all_gather(block, "col", axis=1, tiled=True)
    return lax.all_gather(whole, "row", axis=0, tiled=True)


def scatter_plain(whole):
    part = lax.psum_scatter(whole.astype(BF16), "row", scatter_dimension=0, tiled=True)
    part = lax.psum_scatter(part, "col", scatter_dimension=1, tiled=True)
    return lax.psum(part, "dp").astype(F32)


def scatter_gain(whole):
    part = lax.psum_scatter(whole.astype(BF16), ("row", "col"), scatter_dimension=0, tiled=True)
    return lax.psum(part, "dp").astype(F32)


def on_device(
    inputs,
    segment_ids,
    query_weight,
    key_weight,
    value_weight,
    output_weight,
    gate_weight,
    up_weight,
    down_weight,
    first_gain,
    second_gain,
    cotangent,
):
    grid = (lax.axis_size("row"), lax.axis_size("col"))
    tokens, width = inputs.shape
    hidden_width = gate_weight.shape[1] * grid[1]
    core = lax.axis_index("dp")
    odd = (lax.axis_index("col") & 1) == 1
    place = place_scalars()
    packs = grid == (4, 4) and query_weight.shape[1] == 192 and gate_weight.shape[1] == 512

    def tables(segments):
        token_index = jnp.arange(tokens, dtype=jnp.int32)
        length = tokens // (segments[tokens - 1] + 1)
        starts = segments * length
        positions = (token_index - starts).astype(F32)
        frequencies = ROPE_BASE ** (-2.0 * jnp.arange(HEAD_DIM // 2, dtype=F32) / HEAD_DIM)
        phases = positions[:, None] * frequencies[None, :]
        cosine, sine = jnp.cos(phases), jnp.sin(phases)
        cosine = jnp.concatenate([cosine] * 4, axis=1)
        sine = jnp.concatenate([-sine, sine] * 2, axis=1)
        return cosine, sine, starts[::QUERY_BLOCK] // QUERY_BLOCK

    def backward(grad_context, context, lse, begin, pairs, into):
        return attention_backward(first, query, key, value, grad_context, context, lse, cosine, sine, begin, pairs, into)

    if not packs:
        cosine, sine, first = tables(segment_ids)
        x_turned = inputs.T
        w_query, w_key, w_value, w_output = (
            gather_plain(w) for w in (query_weight, key_weight, value_weight, output_weight)
        )
        w_gate, w_up, w_down = gather_plain(gate_weight), gather_plain(up_weight), gather_plain(down_weight).T
        gains = jnp.stack(
            [lax.all_gather(g, ("row", "col"), axis=0, tiled=True).astype(F32) for g in (first_gain, second_gain)]
        )
        gains = jnp.pad(gains, ((0, 6), (0, 0)))
        query, key, value = project(inputs, w_query, w_key, w_value, cosine, sine)
        context, lse = attention_forward(first, query, key, value, 0, width // LANES)
        (
            layer_out, hidden_in_turned, branch_two_turned, context_turned, hidden, grad_gate, grad_up, grad_first, branch_one, grad_context, gain_grads,
        ) = middle_plain(context, inputs, cotangent, w_output, w_gate, w_up, w_down, gains)
        grads = backward(grad_context, context, lse, 0, width // LANES, ())
        input_grad = input_gradient(grad_first, grads, w_query, w_key, w_value)
        query_out, key_out, value_out = (scatter_plain(dot_nn(x_turned, g)) for g in grads)
        output_out = scatter_plain(dot_nn(context_turned, branch_one))
        gate_out, up_out = (scatter_plain(dot_nn(hidden_in_turned, g)) for g in (grad_gate, grad_up))
        down_out = scatter_plain(dot_nn(branch_two_turned, hidden).T)
        gain_one_out, gain_two_out = scatter_gain(gain_grads[0]), scatter_gain(gain_grads[1])
        return (
            layer_out, input_grad, query_out, key_out, value_out, output_out, gate_out, up_out, down_out, gain_one_out, gain_two_out,
        )

    join = lambda *stacks: jnp.concatenate(stacks, axis=0)
    q0 = pack_attention(query_weight, key_weight, value_weight)[None]
    f0 = pack_feed(place, gate_weight, up_weight, down_weight.T, output_weight, first_gain, second_gain)[None]
    q1 = exchange(q0, grid, 0)
    f1 = exchange(f0, grid, 0)
    q1, f0 = tie(q1, f0)
    q01, segments, x_in = tie(join(q0, q1), segment_ids, inputs)
    q2 = exchange(q01, grid, 1)
    cosine, sine, first = tables(segments)
    x_turned = x_in.T
    q2, f1, cosine, sine, x_turned, first = tie(q2, f1, cosine, sine, x_turned, first)
    q03 = join(q01, q2)
    f01 = join(f0, f1)
    q3, q4 = exchange(q03, grid, 2), exchange(q03, grid, 3)
    q03_other = other_core(q03)
    f2 = exchange(f01, grid, 1)
    q3, q4, q03_other = tie(q3, q4, q03_other)
    q5 = exchange(q3, grid, 3)
    q3_other, q4_other = other_core(q3), other_core(q4)
    q5, q3_other, q4_other, f2 = tie(q5, q3_other, q4_other, f2)
    q5_other = other_core(q5)
    f03 = join(f01, f2)
    f3, f4 = exchange(f03, grid, 2), exchange(f03, grid, 3)
    query, key, value, w_query, w_key, w_value = project_blocks(
        (q03, q3, q4, q5, q03_other, q3_other, q4_other, q5_other), place, grid, inputs, cosine, sine
    )
    f03_other = other_core(f03)
    context, lse = attention_forward(first, query, key, value, 0, width // LANES)
    f3, f4, f03_other, context = tie(f3, f4, f03_other, context)
    f5 = exchange(f3, grid, 3)
    f3_other, f4_other = other_core(f3), other_core(f4)
    f5, f3_other, f4_other = tie(f5, f3_other, f4_other)
    (
        layer_out, hidden_in_turned, branch_two_turned, context_turned, hidden, grad_gate, grad_up, grad_first, branch_one, grad_context, gain_grads,
    ) = middle((f03, f3, f4, f5, f03_other, f3_other, f4_other, other_core(f5)), place, grid, context, inputs, cotangent)

    pairs = width // LANES
    upper, lower, feed = Scatter(grid), Scatter(grid), Scatter(grid)
    own, other = feed_grads(place, grid, hidden_in_turned, (grad_gate, grad_up))
    other, branch_two_turned = tie(other, branch_two_turned)
    received = other_core(other)
    low_own, low_other = down_grads(place, grid, branch_two_turned, hidden, context_turned, branch_one, gain_grads)
    received, low_other = tie(received, low_other)
    low_received = other_core(low_other)
    upper.add(own, received)
    away, low_own = tie(upper.sums([2, 0], [2, 4]), low_own)
    came = upper.send(away, 3)
    lower.add(low_own, low_received)
    away, grad_context = tie(lower.sums([2, 0], [2, 4]), grad_context)
    low_came = lower.send(away, 3)
    grads = backward(grad_context, context, lse, 0, pairs // 2, ())
    grads = backward(grad_context, context, lse, pairs // 2, pairs // 2, grads)
    came, low_came, x_turned, grads = tie(came, low_came, x_turned, grads)
    feed.add(own, received, came)
    feed.add(low_own, low_received, low_came)
    away, x_turned = tie(feed.sums([1, 0], [1, 4]), x_turned)
    came = feed.send(away, 2)
    heads = Scatter(grid)
    own, low, high = attention_grads(place, grid, x_turned, grads)
    heads.add(own)
    heads.put(other_core(low))
    heads.put(other_core(high), (2, 0))
    away, came = tie(heads.sums([2, 0], [2, 4]), came)
    came_heads = heads.send(away, 3)
    feed.put(came)
    away, grad_first = tie(feed.sums([0, 2], [1, 2]), grad_first)
    came = feed.send(away, 1)
    input_grad = input_gradient(grad_first, grads, w_query, w_key, w_value)
    came_heads, input_grad = tie(came_heads, input_grad)
    heads.put(came_heads)
    came_heads = heads.send(heads.sums([1, 0], [1, 4]), 2)
    feed.put(came)
    came_heads, away = tie(came_heads, feed.sums([0, 1], [1, 1]))
    came = feed.send(away, 0)
    heads.put(came_heads)
    came_heads = heads.send(heads.sums([0, 2], [1, 2]), 1)
    heads.put(came_heads)
    came_heads, came = tie(heads.send(heads.sums([0, 1], [1, 1]), 0), came)
    heads.put(came_heads)
    feed.put(came)
    mine = last_sums((feed, heads))
    query_out, key_out, value_out, output_out, gate_out, up_out, down_out, gain_one_out, gain_two_out = finish(
        place, mine, other_core(mine), [query_weight.shape] * 4 + [gate_weight.shape] * 3 + [first_gain.shape] * 2
    )
    return (
        layer_out, input_grad, query_out, key_out, value_out, output_out, gate_out, up_out, down_out.T, gain_one_out, gain_two_out,
    )


def solution(mesh):
    tokens = P(("dp", "row", "col"), None)
    block = P("row", "col")
    gain = P(("row", "col"))
    return jax.shard_map(
        on_device,
        mesh=mesh,
        in_specs=(tokens, P(("dp", "row", "col"))) + (block,) * 7 + (gain, gain, tokens),
        out_specs=(tokens, tokens) + (block,) * 7 + (gain, gain),
        check_vma=False,
    )
```
